32 devices in a mesh: slab: 16 (over z, y, x), sub: 2 (over core).
Axes of the slice: x: 2, y: 2, z: 4, core: 2. Of those that a mesh axis runs over, the one named last changes fastest.
Arguments:
- velocities: float32 [3, 163840], P(None, ('slab', 'sub')), may hold values from -16 to 19
- cell_index: int32 [1, 163840], P(None, ('slab', 'sub')), may hold values from 0 to 511
- axis_choice: int32 [1, 16384], P(None, ('slab', 'sub')), may hold values from 0 to 63
- moves: int32 [1, 4, 4096], P(None, None, ('slab', 'sub')), may hold values from 0 to 5119, as said below
- shear_target: float32 [128], P('sub'), may hold values from -6 to 6
Outputs:
- velocities_final: float32 [3, 163840], P(None, ('slab', 'sub'))
- profile: float32 [16, 128], P('slab', 'sub')
The draws below stay inside these ranges and needn't reach their ends.
Inputs may be any that keep to these rules, and one draw needn't show every extreme that they name: `moves`: in each step the 512 slots of one device's four lists are distinct.
All inputs are finite; a program needn't handle non-finite values.
Results may differ from the reference program's by a relative error of at most 0.0003.
Values sent between devices are 32-bit elements; how exact they have to be, the bound alone decides.
No kernel may reach another device: no remote copies, remote signals or barrier semaphores. Data moves between devices by JAX's collectives and lax.ppermute only.
A program may use at most 64 MiB of HBM per device.

```python
import jax
import jax.numpy as jnp
from jax import lax

CX = 1
CY = 64
CZ = 8
MIG = 128
NAXES = 64
ITERS = 1
CELL_DEV = 512
P_DEV = 5120
GX = 16
GY = 128
BODY_COUNT_ALL = 163840
CELLS = 16384
N_SLAB = 16
N_SUB = 2


def draw_velocities(key, part):
    counter = jnp.arange(BODY_COUNT_ALL, dtype=jnp.int32)
    position = (counter // (P_DEV * N_SUB)).astype(jnp.float32) / N_SLAB
    noise = jnp.clip(jax.random.normal(key, (3, BODY_COUNT_ALL), jnp.float32), -5.0, 5.0)
    thermal = jnp.sqrt(1.0 + 2.0 * position)
    flow = 1.0 + 2.0 * position
    zeros = jnp.zeros_like(flow)
    return noise * thermal + jnp.stack([flow, zeros, zeros])


def draw_moves(key, part):
    devices = N_SLAB * N_SUB
    group = P_DEV // (4 * MIG)
    picks = jax.random.randint(jax.random.fold_in(key, 3), (ITERS, devices, 4 * MIG), 0, group)
    slots = jnp.arange(4 * MIG, dtype=jnp.int32)[None, None, :] * group + picks
    keys = jax.random.split(jax.random.fold_in(key, 7), ITERS * devices)
    order = jax.vmap(lambda single: jax.random.permutation(single, 4 * MIG))(keys).reshape(ITERS, devices, 4 * MIG)
    mixed = jnp.take_along_axis(slots, order.astype(jnp.int32), axis=2)
    return mixed.reshape(ITERS, devices, 4, MIG).transpose(0, 2, 1, 3).reshape(ITERS, 4, devices * MIG).astype(jnp.int32)


def set_ends(values, own_key, low, high):
    dims = values.shape
    index_at = [jax.random.randint(jax.random.fold_in(own_key, axis), (), 0, dims[axis]) for axis in range(len(dims))]
    values = values.at[tuple(index_at)].set(low)
    longest = dims.index(max(dims))
    index_at[longest] = (index_at[longest] + 1) % dims[longest]
    return values.at[tuple(index_at)].set(high)


def block_levels(rng, dims, shards, least, high):
    loudness, own = 1.0, jax.random.fold_in(rng, 6)
    for dim, blocks in shards:
        steps = jnp.exp(jax.random.uniform(jax.random.fold_in(own, dim), (blocks,), jnp.float32, least / len(shards), high / len(shards)))
        loudness = loudness * jnp.repeat(steps, dims[dim] // blocks).reshape([-1 if axis == dim else 1 for axis in range(len(dims))])
    return loudness


def bell_draw(stream_key, shape, scale, bound, cuts=(), kind=jnp.bfloat16):
    result = scale * jax.random.normal(stream_key, shape, jnp.float32)
    if cuts:
        result = result * block_levels(stream_key, shape, cuts, -0.22, 0.18)
    return jnp.clip(result, -bound, bound).astype(kind)


def setup_inputs(seed: int = 0) -> dict:
    arg_keys = jax.random.split(jax.random.key(seed), 6)
    velocities = draw_velocities(jax.random.fold_in(arg_keys[5], 71), 0)
    cell_index = set_ends(jax.random.randint(arg_keys[1], (ITERS, BODY_COUNT_ALL), 0, CELL_DEV), jax.random.fold_in(arg_keys[1], 1), 0, CELL_DEV - 1).astype(jnp.int32)
    axis_choice = set_ends(jax.random.randint(arg_keys[2], (ITERS, CELLS), 0, NAXES), jax.random.fold_in(arg_keys[2], 1), 0, NAXES - 1).astype(jnp.int32)
    moves = draw_moves(jax.random.fold_in(arg_keys[5], 71), 0)
    shear_target = bell_draw(arg_keys[4], (GY,), 1.0, 6.0, ((0, 2),), jnp.float32)
    return {"velocities": velocities, "cell_index": cell_index, "axis_choice": axis_choice, "moves": moves, "shear_target": shear_target}


ROT_COS = -0.6427876096865393
ROT_SIN = 0.766044443118978
RESERVOIR_HEAT = 0.9
FEEDBACK = 1.0
GOLDEN = 2.399963229728653

def axis_table():
    counter = jnp.arange(NAXES, dtype=jnp.int32).astype(jnp.float32)
    height = 1.0 - (2.0 * counter + 1.0) / NAXES
    radius = jnp.sqrt(1.0 - height * height)
    return jnp.stack([radius * jnp.cos(GOLDEN * counter), radius * jnp.sin(GOLDEN * counter), height])

def bin_cells(values, weights, cells, totals):
    stacked = jnp.concatenate([values, weights[None, :]], 0)
    return totals.at[:, cells].add(stacked)

def cell_state(totals, choices, table):
    counts = jnp.maximum(totals[3], 1.0)
    average_value = totals[:3] / counts
    onehot = (jnp.arange(NAXES, dtype=jnp.int32)[:, None] == choices[None, :]).astype(jnp.float32)
    axes = jnp.dot(table, onehot, precision=lax.Precision.HIGHEST)
    columns = lax.optimization_barrier(jnp.sum(totals.reshape(4, CX * CY, CZ), 2))
    block = (columns[0] / jnp.maximum(columns[3], 1.0)).reshape(CX, CY)
    return (average_value, axes, block)

def collide(relative, cells, average_value, axes, speed_multiplier, adjustment_factor):
    normal = axes[:, cells]
    cross = jnp.stack([normal[1] * relative[2] - normal[2] * relative[1], normal[2] * relative[0] - normal[0] * relative[2], normal[0] * relative[1] - normal[1] * relative[0]])
    along = lax.optimization_barrier(jnp.sum(normal * relative, 0))
    rotated = relative * ROT_COS + cross * ROT_SIN + normal * (along * (1.0 - ROT_COS))
    shifted = average_value.at[0].add(adjustment_factor)
    return shifted[:, cells] + speed_multiplier * rotated

def reference(velocities, cell_index, axis_choice, moves, shear_target):
    devices = N_SLAB * N_SUB
    speeds = velocities.reshape(3, devices, P_DEV).transpose(1, 0, 2)
    table = axis_table()
    profile = jnp.zeros((GX, GY), jnp.float32)
    for step in range(ITERS):
        lists = moves[step].reshape(4, devices, MIG).transpose(1, 0, 2)
        outgoing = jax.vmap(lambda speed, slots: speed[:, slots])(speeds, lists).reshape(N_SLAB, N_SUB, 3, 4, MIG)
        east_in = jnp.roll(outgoing[:, :, :, 1], -1, axis=0)
        west_in = jnp.roll(outgoing[:, :, :, 0], 1, axis=0)
        north_incoming = jnp.roll(outgoing[:, :, :, 3], -1, axis=1)
        south_in = jnp.roll(outgoing[:, :, :, 2], 1, axis=1)
        arriving = jnp.stack([east_in, west_in, north_incoming, south_in], 3).reshape(devices, 3, 4 * MIG)
        speeds = jax.vmap(lambda speed, slots, block: speed.at[:, slots.reshape(-1)].set(block))(speeds, lists, arriving)
        cells = cell_index[step].reshape(devices, P_DEV)
        choices = axis_choice[step].reshape(devices, CELL_DEV)
        weights = jnp.ones((devices, P_DEV), jnp.float32)
        totals = jax.vmap(lambda speed, weight, cell: bin_cells(speed, weight, cell, jnp.zeros((4, CELL_DEV), jnp.float32)))(speeds, weights, cells)
        average_value, axes, blocks = jax.vmap(lambda total, picks: cell_state(total, picks, table))(totals, choices)
        profile = blocks.reshape(N_SLAB, N_SUB, CX, CY).transpose(0, 2, 1, 3).reshape(GX, GY)
        drift = lax.optimization_barrier(jnp.sum(profile, 0)) / GX
        relative = jax.vmap(lambda speed, mean_cells, cell: speed - mean_cells[:, cell])(speeds, average_value, cells)
        motion_work = jnp.sum(relative * relative)
        speed_multiplier = lax.rsqrt(motion_work / (3.0 * BODY_COUNT_ALL * RESERVOIR_HEAT) + 1e-06)
        adjustment_factor = FEEDBACK * (shear_target - drift)
        per_cell = jnp.broadcast_to(adjustment_factor.reshape(1, N_SUB, 1, CY, 1), (N_SLAB, N_SUB, CX, CY, CZ)).reshape(devices, CELL_DEV)
        speeds = jax.vmap(lambda deviation, mean_cells, axis_cols, cell, extra: collide(deviation, cell, mean_cells, axis_cols, speed_multiplier, extra))(relative, average_value, axes, cells, per_cell)
    return (speeds.transpose(1, 0, 2).reshape(3, BODY_COUNT_ALL), profile)
```

```python
import functools
import math

import jax
import jax.numpy as jnp
from jax import lax
from jax.experimental import pallas as pl
from jax.experimental.pallas import tpu as pltpu
from jax.sharding import PartitionSpec as P

CX = 1
CY = 64
CZ = 8
NAXES = 64

ROT_COS = -0.6427876096865393
ROT_SIN = 0.766044443118978
RESERVOIR_HEAT = 0.9
FEEDBACK = 1.0
GOLDEN = 2.399963229728653

LANES = 128
SUBLANES = 8
AXES = ("slab", "sub")
VMEM = pl.BlockSpec(memory_space=pltpu.VMEM)
NT = (((1,), (1,)), ((), ()))
TAKE = lax.GatherDimensionNumbers(
    offset_dims=(),
    collapsed_slice_dims=(1,),
    start_index_map=(1,),
    operand_batching_dims=(0,),
    start_indices_batching_dims=(0,),
)


def take(rows, lanes):
    return lax.gather(
        rows,
        lanes[:, :, None],
        dimension_numbers=TAKE,
        slice_sizes=(1, 1),
        mode=lax.GatherScatterMode.PROMISE_IN_BOUNDS,
    )


def lookup(rows, index, shift=7):
    high, low = index >> shift, index & (LANES - 1)
    out = jnp.zeros(index.shape, rows[0].dtype)
    for h, row in enumerate(rows):
        out = jnp.where(high == h, take(jnp.broadcast_to(row, index.shape), low), out)
    return out


def iota(shape, axis):
    return lax.broadcasted_iota(jnp.int32, shape, axis)


def split3(x):
    a = x.astype(jnp.bfloat16).astype(jnp.float32)
    rest = x - a
    b = rest.astype(jnp.bfloat16).astype(jnp.float32)
    return a, b, rest - b


def parity(axis):
    if lax.axis_size(axis) % 2:
        return 0
    return lax.rem(lax.axis_index(axis), 2)


def ordered_lists(moves_ref):
    lists = []
    for base, axis in ((0, "slab"), (2, "sub")):
        odd = parity(axis)
        one, two = moves_ref[base : base + 1], moves_ref[base + 1 : base + 2]
        lists += [jnp.where(odd == 0, one, two), jnp.where(odd == 0, two, one)]
    return lists


def departures(v_ref, moves_ref, *out_refs):
    comps, count = v_ref.shape
    lists = ordered_lists(moves_ref)
    for index, out_ref, lane in zip(
        lists,
        (out_refs[0], out_refs[1], out_refs[2], out_refs[2]),
        (0, 0, 0, LANES),
    ):
        index = jnp.broadcast_to(index, (comps, LANES))
        high, low = index >> 7, index & (LANES - 1)
        out = jnp.zeros((comps, LANES), jnp.float32)
        for r in range(count // LANES):
            tile = v_ref[:, r * LANES : (r + 1) * LANES]
            out = jnp.where(high == r, take(tile, low), out)
        out_ref[:, lane : lane + LANES] = out


def prepare(v_ref, moves_ref, cell_ref, choice_ref, vd_ref, source_ref, celld_ref, base_ref, slotcell_ref, normal_ref, keep_ref):
    comps, count = v_ref.shape
    rows = count // LANES
    cells = choice_ref.shape[1]
    blocks = cells // LANES
    lists = ordered_lists(moves_ref)
    for r in range(rows):
        span = slice(r * LANES, (r + 1) * LANES)
        celld_ref[r : r + 1, :] = cell_ref[0:1, span]
        for c in range(comps):
            vd_ref[c, r : r + 1, :] = v_ref[c : c + 1, span]

    slots = jnp.concatenate(lists, 1)
    many = slots.shape[1]
    low = (iota((LANES, many), 0) == (slots & (LANES - 1))).astype(jnp.bfloat16)
    here = iota((rows, many), 0) == (slots >> 7)
    lane = iota((rows, many), 1)
    marks = jnp.concatenate(
        [
            jnp.where(here, (lane >> 7) + 1, 0).astype(jnp.float32),
            jnp.where(here, lane & (LANES - 1), 0).astype(jnp.float32),
        ]
    ).astype(jnp.bfloat16)
    found = lax.dot_general(marks, low, NT, preferred_element_type=jnp.float32).astype(jnp.int32)
    source = found[:rows] * LANES + found[rows:]
    source_ref[...] = source
    keep_ref[...] = jnp.where(source == 0, 1.0, 0.0)

    celld = celld_ref[...]
    four = jnp.concatenate(lists + lists, 0)
    slotcell_ref[...] = lookup([celld_ref[r : r + 1, :] for r in range(rows)], four)

    counter = (iota((1, LANES), 1) & (NAXES - 1)).astype(jnp.float32)
    height = 1.0 - (2.0 * counter + 1.0) / NAXES
    radius = jnp.sqrt(1.0 - height * height)
    table = (radius * jnp.cos(GOLDEN * counter), radius * jnp.sin(GOLDEN * counter), height)
    picks = [choice_ref[0:1, h * LANES : (h + 1) * LANES] for h in range(blocks)]
    for c in range(comps):
        entries = [take(table[c], pick) for pick in picks]
        normal_ref[c] = lookup(entries, celld)

    ones = (iota((SUBLANES - comps, LANES), 0) == 0).astype(jnp.float32)
    total = jnp.zeros((blocks * 3 * SUBLANES, LANES), jnp.float32)
    group = 4 if rows % 4 == 0 else 1
    for first in range(0, rows, group):
        left, right = [], []
        for r in range(first, first + group):
            cell = cell_ref[0:1, r * LANES : (r + 1) * LANES]
            tile = v_ref[:, r * LANES : (r + 1) * LANES] * keep_ref[r : r + 1, :]
            tile = jnp.concatenate([tile, ones], 0)
            parts = jnp.concatenate(split3(tile), 0)
            left.append(jnp.concatenate([jnp.where((cell >> 7) == h, parts, 0.0) for h in range(blocks)], 0))
            right.append((iota((LANES, LANES), 0) == (cell & (LANES - 1))).astype(jnp.bfloat16))
        left = jnp.concatenate(left, 1).astype(jnp.bfloat16)
        right = jnp.concatenate(right, 1)
        total += lax.dot_general(left, right, NT, preferred_element_type=jnp.float32)
    for h in range(blocks):
        part = total[h * 3 * SUBLANES : (h + 1) * 3 * SUBLANES]
        base_ref[h * SUBLANES : (h + 1) * SUBLANES] = part[:8] + part[8:16] + part[16:]


def relax(a_ref, b_ref, s_ref, vd_ref, source_ref, celld_ref, base_ref, slotcell_ref, normal_ref, send_ref, profile_ref, mean_ref, turned_ref):
    comps, rows, _ = vd_ref.shape
    blocks = base_ref.shape[0] // SUBLANES
    arrived = [a_ref[...], b_ref[...], s_ref[:, :LANES], s_ref[:, LANES:]]

    pad = jnp.zeros((SUBLANES - comps, LANES), jnp.float32)
    left, right = [], []
    for k, block in enumerate(arrived):
        cell = slotcell_ref[k : k + 1, :]
        parts = jnp.concatenate(split3(jnp.concatenate([block, pad], 0)), 0)
        left.append(jnp.concatenate([jnp.where((cell >> 7) == h, parts, 0.0) for h in range(blocks)], 0))
        right.append((iota((LANES, LANES), 0) == (cell & (LANES - 1))).astype(jnp.bfloat16))
    left = jnp.concatenate(left, 1).astype(jnp.bfloat16)
    right = jnp.concatenate(right, 1)
    fresh = lax.dot_general(left, right, NT, preferred_element_type=jnp.float32)
    sums, means = [], []
    for h in range(blocks):
        part = fresh[h * 3 * SUBLANES : (h + 1) * 3 * SUBLANES]
        total = base_ref[h * SUBLANES : (h + 1) * SUBLANES] + (part[:8] + part[8:16] + part[16:])
        sums.append(total)
        means.append(total / jnp.maximum(jnp.broadcast_to(total[comps : comps + 1], total.shape), 1.0))

    both = jnp.concatenate([s[0:1] for s in sums] + [s[comps : comps + 1] for s in sums], 0)
    width = CZ // 2
    while width:
        both = both + pltpu.roll(both, LANES - width, 1)
        width //= 2
    columns = iota((1, LANES), 1)
    start = columns * CZ
    flow = lookup([both[h : h + 1] for h in range(blocks)], start)
    number = lookup([both[blocks + h : blocks + h + 1] for h in range(blocks)], start)
    profile = flow / jnp.maximum(number, 1.0)
    profile_ref[...] = profile[:, :CY]

    source, celld = source_ref[...], celld_ref[...]
    relative, energy = [], jnp.zeros((rows, LANES), jnp.float32)
    for c in range(comps):
        old = vd_ref[c]
        speed = jnp.where(source == 0, old, lookup([x[c : c + 1] for x in arrived], source - LANES))
        mean = lookup([m[c : c + 1] for m in means], celld)
        mean_ref[c] = mean
        relative.append(speed - mean)
        energy += relative[c] * relative[c]
    energy = jnp.sum(energy, 0, keepdims=True)
    energy = energy + pltpu.roll(energy, CY, 1)
    message = jnp.where(columns < CY, profile, energy)
    send_ref[...] = jnp.broadcast_to(message[None], send_ref.shape)

    n = [normal_ref[c] for c in range(comps)]
    along = (n[0] * relative[0] + n[1] * relative[1] + n[2] * relative[2]) * (1.0 - ROT_COS)
    for c in range(comps):
        d, e = (c + 1) % comps, (c + 2) % comps
        cross = n[d] * relative[e] - n[e] * relative[d]
        turned_ref[c] = relative[c] * ROT_COS + cross * ROT_SIN + n[c] * along


def finish(got_ref, shear_ref, mean_ref, turned_ref, celld_ref, out_ref, *, slabs, subs, particles):
    comps, rows, _ = mean_ref.shape
    got = got_ref[...].reshape(slabs * subs, LANES)
    mine = lax.rem(iota(got.shape, 0), subs) == lax.axis_index("sub")
    lane = iota(got.shape, 1)
    drift = jnp.sum(jnp.where(mine, got, 0.0), 0, keepdims=True) / (CX * slabs)
    work = jnp.sum(jnp.where(lane < CY, 0.0, got), 0, keepdims=True)
    work = jnp.sum(work, 1, keepdims=True)
    scale = lax.rsqrt(work / (3.0 * particles * RESERVOIR_HEAT) + 1e-06)
    scale = jnp.broadcast_to(scale, (rows, LANES))
    target = jnp.concatenate([shear_ref[...], jnp.zeros((1, LANES - CY), jnp.float32)], 1)
    extra = FEEDBACK * (target - drift)
    line = (celld_ref[...] // CZ) & (CY - 1)
    extra = take(jnp.broadcast_to(extra, (rows, LANES)), line)
    for c in range(comps):
        base = mean_ref[c] + extra if c == 0 else mean_ref[c]
        out = base + scale * turned_ref[c]
        for r in range(rows):
            out_ref[c : c + 1, r * LANES : (r + 1) * LANES] = out[r : r + 1, :]


def swap(blocks, axis):
    size = lax.axis_size(axis)
    one, two = blocks
    if size % 2:
        forth = [(i, (i + 1) % size) for i in range(size)]
        back = [(i, (i - 1) % size) for i in range(size)]
        return [lax.ppermute(two, axis, back), lax.ppermute(one, axis, forth)]
    even = [(i, i ^ 1) for i in range(size)]
    odd = [(i, (i + 1 if i % 2 else i - 1) % size) for i in range(size)]
    return [lax.ppermute(one, axis, even), lax.ppermute(two, axis, odd)]


def swap_joined(block, axis):
    size = lax.axis_size(axis)
    if size == 2:
        return lax.ppermute(block, axis, [(0, 1), (1, 0)])
    return jnp.concatenate(swap([block[:, :LANES], block[:, LANES:]], axis), 1)


def f32(*shape):
    return jax.ShapeDtypeStruct(shape, jnp.float32)


def i32(*shape):
    return jax.ShapeDtypeStruct(shape, jnp.int32)


def call(kernel, out_shape, inputs, scratch=(), flops=0):
    outs = jax.tree.leaves(out_shape)
    size = sum(4 * math.prod(x.shape) for x in list(inputs) + outs)
    return pl.pallas_call(
        kernel,
        out_shape=out_shape,
        in_specs=[VMEM] * len(inputs),
        out_specs=jax.tree.map(lambda _: VMEM, out_shape),
        scratch_shapes=list(scratch),
        cost_estimate=pl.CostEstimate(flops=flops, bytes_accessed=size, transcendentals=0),
    )(*inputs)


def step(speeds, cells, choices, moves, shear_target):
    slabs, subs = lax.axis_size("slab"), lax.axis_size("sub")
    comps, count = speeds.shape
    rows = count // LANES
    blocks = choices.shape[1] // LANES
    a, b, s = call(
        departures,
        (f32(comps, LANES), f32(comps, LANES), f32(comps, 2 * LANES)),
        (speeds, moves),
    )
    a, b = swap([a, b], "slab")
    s = swap_joined(s, "sub")
    dense = f32(comps, rows, LANES)
    index = i32(rows, LANES)
    vd, source, celld, base, slotcell, normal = call(
        prepare,
        (dense, index, index, f32(blocks * SUBLANES, LANES), i32(SUBLANES, LANES), dense),
        (speeds, moves, cells, choices),
        scratch=[pltpu.VMEM((rows, LANES), jnp.float32)],
        flops=2 * count * LANES * 96,
    )
    send, profile, mean, turned = call(
        relax,
        (f32(slabs * subs, 1, LANES), f32(1, CX * CY), dense, dense),
        (a, b, s, vd, source, celld, base, slotcell, normal),
    )
    got = lax.all_to_all(send, AXES, 0, 0, tiled=True)
    out = call(
        functools.partial(finish, slabs=slabs, subs=subs, particles=count * slabs * subs),
        f32(comps, count),
        (got, shear_target[None, :], mean, turned, celld),
    )
    return out, profile


def body(velocities, cell_index, axis_choice, moves, shear_target):
    speeds, profile = velocities, None
    for t in range(moves.shape[0]):
        speeds, profile = step(speeds, cell_index[t : t + 1], axis_choice[t : t + 1], moves[t], shear_target)
    return speeds, profile


def solution(mesh):
    in_specs = (
        P(None, ("slab", "sub")),
        P(None, ("slab", "sub")),
        P(None, ("slab", "sub")),
        P(None, None, ("slab", "sub")),
        P("sub"),
    )
    out_specs = (P(None, ("slab", "sub")), P("slab", "sub"))
    return jax.shard_map(body, mesh=mesh, in_specs=in_specs, out_specs=out_specs, check_vma=False)
```

```python
import functools
import math

import jax
import jax.numpy as jnp
from jax import lax
from jax.experimental import pallas as pl
from jax.experimental.pallas import tpu as pltpu
from jax.sharding import PartitionSpec as P

CX = 1
CY = 64
CZ = 8
NAXES = 64

ROT_COS = -0.6427876096865393
ROT_SIN = 0.766044443118978
RESERVOIR_HEAT = 0.9
FEEDBACK = 1.0
GOLDEN = 2.399963229728653

LANES = 128
SUBLANES = 8
AXES = ("slab", "sub")
VMEM = pl.BlockSpec(memory_space=pltpu.VMEM)
NT = (((1,), (1,)), ((), ()))
TAKE = lax.GatherDimensionNumbers(
    offset_dims=(),
    collapsed_slice_dims=(1,),
    start_index_map=(1,),
    operand_batching_dims=(0,),
    start_indices_batching_dims=(0,),
)


def take(rows, lanes):
    return lax.gather(
        rows,
        lanes[:, :, None],
        dimension_numbers=TAKE,
        slice_sizes=(1, 1),
        mode=lax.GatherScatterMode.PROMISE_IN_BOUNDS,
    )


def lookup(rows, index, shift=7):
    high, low = index >> shift, index & (LANES - 1)
    out = jnp.zeros(index.shape, rows[0].dtype)
    for h, row in enumerate(rows):
        out = jnp.where(high == h, take(jnp.broadcast_to(row, index.shape), low), out)
    return out


def iota(shape, axis):
    return lax.broadcasted_iota(jnp.int32, shape, axis)


def split3(x):
    a = x.astype(jnp.bfloat16).astype(jnp.float32)
    rest = x - a
    b = rest.astype(jnp.bfloat16).astype(jnp.float32)
    return a, b, rest - b


def parity(axis):
    if lax.axis_size(axis) % 2:
        return 0
    return lax.rem(lax.axis_index(axis), 2)


def ordered_lists(moves_ref):
    lists = []
    for base, axis in ((0, "slab"), (2, "sub")):
        odd = parity(axis)
        one, two = moves_ref[base : base + 1], moves_ref[base + 1 : base + 2]
        lists += [jnp.where(odd == 0, one, two), jnp.where(odd == 0, two, one)]
    return lists


def departures(v_ref, moves_ref, *out_refs):
    comps, count = v_ref.shape
    lists = ordered_lists(moves_ref)
    for index, out_ref, lane in zip(
        lists,
        (out_refs[0], out_refs[1], out_refs[2], out_refs[2]),
        (0, 0, 0, LANES),
    ):
        index = jnp.broadcast_to(index, (comps, LANES))
        high, low = index >> 7, index & (LANES - 1)
        out = jnp.zeros((comps, LANES), jnp.float32)
        for r in range(count // LANES):
            tile = v_ref[:, r * LANES : (r + 1) * LANES]
            out = jnp.where(high == r, take(tile, low), out)
        out_ref[:, lane : lane + LANES] = out


def prepare(v_ref, moves_ref, cell_ref, choice_ref, shear_ref, vd_ref, source_ref, celld_ref, base_ref, slotcell_ref, normal_ref, target_ref, keep_ref):
    comps, count = v_ref.shape
    rows = count // LANES
    cells = choice_ref.shape[1]
    blocks = cells // LANES
    lists = ordered_lists(moves_ref)
    target_ref[...] = jnp.concatenate([shear_ref[...], jnp.zeros((1, LANES - CY), jnp.float32)], 1)
    for r in range(rows):
        span = slice(r * LANES, (r + 1) * LANES)
        celld_ref[r : r + 1, :] = cell_ref[0:1, span]
        for c in range(comps):
            vd_ref[c, r : r + 1, :] = v_ref[c : c + 1, span]

    slots = jnp.concatenate(lists, 1)
    many = slots.shape[1]
    low = (iota((LANES, many), 0) == (slots & (LANES - 1))).astype(jnp.bfloat16)
    here = iota((rows, many), 0) == (slots >> 7)
    lane = iota((rows, many), 1)
    marks = jnp.concatenate(
        [
            jnp.where(here, (lane >> 7) + 1, 0).astype(jnp.float32),
            jnp.where(here, lane & (LANES - 1), 0).astype(jnp.float32),
        ]
    ).astype(jnp.bfloat16)
    found = lax.dot_general(marks, low, NT, preferred_element_type=jnp.float32).astype(jnp.int32)
    source = found[:rows] * LANES + found[rows:]
    source_ref[...] = source
    keep_ref[...] = jnp.where(source == 0, 1.0, 0.0)

    celld = celld_ref[...]
    four = jnp.concatenate(lists + lists, 0)
    slotcell_ref[...] = lookup([celld_ref[r : r + 1, :] for r in range(rows)], four)

    counter = (iota((1, LANES), 1) & (NAXES - 1)).astype(jnp.float32)
    height = 1.0 - (2.0 * counter + 1.0) / NAXES
    radius = jnp.sqrt(1.0 - height * height)
    table = (radius * jnp.cos(GOLDEN * counter), radius * jnp.sin(GOLDEN * counter), height)
    picks = [choice_ref[0:1, h * LANES : (h + 1) * LANES] for h in range(blocks)]
    for c in range(comps):
        entries = [take(table[c], pick) for pick in picks]
        normal_ref[c] = lookup(entries, celld)

    ones = (iota((SUBLANES - comps, LANES), 0) == 0).astype(jnp.float32)
    total = jnp.zeros((blocks * 3 * SUBLANES, LANES), jnp.float32)
    group = 4 if rows % 4 == 0 else 1
    for first in range(0, rows, group):
        left, right = [], []
        for r in range(first, first + group):
            cell = cell_ref[0:1, r * LANES : (r + 1) * LANES]
            tile = v_ref[:, r * LANES : (r + 1) * LANES] * keep_ref[r : r + 1, :]
            tile = jnp.concatenate([tile, ones], 0)
            parts = jnp.concatenate(split3(tile), 0)
            left.append(jnp.concatenate([jnp.where((cell >> 7) == h, parts, 0.0) for h in range(blocks)], 0))
            right.append((iota((LANES, LANES), 0) == (cell & (LANES - 1))).astype(jnp.bfloat16))
        left = jnp.concatenate(left, 1).astype(jnp.bfloat16)
        right = jnp.concatenate(right, 1)
        total += lax.dot_general(left, right, NT, preferred_element_type=jnp.float32)
    for h in range(blocks):
        part = total[h * 3 * SUBLANES : (h + 1) * 3 * SUBLANES]
        base_ref[h * SUBLANES : (h + 1) * SUBLANES] = part[:8] + part[8:16] + part[16:]


def relax(a_ref, b_ref, s_ref, vd_ref, source_ref, celld_ref, base_ref, slotcell_ref, normal_ref, send_ref, profile_ref, mean_ref, turned_ref):
    comps, rows, _ = vd_ref.shape
    blocks = base_ref.shape[0] // SUBLANES
    arrived = [a_ref[...], b_ref[...], s_ref[:, :LANES], s_ref[:, LANES:]]

    pad = jnp.zeros((SUBLANES - comps, LANES), jnp.float32)
    left, right = [], []
    for k, block in enumerate(arrived):
        cell = slotcell_ref[k : k + 1, :]
        parts = jnp.concatenate(split3(jnp.concatenate([block, pad], 0)), 0)
        left.append(jnp.concatenate([jnp.where((cell >> 7) == h, parts, 0.0) for h in range(blocks)], 0))
        right.append((iota((LANES, LANES), 0) == (cell & (LANES - 1))).astype(jnp.bfloat16))
    left = jnp.concatenate(left, 1).astype(jnp.bfloat16)
    right = jnp.concatenate(right, 1)
    fresh = lax.dot_general(left, right, NT, preferred_element_type=jnp.float32)
    sums, means = [], []
    for h in range(blocks):
        part = fresh[h * 3 * SUBLANES : (h + 1) * 3 * SUBLANES]
        total = base_ref[h * SUBLANES : (h + 1) * SUBLANES] + (part[:8] + part[8:16] + part[16:])
        sums.append(total)
        means.append(total / jnp.maximum(jnp.broadcast_to(total[comps : comps + 1], total.shape), 1.0))

    both = jnp.concatenate([s[0:1] for s in sums] + [s[comps : comps + 1] for s in sums], 0)
    width = CZ // 2
    while width:
        both = both + pltpu.roll(both, LANES - width, 1)
        width //= 2
    columns = iota((1, LANES), 1)
    start = columns * CZ
    flow = lookup([both[h : h + 1] for h in range(blocks)], start)
    number = lookup([both[blocks + h : blocks + h + 1] for h in range(blocks)], start)
    profile = flow / jnp.maximum(number, 1.0)
    profile_ref[...] = profile[:, :CY]

    source, celld = source_ref[...], celld_ref[...]
    relative, energy = [], jnp.zeros((rows, LANES), jnp.float32)
    for c in range(comps):
        old = vd_ref[c]
        speed = jnp.where(source == 0, old, lookup([x[c : c + 1] for x in arrived], source - LANES))
        mean = lookup([m[c : c + 1] for m in means], celld)
        mean_ref[c] = mean
        relative.append(speed - mean)
        energy += relative[c] * relative[c]
    energy = jnp.sum(energy, 0, keepdims=True)
    energy = energy + pltpu.roll(energy, CY, 1)
    message = jnp.where(columns < CY, profile, energy)
    send_ref[...] = jnp.broadcast_to(message[None], send_ref.shape)

    n = [normal_ref[c] for c in range(comps)]
    along = (n[0] * relative[0] + n[1] * relative[1] + n[2] * relative[2]) * (1.0 - ROT_COS)
    for c in range(comps):
        d, e = (c + 1) % comps, (c + 2) % comps
        cross = n[d] * relative[e] - n[e] * relative[d]
        turned_ref[c] = relative[c] * ROT_COS + cross * ROT_SIN + n[c] * along


def finish(got_ref, target_ref, mean_ref, turned_ref, celld_ref, out_ref, *, slabs, subs, particles):
    comps, rows, _ = mean_ref.shape
    got = got_ref[...].reshape(slabs * subs, LANES)
    mine = lax.rem(iota(got.shape, 0), subs) == lax.axis_index("sub")
    lane = iota(got.shape, 1)
    drift = jnp.sum(jnp.where(mine, got, 0.0), 0, keepdims=True) / (CX * slabs)
    work = jnp.sum(jnp.where(lane < CY, 0.0, got), 0, keepdims=True)
    work = jnp.sum(work, 1, keepdims=True)
    scale = lax.rsqrt(work / (3.0 * particles * RESERVOIR_HEAT) + 1e-06)
    scale = jnp.broadcast_to(scale, (rows, LANES))
    extra = FEEDBACK * (target_ref[...] - drift)
    line = (celld_ref[...] // CZ) & (CY - 1)
    extra = take(jnp.broadcast_to(extra, (rows, LANES)), line)
    for c in range(comps):
        base = mean_ref[c] + extra if c == 0 else mean_ref[c]
        out = base + scale * turned_ref[c]
        for r in range(rows):
            out_ref[c : c + 1, r * LANES : (r + 1) * LANES] = out[r : r + 1, :]


def swap(blocks, axis):
    size = lax.axis_size(axis)
    one, two = blocks
    if size % 2:
        forth = [(i, (i + 1) % size) for i in range(size)]
        back = [(i, (i - 1) % size) for i in range(size)]
        return [lax.ppermute(two, axis, back), lax.ppermute(one, axis, forth)]
    even = [(i, i ^ 1) for i in range(size)]
    odd = [(i, (i + 1 if i % 2 else i - 1) % size) for i in range(size)]
    second = lax.ppermute(two, axis, odd)
    return [lax.ppermute(one, axis, even), second]


def swap_joined(block, axis):
    size = lax.axis_size(axis)
    if size == 2:
        return lax.ppermute(block, axis, [(0, 1), (1, 0)])
    return jnp.concatenate(swap([block[:, :LANES], block[:, LANES:]], axis), 1)


def f32(*shape):
    return pltpu.VMEM(shape, jnp.float32)


def i32(*shape):
    return pltpu.VMEM(shape, jnp.int32)


def call(kernel, out_shape, inputs, scratch=(), flops=0, resident=True):
    size = sum(4 * math.prod(x.shape) for x in inputs)
    if resident:
        inputs = [pltpu.with_memory_space_constraint(x, pltpu.VMEM) for x in inputs]
    return pl.pallas_call(
        kernel,
        out_shape=out_shape,
        in_specs=[VMEM] * len(inputs),
        out_specs=jax.tree.map(lambda _: VMEM, out_shape),
        scratch_shapes=list(scratch),
        cost_estimate=pl.CostEstimate(flops=flops, bytes_accessed=size, transcendentals=0),
    )(*inputs)


def step(speeds, cells, choices, moves, shear_target):
    slabs, subs = lax.axis_size("slab"), lax.axis_size("sub")
    comps, count = speeds.shape
    rows = count // LANES
    blocks = choices.shape[1] // LANES
    a, b, s = call(
        departures,
        (f32(comps, LANES), f32(comps, LANES), f32(comps, 2 * LANES)),
        (speeds, moves),
        resident=False,
    )
    a, b = swap([a, b], "slab")
    s = swap_joined(s, "sub")
    dense = f32(comps, rows, LANES)
    index = i32(rows, LANES)
    vd, source, celld, base, slotcell, normal, target = call(
        prepare,
        (dense, index, index, f32(blocks * SUBLANES, LANES), i32(SUBLANES, LANES), dense, f32(1, LANES)),
        (speeds, moves, cells, choices, shear_target[None, :]),
        scratch=[pltpu.VMEM((rows, LANES), jnp.float32)],
        flops=2 * count * LANES * 96,
    )
    send, profile, mean, turned = call(
        relax,
        (f32(slabs * subs, 1, LANES), jax.ShapeDtypeStruct((1, CX * CY), jnp.float32), dense, dense),
        (a, b, s, vd, source, celld, base, slotcell, normal),
    )
    got = lax.all_to_all(send, AXES, 0, 0, tiled=True)
    out = call(
        functools.partial(finish, slabs=slabs, subs=subs, particles=count * slabs * subs),
        jax.ShapeDtypeStruct((comps, count), jnp.float32),
        (got, target, mean, turned, celld),
    )
    return out, profile


def body(velocities, cell_index, axis_choice, moves, shear_target):
    speeds, profile = velocities, None
    for t in range(moves.shape[0]):
        speeds, profile = step(speeds, cell_index[t : t + 1], axis_choice[t : t + 1], moves[t], shear_target)
    return speeds, profile


def solution(mesh):
    in_specs = (
        P(None, ("slab", "sub")),
        P(None, ("slab", "sub")),
        P(None, ("slab", "sub")),
        P(None, None, ("slab", "sub")),
        P("sub"),
    )
    out_specs = (P(None, ("slab", "sub")), P("slab", "sub"))
    return jax.shard_map(body, mesh=mesh, in_specs=in_specs, out_specs=out_specs, check_vma=False)
```

```python
import functools
import math

import jax
import jax.numpy as jnp
from jax import lax
from jax.experimental import pallas as pl
from jax.experimental.pallas import tpu as pltpu
from jax.sharding import PartitionSpec as P


CX = 1
CY = 64
CZ = 8
NAXES = 64

ROT_COS = -0.6427876096865393
ROT_SIN = 0.766044443118978
RESERVOIR_HEAT = 0.9
FEEDBACK = 1.0
GOLDEN = 2.399963229728653

LANES = 128
SUBLANES = 8
AXES = ("slab", "sub")
VMEM = pl.BlockSpec(memory_space=pltpu.VMEM)
NT = (((1,), (1,)), ((), ()))
TAKE = lax.GatherDimensionNumbers(
    offset_dims=(),
    collapsed_slice_dims=(1,),
    start_index_map=(1,),
    operand_batching_dims=(0,),
    start_indices_batching_dims=(0,),
)


def take(rows, lanes):
    return lax.gather(
        rows,
        lanes[:, :, None],
        dimension_numbers=TAKE,
        slice_sizes=(1, 1),
        mode=lax.GatherScatterMode.PROMISE_IN_BOUNDS,
    )


def lookup(rows, index, shift=7):
    high, low = index >> shift, index & (LANES - 1)
    out = jnp.zeros(index.shape, rows[0].dtype)
    for h, row in enumerate(rows):
        out = jnp.where(high == h, take(jnp.broadcast_to(row, index.shape), low), out)
    return out


def iota(shape, axis):
    return lax.broadcasted_iota(jnp.int32, shape, axis)


def split3(x):
    a = x.astype(jnp.bfloat16).astype(jnp.float32)
    rest = x - a
    b = rest.astype(jnp.bfloat16).astype(jnp.float32)
    return a, b, rest - b


def parity(axis):
    if lax.axis_size(axis) % 2:
        return 0
    return lax.rem(lax.axis_index(axis), 2)


def ordered_lists(moves_ref):
    lists = []
    for base, axis in ((0, "slab"), (2, "sub")):
        odd = parity(axis)
        one, two = moves_ref[base : base + 1], moves_ref[base + 1 : base + 2]
        lists += [jnp.where(odd == 0, one, two), jnp.where(odd == 0, two, one)]
    return lists


def departures(v_ref, moves_ref, *out_refs, which):
    comps, count = v_ref.shape
    lists = ordered_lists(moves_ref)
    for k, out_ref, lane in zip(which, out_refs[:1] + out_refs[1:] * 2, (0, 0, LANES)):
        index = lists[k]
        index = jnp.broadcast_to(index, (comps, LANES))
        high, low = index >> 7, index & (LANES - 1)
        out = jnp.zeros((comps, LANES), jnp.float32)
        for r in range(count // LANES):
            tile = v_ref[:, r * LANES : (r + 1) * LANES]
            out = jnp.where(high == r, take(tile, low), out)
        out_ref[:, lane : lane + LANES] = out


def prepare(v_ref, moves_ref, cell_ref, choice_ref, shear_ref, vd_ref, source_ref, celld_ref, base_ref, slotcell_ref, normal_ref, target_ref, keep_ref):
    comps, count = v_ref.shape
    rows = count // LANES
    cells = choice_ref.shape[1]
    blocks = cells // LANES
    lists = ordered_lists(moves_ref)
    target_ref[...] = jnp.concatenate([shear_ref[...], jnp.zeros((1, LANES - CY), jnp.float32)], 1)
    for r in range(rows):
        span = slice(r * LANES, (r + 1) * LANES)
        celld_ref[r : r + 1, :] = cell_ref[0:1, span]
        for c in range(comps):
            vd_ref[c, r : r + 1, :] = v_ref[c : c + 1, span]

    slots = jnp.concatenate(lists, 1)
    many = slots.shape[1]
    low = (iota((LANES, many), 0) == (slots & (LANES - 1))).astype(jnp.bfloat16)
    here = iota((rows, many), 0) == (slots >> 7)
    lane = iota((rows, many), 1)
    marks = jnp.concatenate(
        [
            jnp.where(here, (lane >> 7) + 1, 0).astype(jnp.float32),
            jnp.where(here, lane & (LANES - 1), 0).astype(jnp.float32),
        ]
    ).astype(jnp.bfloat16)
    found = lax.dot_general(marks, low, NT, preferred_element_type=jnp.float32).astype(jnp.int32)
    source = found[:rows] * LANES + found[rows:]
    source_ref[...] = source
    keep_ref[...] = jnp.where(source == 0, 1.0, 0.0)

    celld = celld_ref[...]
    four = jnp.concatenate(lists + lists, 0)
    slotcell_ref[...] = lookup([celld_ref[r : r + 1, :] for r in range(rows)], four)

    counter = (iota((1, LANES), 1) & (NAXES - 1)).astype(jnp.float32)
    height = 1.0 - (2.0 * counter + 1.0) / NAXES
    radius = jnp.sqrt(1.0 - height * height)
    table = (radius * jnp.cos(GOLDEN * counter), radius * jnp.sin(GOLDEN * counter), height)
    picks = [choice_ref[0:1, h * LANES : (h + 1) * LANES] for h in range(blocks)]
    for c in range(comps):
        entries = [take(table[c], pick) for pick in picks]
        normal_ref[c] = lookup(entries, celld)

    ones = (iota((SUBLANES - comps, LANES), 0) == 0).astype(jnp.float32)
    total = jnp.zeros((blocks * 3 * SUBLANES, LANES), jnp.float32)
    group = 4 if rows % 4 == 0 else 1
    for first in range(0, rows, group):
        left, right = [], []
        for r in range(first, first + group):
            cell = cell_ref[0:1, r * LANES : (r + 1) * LANES]
            tile = v_ref[:, r * LANES : (r + 1) * LANES] * keep_ref[r : r + 1, :]
            tile = jnp.concatenate([tile, ones], 0)
            parts = jnp.concatenate(split3(tile), 0)
            left.append(jnp.concatenate([jnp.where((cell >> 7) == h, parts, 0.0) for h in range(blocks)], 0))
            right.append((iota((LANES, LANES), 0) == (cell & (LANES - 1))).astype(jnp.bfloat16))
        left = jnp.concatenate(left, 1).astype(jnp.bfloat16)
        right = jnp.concatenate(right, 1)
        total += lax.dot_general(left, right, NT, preferred_element_type=jnp.float32)
    for h in range(blocks):
        part = total[h * 3 * SUBLANES : (h + 1) * 3 * SUBLANES]
        base_ref[h * SUBLANES : (h + 1) * SUBLANES] = part[:8] + part[8:16] + part[16:]


def relax(a_ref, b_ref, s_ref, vd_ref, source_ref, celld_ref, base_ref, slotcell_ref, normal_ref, send_ref, profile_ref, mean_ref, turned_ref):
    comps, rows, _ = vd_ref.shape
    blocks = base_ref.shape[0] // SUBLANES
    arrived = [a_ref[...], b_ref[...], s_ref[:, :LANES], s_ref[:, LANES:]]

    pad = jnp.zeros((SUBLANES - comps, LANES), jnp.float32)
    left, right = [], []
    for k, block in enumerate(arrived):
        cell = slotcell_ref[k : k + 1, :]
        parts = jnp.concatenate(split3(jnp.concatenate([block, pad], 0)), 0)
        left.append(jnp.concatenate([jnp.where((cell >> 7) == h, parts, 0.0) for h in range(blocks)], 0))
        right.append((iota((LANES, LANES), 0) == (cell & (LANES - 1))).astype(jnp.bfloat16))
    left = jnp.concatenate(left, 1).astype(jnp.bfloat16)
    right = jnp.concatenate(right, 1)
    fresh = lax.dot_general(left, right, NT, preferred_element_type=jnp.float32)
    sums, means = [], []
    for h in range(blocks):
        part = fresh[h * 3 * SUBLANES : (h + 1) * 3 * SUBLANES]
        total = base_ref[h * SUBLANES : (h + 1) * SUBLANES] + (part[:8] + part[8:16] + part[16:])
        sums.append(total)
        means.append(total / jnp.maximum(jnp.broadcast_to(total[comps : comps + 1], total.shape), 1.0))

    both = jnp.concatenate([s[0:1] for s in sums] + [s[comps : comps + 1] for s in sums], 0)
    width = CZ // 2
    while width:
        both = both + pltpu.roll(both, LANES - width, 1)
        width //= 2
    columns = iota((1, LANES), 1)
    start = columns * CZ
    flow = lookup([both[h : h + 1] for h in range(blocks)], start)
    number = lookup([both[blocks + h : blocks + h + 1] for h in range(blocks)], start)
    profile = flow / jnp.maximum(number, 1.0)
    profile_ref[...] = profile[:, :CY]

    source, celld = source_ref[...], celld_ref[...]
    relative, energy = [], jnp.zeros((rows, LANES), jnp.float32)
    for c in range(comps):
        old = vd_ref[c]
        speed = jnp.where(source == 0, old, lookup([x[c : c + 1] for x in arrived], source - LANES))
        mean = lookup([m[c : c + 1] for m in means], celld)
        mean_ref[c] = mean
        relative.append(speed - mean)
        energy += relative[c] * relative[c]
    energy = jnp.sum(energy, 0, keepdims=True)
    energy = energy + pltpu.roll(energy, CY, 1)
    message = jnp.where(columns < CY, profile, energy)
    send_ref[...] = jnp.broadcast_to(message[None], send_ref.shape)

    n = [normal_ref[c] for c in range(comps)]
    along = (n[0] * relative[0] + n[1] * relative[1] + n[2] * relative[2]) * (1.0 - ROT_COS)
    for c in range(comps):
        d, e = (c + 1) % comps, (c + 2) % comps
        cross = n[d] * relative[e] - n[e] * relative[d]
        turned_ref[c] = relative[c] * ROT_COS + cross * ROT_SIN + n[c] * along


def finish(got_ref, target_ref, mean_ref, turned_ref, celld_ref, out_ref, *, slabs, subs, particles):
    comps, rows, _ = mean_ref.shape
    got = got_ref[...].reshape(slabs * subs, LANES)
    mine = lax.rem(iota(got.shape, 0), subs) == lax.axis_index("sub")
    lane = iota(got.shape, 1)
    drift = jnp.sum(jnp.where(mine, got, 0.0), 0, keepdims=True) / (CX * slabs)
    work = jnp.sum(jnp.where(lane < CY, 0.0, got), 0, keepdims=True)
    work = jnp.sum(work, 1, keepdims=True)
    scale = lax.rsqrt(work / (3.0 * particles * RESERVOIR_HEAT) + 1e-06)
    scale = jnp.broadcast_to(scale, (rows, LANES))
    extra = FEEDBACK * (target_ref[...] - drift)
    line = (celld_ref[...] // CZ) & (CY - 1)
    extra = take(jnp.broadcast_to(extra, (rows, LANES)), line)
    for c in range(comps):
        base = mean_ref[c] + extra if c == 0 else mean_ref[c]
        out = base + scale * turned_ref[c]
        for r in range(rows):
            out_ref[c : c + 1, r * LANES : (r + 1) * LANES] = out[r : r + 1, :]


def swap(blocks, axis):
    size = lax.axis_size(axis)
    one, two = blocks
    if size % 2:
        forth = [(i, (i + 1) % size) for i in range(size)]
        back = [(i, (i - 1) % size) for i in range(size)]
        return [lax.ppermute(two, axis, back), lax.ppermute(one, axis, forth)]
    even = [(i, i ^ 1) for i in range(size)]
    odd = [(i, (i + 1 if i % 2 else i - 1) % size) for i in range(size)]
    second = lax.ppermute(two, axis, odd)
    first = lax.ppermute(one, axis, even)
    return [first, second]


def swap_joined(block, axis):
    size = lax.axis_size(axis)
    if size == 2:
        return lax.ppermute(block, axis, [(0, 1), (1, 0)])
    return jnp.concatenate(swap([block[:, :LANES], block[:, LANES:]], axis), 1)


def f32(*shape):
    return pltpu.VMEM(shape, jnp.float32)


def i32(*shape):
    return pltpu.VMEM(shape, jnp.int32)


def call(kernel, out_shape, inputs, scratch=(), flops=0, resident=True):
    size = sum(4 * math.prod(x.shape) for x in inputs)
    if resident:
        inputs = [pltpu.with_memory_space_constraint(x, pltpu.VMEM) for x in inputs]
    return pl.pallas_call(
        kernel,
        out_shape=out_shape,
        in_specs=[VMEM] * len(inputs),
        out_specs=jax.tree.map(lambda _: VMEM, out_shape),
        scratch_shapes=list(scratch),
        cost_estimate=pl.CostEstimate(flops=flops, bytes_accessed=size, transcendentals=0),
    )(*inputs)


def step(speeds, cells, choices, moves, shear_target):
    slabs, subs = lax.axis_size("slab"), lax.axis_size("sub")
    comps, count = speeds.shape
    rows = count // LANES
    blocks = choices.shape[1] // LANES
    (b,) = call(
        functools.partial(departures, which=(1,)),
        (f32(comps, LANES),),
        (speeds, moves),
        resident=False,
    )
    a, s = call(
        functools.partial(departures, which=(0, 2, 3)),
        (f32(comps, LANES), f32(comps, 2 * LANES)),
        (speeds, moves),
    )
    a, b = swap([a, b], "slab")
    s = swap_joined(s, "sub")
    dense = f32(comps, rows, LANES)
    index = i32(rows, LANES)
    vd, source, celld, base, slotcell, normal, target = call(
        prepare,
        (dense, index, index, f32(blocks * SUBLANES, LANES), i32(SUBLANES, LANES), dense, f32(1, LANES)),
        (speeds, moves, cells, choices, shear_target[None, :]),
        scratch=[pltpu.VMEM((rows, LANES), jnp.float32)],
        flops=2 * count * LANES * 96,
    )
    send, profile, mean, turned = call(
        relax,
        (f32(slabs * subs, 1, LANES), jax.ShapeDtypeStruct((1, CX * CY), jnp.float32), dense, dense),
        (a, b, s, vd, source, celld, base, slotcell, normal),
    )
    got = lax.all_to_all(send, AXES, 0, 0, tiled=True)
    out = call(
        functools.partial(finish, slabs=slabs, subs=subs, particles=count * slabs * subs),
        jax.ShapeDtypeStruct((comps, count), jnp.float32),
        (got, target, mean, turned, celld),
    )
    return out, profile


def body(velocities, cell_index, axis_choice, moves, shear_target):
    speeds, profile = velocities, None
    for t in range(moves.shape[0]):
        speeds, profile = step(speeds, cell_index[t : t + 1], axis_choice[t : t + 1], moves[t], shear_target)
    return speeds, profile


def solution(mesh):
    in_specs = (
        P(None, ("slab", "sub")),
        P(None, ("slab", "sub")),
        P(None, ("slab", "sub")),
        P(None, None, ("slab", "sub")),
        P("sub"),
    )
    out_specs = (P(None, ("slab", "sub")), P("slab", "sub"))
    return jax.shard_map(body, mesh=mesh, in_specs=in_specs, out_specs=out_specs, check_vma=False)
```

```python
import functools
import math

import jax
import jax.numpy as jnp
from jax import lax
from jax.experimental import pallas as pl
from jax.experimental.pallas import tpu as pltpu
from jax.sharding import PartitionSpec as P


CX = 1
CY = 64
CZ = 8
NAXES = 64

ROT_COS = -0.6427876096865393
ROT_SIN = 0.766044443118978
RESERVOIR_HEAT = 0.9
FEEDBACK = 1.0
GOLDEN = 2.399963229728653

LANES = 128
SUBLANES = 8
AXES = ("slab", "sub")
VMEM = pl.BlockSpec(memory_space=pltpu.VMEM)
NT = (((1,), (1,)), ((), ()))
TAKE = lax.GatherDimensionNumbers(
    offset_dims=(),
    collapsed_slice_dims=(1,),
    start_index_map=(1,),
    operand_batching_dims=(0,),
    start_indices_batching_dims=(0,),
)


def take(rows, lanes):
    return lax.gather(
        rows,
        lanes[:, :, None],
        dimension_numbers=TAKE,
        slice_sizes=(1, 1),
        mode=lax.GatherScatterMode.PROMISE_IN_BOUNDS,
    )


def lookup(rows, index, shift=7):
    high, low = index >> shift, index & (LANES - 1)
    out = jnp.zeros(index.shape, rows[0].dtype)
    for h, row in enumerate(rows):
        out = jnp.where(high == h, take(jnp.broadcast_to(row, index.shape), low), out)
    return out


def iota(shape, axis):
    return lax.broadcasted_iota(jnp.int32, shape, axis)


def split3(x):
    a = x.astype(jnp.bfloat16).astype(jnp.float32)
    rest = x - a
    b = rest.astype(jnp.bfloat16).astype(jnp.float32)
    return a, b, rest - b


def parity(axis):
    if lax.axis_size(axis) % 2:
        return 0
    return lax.rem(lax.axis_index(axis), 2)


def ordered_lists(moves_ref):
    lists = []
    for base, axis in ((0, "slab"), (2, "sub")):
        odd = parity(axis)
        one, two = moves_ref[base : base + 1], moves_ref[base + 1 : base + 2]
        lists += [jnp.where(odd == 0, one, two), jnp.where(odd == 0, two, one)]
    return lists


def chunks(count):
    size = SUBLANES * LANES if count % (SUBLANES * LANES) == 0 else LANES
    return [(k, pl.ds(k * size, size), range(k * size // LANES, (k + 1) * size // LANES)) for k in range(count // size)]


def first_departure(v_hbm, moves_hbm, out_ref, v_ref, moves_ref, sems):
    parts = chunks(v_ref.shape[1])
    copies = [pltpu.make_async_copy(moves_hbm, moves_ref, sems.at[len(parts)])]
    copies += [pltpu.make_async_copy(v_hbm.at[:, span], v_ref.at[:, span], sems.at[k]) for k, span, _ in parts]
    for copy in copies:
        copy.start()
    copies[0].wait()
    index = ordered_lists(moves_ref)[1]
    comps = v_ref.shape[0]
    index = jnp.broadcast_to(index, (comps, LANES))
    high, low = index >> 7, index & (LANES - 1)
    out = jnp.zeros((comps, LANES), jnp.float32)
    for copy, (_, _, rows) in zip(copies[1:], parts):
        copy.wait()
        for r in rows:
            out = jnp.where(high == r, take(v_ref[:, r * LANES : (r + 1) * LANES], low), out)
    out_ref[...] = out


def other_departures(v_ref, moves_ref, a_ref, s_ref):
    comps, count = v_ref.shape
    lists = ordered_lists(moves_ref)
    for k, out_ref, lane in ((0, a_ref, 0), (2, s_ref, 0), (3, s_ref, LANES)):
        index = jnp.broadcast_to(lists[k], (comps, LANES))
        high, low = index >> 7, index & (LANES - 1)
        out = jnp.zeros((comps, LANES), jnp.float32)
        for r in range(count // LANES):
            out = jnp.where(high == r, take(v_ref[:, r * LANES : (r + 1) * LANES], low), out)
        out_ref[:, lane : lane + LANES] = out


def prepare(v_ref, moves_ref, cell_ref, choice_ref, shear_ref, vd_ref, source_ref, celld_ref, base_ref, slotcell_ref, normal_ref, target_ref, keep_ref):
    comps, count = v_ref.shape
    rows = count // LANES
    cells = choice_ref.shape[1]
    blocks = cells // LANES
    lists = ordered_lists(moves_ref)
    target_ref[...] = jnp.concatenate([shear_ref[...], jnp.zeros((1, LANES - CY), jnp.float32)], 1)
    for r in range(rows):
        span = slice(r * LANES, (r + 1) * LANES)
        celld_ref[r : r + 1, :] = cell_ref[0:1, span]
        for c in range(comps):
            vd_ref[c, r : r + 1, :] = v_ref[c : c + 1, span]

    slots = jnp.concatenate(lists, 1)
    many = slots.shape[1]
    low = (iota((LANES, many), 0) == (slots & (LANES - 1))).astype(jnp.bfloat16)
    here = iota((rows, many), 0) == (slots >> 7)
    lane = iota((rows, many), 1)
    marks = jnp.concatenate(
        [
            jnp.where(here, (lane >> 7) + 1, 0).astype(jnp.float32),
            jnp.where(here, lane & (LANES - 1), 0).astype(jnp.float32),
        ]
    ).astype(jnp.bfloat16)
    found = lax.dot_general(marks, low, NT, preferred_element_type=jnp.float32).astype(jnp.int32)
    source = found[:rows] * LANES + found[rows:]
    source_ref[...] = source
    keep_ref[...] = jnp.where(source == 0, 1.0, 0.0)

    celld = celld_ref[...]
    four = jnp.concatenate(lists + lists, 0)
    slotcell_ref[...] = lookup([celld_ref[r : r + 1, :] for r in range(rows)], four)

    counter = (iota((1, LANES), 1) & (NAXES - 1)).astype(jnp.float32)
    height = 1.0 - (2.0 * counter + 1.0) / NAXES
    radius = jnp.sqrt(1.0 - height * height)
    table = (radius * jnp.cos(GOLDEN * counter), radius * jnp.sin(GOLDEN * counter), height)
    picks = [choice_ref[0:1, h * LANES : (h + 1) * LANES] for h in range(blocks)]
    for c in range(comps):
        entries = [take(table[c], pick) for pick in picks]
        normal_ref[c] = lookup(entries, celld)

    ones = (iota((SUBLANES - comps, LANES), 0) == 0).astype(jnp.float32)
    total = jnp.zeros((blocks * 3 * SUBLANES, LANES), jnp.float32)
    group = 4 if rows % 4 == 0 else 1
    for first in range(0, rows, group):
        left, right = [], []
        for r in range(first, first + group):
            cell = cell_ref[0:1, r * LANES : (r + 1) * LANES]
            tile = v_ref[:, r * LANES : (r + 1) * LANES] * keep_ref[r : r + 1, :]
            tile = jnp.concatenate([tile, ones], 0)
            parts = jnp.concatenate(split3(tile), 0)
            left.append(jnp.concatenate([jnp.where((cell >> 7) == h, parts, 0.0) for h in range(blocks)], 0))
            right.append((iota((LANES, LANES), 0) == (cell & (LANES - 1))).astype(jnp.bfloat16))
        left = jnp.concatenate(left, 1).astype(jnp.bfloat16)
        right = jnp.concatenate(right, 1)
        total += lax.dot_general(left, right, NT, preferred_element_type=jnp.float32)
    for h in range(blocks):
        part = total[h * 3 * SUBLANES : (h + 1) * 3 * SUBLANES]
        base_ref[h * SUBLANES : (h + 1) * SUBLANES] = part[:8] + part[8:16] + part[16:]


def relax(a_ref, b_ref, s_ref, vd_ref, source_ref, celld_ref, base_ref, slotcell_ref, normal_ref, send_ref, profile_ref, mean_ref, turned_ref):
    comps, rows, _ = vd_ref.shape
    blocks = base_ref.shape[0] // SUBLANES
    arrived = [a_ref[...], b_ref[...], s_ref[:, :LANES], s_ref[:, LANES:]]

    pad = jnp.zeros((SUBLANES - comps, LANES), jnp.float32)
    left, right = [], []
    for k, block in enumerate(arrived):
        cell = slotcell_ref[k : k + 1, :]
        parts = jnp.concatenate(split3(jnp.concatenate([block, pad], 0)), 0)
        left.append(jnp.concatenate([jnp.where((cell >> 7) == h, parts, 0.0) for h in range(blocks)], 0))
        right.append((iota((LANES, LANES), 0) == (cell & (LANES - 1))).astype(jnp.bfloat16))
    left = jnp.concatenate(left, 1).astype(jnp.bfloat16)
    right = jnp.concatenate(right, 1)
    fresh = lax.dot_general(left, right, NT, preferred_element_type=jnp.float32)
    sums, means = [], []
    for h in range(blocks):
        part = fresh[h * 3 * SUBLANES : (h + 1) * 3 * SUBLANES]
        total = base_ref[h * SUBLANES : (h + 1) * SUBLANES] + (part[:8] + part[8:16] + part[16:])
        sums.append(total)
        means.append(total / jnp.maximum(jnp.broadcast_to(total[comps : comps + 1], total.shape), 1.0))

    both = jnp.concatenate([s[0:1] for s in sums] + [s[comps : comps + 1] for s in sums], 0)
    width = CZ // 2
    while width:
        both = both + pltpu.roll(both, LANES - width, 1)
        width //= 2
    columns = iota((1, LANES), 1)
    start = columns * CZ
    flow = lookup([both[h : h + 1] for h in range(blocks)], start)
    number = lookup([both[blocks + h : blocks + h + 1] for h in range(blocks)], start)
    profile = flow / jnp.maximum(number, 1.0)
    profile_ref[...] = profile[:, :CY]

    source, celld = source_ref[...], celld_ref[...]
    relative, energy = [], jnp.zeros((rows, LANES), jnp.float32)
    for c in range(comps):
        old = vd_ref[c]
        speed = jnp.where(source == 0, old, lookup([x[c : c + 1] for x in arrived], source - LANES))
        mean = lookup([m[c : c + 1] for m in means], celld)
        mean_ref[c] = mean
        relative.append(speed - mean)
        energy += relative[c] * relative[c]
    energy = jnp.sum(energy, 0, keepdims=True)
    energy = energy + pltpu.roll(energy, CY, 1)
    message = jnp.where(columns < CY, profile, energy)
    send_ref[...] = jnp.broadcast_to(message[None], send_ref.shape)

    n = [normal_ref[c] for c in range(comps)]
    along = (n[0] * relative[0] + n[1] * relative[1] + n[2] * relative[2]) * (1.0 - ROT_COS)
    for c in range(comps):
        d, e = (c + 1) % comps, (c + 2) % comps
        cross = n[d] * relative[e] - n[e] * relative[d]
        turned_ref[c] = relative[c] * ROT_COS + cross * ROT_SIN + n[c] * along


def finish(got_ref, target_ref, profile_ref, mean_ref, turned_ref, celld_ref, out_hbm, profile_hbm, out_ref, sems, *, slabs, subs, particles):
    comps, _, _ = mean_ref.shape
    parts = chunks(out_ref.shape[1])
    copies = [pltpu.make_async_copy(profile_ref, profile_hbm, sems.at[len(parts)])]
    copies[0].start()
    got = got_ref[...].reshape(slabs * subs, LANES)
    mine = lax.rem(iota(got.shape, 0), subs) == lax.axis_index("sub")
    lane = iota(got.shape, 1)
    drift = jnp.sum(jnp.where(mine, got, 0.0), 0, keepdims=True) / (CX * slabs)
    work = jnp.sum(jnp.where(lane < CY, 0.0, got), 0, keepdims=True)
    work = jnp.sum(work, 1, keepdims=True)
    scale = lax.rsqrt(work / (3.0 * particles * RESERVOIR_HEAT) + 1e-06)
    extra = FEEDBACK * (target_ref[...] - drift)
    for k, span, own in parts:
        own = slice(own.start, own.stop)
        shape = (own.stop - own.start, LANES)
        line = (celld_ref[own, :] // CZ) & (CY - 1)
        shift = take(jnp.broadcast_to(extra, shape), line)
        for c in range(comps):
            base = mean_ref[c, own, :] + shift if c == 0 else mean_ref[c, own, :]
            out = base + scale * turned_ref[c, own, :]
            for r in range(shape[0]):
                lanes = slice((own.start + r) * LANES, (own.start + r + 1) * LANES)
                out_ref[c : c + 1, lanes] = out[r : r + 1, :]
        copies.append(pltpu.make_async_copy(out_ref.at[:, span], out_hbm.at[:, span], sems.at[k]))
        copies[-1].start()
    for copy in copies:
        copy.wait()


def swap(blocks, axis):
    size = lax.axis_size(axis)
    one, two = blocks
    if size % 2:
        forth = [(i, (i + 1) % size) for i in range(size)]
        back = [(i, (i - 1) % size) for i in range(size)]
        return [lax.ppermute(two, axis, back), lax.ppermute(one, axis, forth)]
    even = [(i, i ^ 1) for i in range(size)]
    odd = [(i, (i + 1 if i % 2 else i - 1) % size) for i in range(size)]
    second = lax.ppermute(two, axis, odd)
    first = lax.ppermute(one, axis, even)
    return [first, second]


def swap_joined(block, axis):
    size = lax.axis_size(axis)
    if size == 2:
        return lax.ppermute(block, axis, [(0, 1), (1, 0)])
    return jnp.concatenate(swap([block[:, :LANES], block[:, LANES:]], axis), 1)


def f32(*shape):
    return pltpu.VMEM(shape, jnp.float32)


def i32(*shape):
    return pltpu.VMEM(shape, jnp.int32)


def call(kernel, out_shape, inputs, scratch=(), flops=0, resident=True):
    size = sum(4 * math.prod(x.shape) for x in inputs)
    place = VMEM
    if resident:
        inputs = [pltpu.with_memory_space_constraint(x, pltpu.VMEM) for x in inputs]
    else:
        place = pl.BlockSpec(memory_space=pl.ANY)
    return pl.pallas_call(
        kernel,
        out_shape=out_shape,
        in_specs=[place] * len(inputs),
        out_specs=jax.tree.map(lambda x: VMEM if isinstance(x, pl.MemoryRef) else pl.BlockSpec(memory_space=pl.ANY), out_shape),
        scratch_shapes=list(scratch),
        cost_estimate=pl.CostEstimate(flops=flops, bytes_accessed=size, transcendentals=0),
    )(*inputs)


def step(speeds, cells, choices, moves, shear_target):
    slabs, subs = lax.axis_size("slab"), lax.axis_size("sub")
    comps, count = speeds.shape
    rows = count // LANES
    blocks = choices.shape[1] // LANES
    many = len(chunks(count)) + 1
    b = call(
        first_departure,
        f32(comps, LANES),
        (speeds, moves),
        scratch=[pltpu.VMEM(speeds.shape, jnp.float32), pltpu.VMEM(moves.shape, jnp.int32), pltpu.SemaphoreType.DMA((many,))],
        resident=False,
    )
    a, s = call(
        other_departures,
        (f32(comps, LANES), f32(comps, 2 * LANES)),
        (speeds, moves),
    )
    a, b = swap([a, b], "slab")
    s = swap_joined(s, "sub")
    dense = f32(comps, rows, LANES)
    index = i32(rows, LANES)
    vd, source, celld, base, slotcell, normal, target = call(
        prepare,
        (dense, index, index, f32(blocks * SUBLANES, LANES), i32(SUBLANES, LANES), dense, f32(1, LANES)),
        (speeds, moves, cells, choices, shear_target[None, :]),
        scratch=[pltpu.VMEM((rows, LANES), jnp.float32)],
        flops=2 * count * LANES * 96,
    )
    send, profile, mean, turned = call(
        relax,
        (f32(slabs * subs, 1, LANES), f32(1, CX * CY), dense, dense),
        (a, b, s, vd, source, celld, base, slotcell, normal),
    )
    got = lax.all_to_all(send, AXES, 0, 0, tiled=True)
    return call(
        functools.partial(finish, slabs=slabs, subs=subs, particles=count * slabs * subs),
        (jax.ShapeDtypeStruct((comps, count), jnp.float32), jax.ShapeDtypeStruct((1, CX * CY), jnp.float32)),
        (got, target, profile, mean, turned, celld),
        scratch=[pltpu.VMEM((comps, count), jnp.float32), pltpu.SemaphoreType.DMA((many,))],
    )


def body(velocities, cell_index, axis_choice, moves, shear_target):
    speeds, profile = velocities, None
    for t in range(moves.shape[0]):
        speeds, profile = step(speeds, cell_index[t : t + 1], axis_choice[t : t + 1], moves[t], shear_target)
    return speeds, profile


def solution(mesh):
    in_specs = (
        P(None, ("slab", "sub")),
        P(None, ("slab", "sub")),
        P(None, ("slab", "sub")),
        P(None, None, ("slab", "sub")),
        P("sub"),
    )
    out_specs = (P(None, ("slab", "sub")), P("slab", "sub"))
    return jax.shard_map(body, mesh=mesh, in_specs=in_specs, out_specs=out_specs, check_vma=False)
```

```python
import functools
import math

import jax
import jax.numpy as jnp
from jax import lax
from jax.experimental import pallas as pl
from jax.experimental.pallas import tpu as pltpu
from jax.sharding import PartitionSpec as P


CX = 1
CY = 64
CZ = 8
NAXES = 64

ROT_COS = -0.6427876096865393
ROT_SIN = 0.766044443118978
RESERVOIR_HEAT = 0.9
FEEDBACK = 1.0
GOLDEN = 2.399963229728653

LANES = 128
SUBLANES = 8
AXES = ("slab", "sub")
VMEM = pl.BlockSpec(memory_space=pltpu.VMEM)
NT = (((1,), (1,)), ((), ()))
TAKE = lax.GatherDimensionNumbers(
    offset_dims=(),
    collapsed_slice_dims=(1,),
    start_index_map=(1,),
    operand_batching_dims=(0,),
    start_indices_batching_dims=(0,),
)


def take(rows, lanes):
    return lax.gather(
        rows,
        lanes[:, :, None],
        dimension_numbers=TAKE,
        slice_sizes=(1, 1),
        mode=lax.GatherScatterMode.PROMISE_IN_BOUNDS,
    )


def lookup(rows, index, shift=7):
    high, low = index >> shift, index & (LANES - 1)
    out = jnp.zeros(index.shape, rows[0].dtype)
    for h, row in enumerate(rows):
        out = jnp.where(high == h, take(jnp.broadcast_to(row, index.shape), low), out)
    return out


def iota(shape, axis):
    return lax.broadcasted_iota(jnp.int32, shape, axis)


def split3(x):
    a = x.astype(jnp.bfloat16).astype(jnp.float32)
    rest = x - a
    b = rest.astype(jnp.bfloat16).astype(jnp.float32)
    return a, b, rest - b


def parity(axis):
    if lax.axis_size(axis) % 2:
        return 0
    return lax.rem(lax.axis_index(axis), 2)


def ordered_lists(moves_ref):
    lists = []
    for base, axis in ((0, "slab"), (2, "sub")):
        odd = parity(axis)
        one, two = moves_ref[base : base + 1], moves_ref[base + 1 : base + 2]
        lists += [jnp.where(odd == 0, one, two), jnp.where(odd == 0, two, one)]
    return lists


def chunks(count):
    size = SUBLANES * LANES if count % (SUBLANES * LANES) == 0 else LANES
    return [(k, pl.ds(k * size, size), range(k * size // LANES, (k + 1) * size // LANES)) for k in range(count // size)]


def first_departure(v_hbm, moves_hbm, cell_hbm, choice_hbm, shear_hbm, out_ref, v_ref, moves_ref, cell_ref, choice_ref, shear_ref, sems):
    parts = chunks(v_ref.shape[1])
    copies = [pltpu.make_async_copy(moves_hbm, moves_ref, sems.at[len(parts)])]
    copies += [pltpu.make_async_copy(v_hbm.at[:, span], v_ref.at[:, span], sems.at[k]) for k, span, _ in parts]
    pairs = ((cell_hbm, cell_ref), (choice_hbm, choice_ref), (shear_hbm, shear_ref))
    others = [pltpu.make_async_copy(x, y, sems.at[len(parts) + 1 + k]) for k, (x, y) in enumerate(pairs)]
    for copy in copies + others:
        copy.start()
    copies[0].wait()
    index = ordered_lists(moves_ref)[1]
    comps = v_ref.shape[0]
    index = jnp.broadcast_to(index, (comps, LANES))
    high, low = index >> 7, index & (LANES - 1)
    out = jnp.zeros((comps, LANES), jnp.float32)
    for copy, (_, _, rows) in zip(copies[1:], parts):
        copy.wait()
        for r in rows:
            out = jnp.where(high == r, take(v_ref[:, r * LANES : (r + 1) * LANES], low), out)
    out_ref[...] = out
    for copy in others:
        copy.wait()


def other_departures(v_ref, moves_ref, a_ref, s_ref):
    comps, count = v_ref.shape
    lists = ordered_lists(moves_ref)
    for k, out_ref, lane in ((0, a_ref, 0), (2, s_ref, 0), (3, s_ref, LANES)):
        index = jnp.broadcast_to(lists[k], (comps, LANES))
        high, low = index >> 7, index & (LANES - 1)
        out = jnp.zeros((comps, LANES), jnp.float32)
        for r in range(count // LANES):
            out = jnp.where(high == r, take(v_ref[:, r * LANES : (r + 1) * LANES], low), out)
        out_ref[:, lane : lane + LANES] = out


def prepare(v_ref, moves_ref, cell_ref, choice_ref, shear_ref, vd_ref, source_ref, celld_ref, base_ref, slotcell_ref, normal_ref, target_ref, keep_ref):
    comps, count = v_ref.shape
    rows = count // LANES
    cells = choice_ref.shape[1]
    blocks = cells // LANES
    lists = ordered_lists(moves_ref)
    target_ref[...] = jnp.concatenate([shear_ref[...], jnp.zeros((1, LANES - CY), jnp.float32)], 1)
    for r in range(rows):
        span = slice(r * LANES, (r + 1) * LANES)
        celld_ref[r : r + 1, :] = cell_ref[0:1, span]
        for c in range(comps):
            vd_ref[c, r : r + 1, :] = v_ref[c : c + 1, span]

    slots = jnp.concatenate(lists, 1)
    many = slots.shape[1]
    low = (iota((LANES, many), 0) == (slots & (LANES - 1))).astype(jnp.bfloat16)
    here = iota((rows, many), 0) == (slots >> 7)
    lane = iota((rows, many), 1)
    marks = jnp.concatenate(
        [
            jnp.where(here, (lane >> 7) + 1, 0).astype(jnp.float32),
            jnp.where(here, lane & (LANES - 1), 0).astype(jnp.float32),
        ]
    ).astype(jnp.bfloat16)
    found = lax.dot_general(marks, low, NT, preferred_element_type=jnp.float32).astype(jnp.int32)
    source = found[:rows] * LANES + found[rows:]
    source_ref[...] = source
    keep_ref[...] = jnp.where(source == 0, 1.0, 0.0)

    celld = celld_ref[...]
    four = jnp.concatenate(lists + lists, 0)
    slotcell_ref[...] = lookup([celld_ref[r : r + 1, :] for r in range(rows)], four)

    counter = (iota((1, LANES), 1) & (NAXES - 1)).astype(jnp.float32)
    height = 1.0 - (2.0 * counter + 1.0) / NAXES
    radius = jnp.sqrt(1.0 - height * height)
    table = (radius * jnp.cos(GOLDEN * counter), radius * jnp.sin(GOLDEN * counter), height)
    picks = [choice_ref[0:1, h * LANES : (h + 1) * LANES] for h in range(blocks)]
    for c in range(comps):
        entries = [take(table[c], pick) for pick in picks]
        normal_ref[c] = lookup(entries, celld)

    ones = (iota((SUBLANES - comps, LANES), 0) == 0).astype(jnp.float32)
    total = jnp.zeros((blocks * 3 * SUBLANES, LANES), jnp.float32)
    group = 4 if rows % 4 == 0 else 1
    for first in range(0, rows, group):
        left, right = [], []
        for r in range(first, first + group):
            cell = cell_ref[0:1, r * LANES : (r + 1) * LANES]
            tile = v_ref[:, r * LANES : (r + 1) * LANES] * keep_ref[r : r + 1, :]
            tile = jnp.concatenate([tile, ones], 0)
            parts = jnp.concatenate(split3(tile), 0)
            left.append(jnp.concatenate([jnp.where((cell >> 7) == h, parts, 0.0) for h in range(blocks)], 0))
            right.append((iota((LANES, LANES), 0) == (cell & (LANES - 1))).astype(jnp.bfloat16))
        left = jnp.concatenate(left, 1).astype(jnp.bfloat16)
        right = jnp.concatenate(right, 1)
        total += lax.dot_general(left, right, NT, preferred_element_type=jnp.float32)
    for h in range(blocks):
        part = total[h * 3 * SUBLANES : (h + 1) * 3 * SUBLANES]
        base_ref[h * SUBLANES : (h + 1) * SUBLANES] = part[:8] + part[8:16] + part[16:]


def relax(a_ref, b_ref, s_ref, vd_ref, source_ref, celld_ref, base_ref, slotcell_ref, normal_ref, send_ref, profile_ref, mean_ref, turned_ref):
    comps, rows, _ = vd_ref.shape
    blocks = base_ref.shape[0] // SUBLANES
    arrived = [a_ref[...], b_ref[...], s_ref[:, :LANES], s_ref[:, LANES:]]

    pad = jnp.zeros((SUBLANES - comps, LANES), jnp.float32)
    left, right = [], []
    for k, block in enumerate(arrived):
        cell = slotcell_ref[k : k + 1, :]
        parts = jnp.concatenate(split3(jnp.concatenate([block, pad], 0)), 0)
        left.append(jnp.concatenate([jnp.where((cell >> 7) == h, parts, 0.0) for h in range(blocks)], 0))
        right.append((iota((LANES, LANES), 0) == (cell & (LANES - 1))).astype(jnp.bfloat16))
    left = jnp.concatenate(left, 1).astype(jnp.bfloat16)
    right = jnp.concatenate(right, 1)
    fresh = lax.dot_general(left, right, NT, preferred_element_type=jnp.float32)
    sums, means = [], []
    for h in range(blocks):
        part = fresh[h * 3 * SUBLANES : (h + 1) * 3 * SUBLANES]
        total = base_ref[h * SUBLANES : (h + 1) * SUBLANES] + (part[:8] + part[8:16] + part[16:])
        sums.append(total)
        means.append(total / jnp.maximum(jnp.broadcast_to(total[comps : comps + 1], total.shape), 1.0))

    both = jnp.concatenate([s[0:1] for s in sums] + [s[comps : comps + 1] for s in sums], 0)
    width = CZ // 2
    while width:
        both = both + pltpu.roll(both, LANES - width, 1)
        width //= 2
    columns = iota((1, LANES), 1)
    start = columns * CZ
    flow = lookup([both[h : h + 1] for h in range(blocks)], start)
    number = lookup([both[blocks + h : blocks + h + 1] for h in range(blocks)], start)
    profile = flow / jnp.maximum(number, 1.0)
    profile_ref[...] = profile[:, :CY]

    source, celld = source_ref[...], celld_ref[...]
    relative, energy = [], jnp.zeros((rows, LANES), jnp.float32)
    for c in range(comps):
        old = vd_ref[c]
        speed = jnp.where(source == 0, old, lookup([x[c : c + 1] for x in arrived], source - LANES))
        mean = lookup([m[c : c + 1] for m in means], celld)
        mean_ref[c] = mean
        relative.append(speed - mean)
        energy += relative[c] * relative[c]
    energy = jnp.sum(energy, 0, keepdims=True)
    energy = energy + pltpu.roll(energy, CY, 1)
    message = jnp.where(columns < CY, profile, energy)
    send_ref[...] = jnp.broadcast_to(message[None], send_ref.shape)

    n = [normal_ref[c] for c in range(comps)]
    along = (n[0] * relative[0] + n[1] * relative[1] + n[2] * relative[2]) * (1.0 - ROT_COS)
    for c in range(comps):
        d, e = (c + 1) % comps, (c + 2) % comps
        cross = n[d] * relative[e] - n[e] * relative[d]
        turned_ref[c] = relative[c] * ROT_COS + cross * ROT_SIN + n[c] * along


def finish(got_ref, target_ref, profile_ref, mean_ref, turned_ref, celld_ref, out_hbm, profile_hbm, out_ref, sems, *, slabs, subs, particles):
    comps, _, _ = mean_ref.shape
    parts = chunks(out_ref.shape[1])
    copies = [pltpu.make_async_copy(profile_ref, profile_hbm, sems.at[len(parts)])]
    copies[0].start()
    got = got_ref[...].reshape(slabs * subs, LANES)
    mine = lax.rem(iota(got.shape, 0), subs) == lax.axis_index("sub")
    lane = iota(got.shape, 1)
    drift = jnp.sum(jnp.where(mine, got, 0.0), 0, keepdims=True) / (CX * slabs)
    work = jnp.sum(jnp.where(lane < CY, 0.0, got), 0, keepdims=True)
    work = jnp.sum(work, 1, keepdims=True)
    scale = lax.rsqrt(work / (3.0 * particles * RESERVOIR_HEAT) + 1e-06)
    extra = FEEDBACK * (target_ref[...] - drift)
    for k, span, own in parts:
        own = slice(own.start, own.stop)
        shape = (own.stop - own.start, LANES)
        line = (celld_ref[own, :] // CZ) & (CY - 1)
        shift = take(jnp.broadcast_to(extra, shape), line)
        for c in range(comps):
            base = mean_ref[c, own, :] + shift if c == 0 else mean_ref[c, own, :]
            out = base + scale * turned_ref[c, own, :]
            for r in range(shape[0]):
                lanes = slice((own.start + r) * LANES, (own.start + r + 1) * LANES)
                out_ref[c : c + 1, lanes] = out[r : r + 1, :]
        copies.append(pltpu.make_async_copy(out_ref.at[:, span], out_hbm.at[:, span], sems.at[k]))
        copies[-1].start()
    for copy in copies:
        copy.wait()


def swap(blocks, axis):
    size = lax.axis_size(axis)
    one, two = blocks
    if size % 2:
        forth = [(i, (i + 1) % size) for i in range(size)]
        back = [(i, (i - 1) % size) for i in range(size)]
        return [lax.ppermute(two, axis, back), lax.ppermute(one, axis, forth)]
    even = [(i, i ^ 1) for i in range(size)]
    odd = [(i, (i + 1 if i % 2 else i - 1) % size) for i in range(size)]
    second = lax.ppermute(two, axis, odd)
    first = lax.ppermute(one, axis, even)
    return [first, second]


def swap_joined(block, axis):
    size = lax.axis_size(axis)
    if size == 2:
        return lax.ppermute(block, axis, [(0, 1), (1, 0)])
    return jnp.concatenate(swap([block[:, :LANES], block[:, LANES:]], axis), 1)


def f32(*shape):
    return pltpu.VMEM(shape, jnp.float32)


def i32(*shape):
    return pltpu.VMEM(shape, jnp.int32)


def call(kernel, out_shape, inputs, scratch=(), flops=0, resident=True):
    size = sum(4 * math.prod(x.shape) for x in inputs)
    place = VMEM
    if resident:
        inputs = [pltpu.with_memory_space_constraint(x, pltpu.VMEM) for x in inputs]
    else:
        place = pl.BlockSpec(memory_space=pl.ANY)
    return pl.pallas_call(
        kernel,
        out_shape=out_shape,
        in_specs=[place] * len(inputs),
        out_specs=jax.tree.map(lambda x: VMEM if isinstance(x, pl.MemoryRef) else pl.BlockSpec(memory_space=pl.ANY), out_shape),
        scratch_shapes=list(scratch),
        cost_estimate=pl.CostEstimate(flops=flops, bytes_accessed=size, transcendentals=0),
    )(*inputs)


def step(speeds, cells, choices, moves, shear_target):
    slabs, subs = lax.axis_size("slab"), lax.axis_size("sub")
    comps, count = speeds.shape
    rows = count // LANES
    blocks = choices.shape[1] // LANES
    many = len(chunks(count)) + 1
    given = (speeds, moves, cells, choices, shear_target[None, :])
    b, speeds, moves, cells, choices, shear_target = call(
        first_departure,
        (f32(comps, LANES), *(pltpu.VMEM(x.shape, x.dtype) for x in given)),
        given,
        scratch=[pltpu.SemaphoreType.DMA((many + 3,))],
        resident=False,
    )
    a, s = call(
        other_departures,
        (f32(comps, LANES), f32(comps, 2 * LANES)),
        (speeds, moves),
    )
    a, b = swap([a, b], "slab")
    s = swap_joined(s, "sub")
    dense = f32(comps, rows, LANES)
    index = i32(rows, LANES)
    vd, source, celld, base, slotcell, normal, target = call(
        prepare,
        (dense, index, index, f32(blocks * SUBLANES, LANES), i32(SUBLANES, LANES), dense, f32(1, LANES)),
        (speeds, moves, cells, choices, shear_target),
        scratch=[pltpu.VMEM((rows, LANES), jnp.float32)],
        flops=2 * count * LANES * 96,
    )
    send, profile, mean, turned = call(
        relax,
        (f32(slabs * subs, 1, LANES), f32(1, CX * CY), dense, dense),
        (a, b, s, vd, source, celld, base, slotcell, normal),
    )
    got = lax.all_to_all(send, AXES, 0, 0, tiled=True)
    return call(
        functools.partial(finish, slabs=slabs, subs=subs, particles=count * slabs * subs),
        (jax.ShapeDtypeStruct((comps, count), jnp.float32), jax.ShapeDtypeStruct((1, CX * CY), jnp.float32)),
        (got, target, profile, mean, turned, celld),
        scratch=[pltpu.VMEM((comps, count), jnp.float32), pltpu.SemaphoreType.DMA((many,))],
    )


def body(velocities, cell_index, axis_choice, moves, shear_target):
    speeds, profile = velocities, None
    for t in range(moves.shape[0]):
        speeds, profile = step(speeds, cell_index[t : t + 1], axis_choice[t : t + 1], moves[t], shear_target)
    return speeds, profile


def solution(mesh):
    in_specs = (
        P(None, ("slab", "sub")),
        P(None, ("slab", "sub")),
        P(None, ("slab", "sub")),
        P(None, None, ("slab", "sub")),
        P("sub"),
    )
    out_specs = (P(None, ("slab", "sub")), P("slab", "sub"))
    return jax.shard_map(body, mesh=mesh, in_specs=in_specs, out_specs=out_specs, check_vma=False)
```

```python
import functools
import math

import jax
import jax.numpy as jnp
from jax import lax
from jax.experimental import pallas as pl
from jax.experimental.pallas import tpu as pltpu
from jax.sharding import PartitionSpec as P


CX = 1
CY = 64
CZ = 8
NAXES = 64

ROT_COS = -0.6427876096865393
ROT_SIN = 0.766044443118978
RESERVOIR_HEAT = 0.9
FEEDBACK = 1.0
GOLDEN = 2.399963229728653

LANES = 128
SUBLANES = 8
AXES = ("slab", "sub")
VMEM = pl.BlockSpec(memory_space=pltpu.VMEM)
NT = (((1,), (1,)), ((), ()))
TAKE = lax.GatherDimensionNumbers(
    offset_dims=(),
    collapsed_slice_dims=(1,),
    start_index_map=(1,),
    operand_batching_dims=(0,),
    start_indices_batching_dims=(0,),
)


def take(rows, lanes):
    return lax.gather(
        rows,
        lanes[:, :, None],
        dimension_numbers=TAKE,
        slice_sizes=(1, 1),
        mode=lax.GatherScatterMode.PROMISE_IN_BOUNDS,
    )


def lookup(rows, index, shift=7):
    high, low = index >> shift, index & (LANES - 1)
    out = jnp.zeros(index.shape, rows[0].dtype)
    for h, row in enumerate(rows):
        out = jnp.where(high == h, take(jnp.broadcast_to(row, index.shape), low), out)
    return out


def iota(shape, axis):
    return lax.broadcasted_iota(jnp.int32, shape, axis)


def split3(x):
    a = x.astype(jnp.bfloat16).astype(jnp.float32)
    rest = x - a
    b = rest.astype(jnp.bfloat16).astype(jnp.float32)
    return a, b, rest - b


def parity(axis):
    if lax.axis_size(axis) % 2:
        return 0
    return lax.rem(lax.axis_index(axis), 2)


def ordered_lists(moves_ref):
    lists = []
    for base, axis in ((0, "slab"), (2, "sub")):
        odd = parity(axis)
        one, two = moves_ref[base : base + 1], moves_ref[base + 1 : base + 2]
        lists += [jnp.where(odd == 0, one, two), jnp.where(odd == 0, two, one)]
    return lists


def chunks(count, pieces):
    rows = count // LANES
    pieces = math.gcd(pieces, rows)
    size = rows // pieces
    return [(k, pl.ds(k * size * LANES, size * LANES), range(k * size, (k + 1) * size)) for k in range(pieces)]


def first_departure(v_hbm, moves_hbm, out_ref, v_ref, moves_ref, sems):
    parts = chunks(v_ref.shape[1], 2)
    copies = [pltpu.make_async_copy(moves_hbm, moves_ref, sems.at[len(parts)])]
    copies += [pltpu.make_async_copy(v_hbm.at[:, span], v_ref.at[:, span], sems.at[k]) for k, span, _ in parts]
    for copy in copies:
        copy.start()
    copies[0].wait()
    index = ordered_lists(moves_ref)[1]
    comps = v_ref.shape[0]
    index = jnp.broadcast_to(index, (comps, LANES))
    high, low = index >> 7, index & (LANES - 1)
    out = jnp.zeros((comps, LANES), jnp.float32)
    for copy, (_, _, rows) in zip(copies[1:], parts):
        copy.wait()
        for r in rows:
            out = jnp.where(high == r, take(v_ref[:, r * LANES : (r + 1) * LANES], low), out)
    out_ref[...] = out


def other_departures(v_ref, moves_ref, a_ref, s_ref):
    comps, count = v_ref.shape
    lists = ordered_lists(moves_ref)
    for k, out_ref, lane in ((0, a_ref, 0), (2, s_ref, 0), (3, s_ref, LANES)):
        index = jnp.broadcast_to(lists[k], (comps, LANES))
        high, low = index >> 7, index & (LANES - 1)
        out = jnp.zeros((comps, LANES), jnp.float32)
        for r in range(count // LANES):
            out = jnp.where(high == r, take(v_ref[:, r * LANES : (r + 1) * LANES], low), out)
        out_ref[:, lane : lane + LANES] = out


def prepare(v_ref, moves_ref, cell_ref, choice_ref, shear_ref, vd_ref, source_ref, celld_ref, base_ref, slotcell_ref, normal_ref, target_ref, keep_ref):
    comps, count = v_ref.shape
    rows = count // LANES
    cells = choice_ref.shape[1]
    blocks = cells // LANES
    lists = ordered_lists(moves_ref)
    target_ref[...] = jnp.concatenate([shear_ref[...], jnp.zeros((1, LANES - CY), jnp.float32)], 1)
    for r in range(rows):
        span = slice(r * LANES, (r + 1) * LANES)
        celld_ref[r : r + 1, :] = cell_ref[0:1, span]
        for c in range(comps):
            vd_ref[c, r : r + 1, :] = v_ref[c : c + 1, span]

    slots = jnp.concatenate(lists, 1)
    many = slots.shape[1]
    low = (iota((LANES, many), 0) == (slots & (LANES - 1))).astype(jnp.bfloat16)
    here = iota((rows, many), 0) == (slots >> 7)
    lane = iota((rows, many), 1)
    marks = jnp.concatenate(
        [
            jnp.where(here, (lane >> 7) + 1, 0).astype(jnp.float32),
            jnp.where(here, lane & (LANES - 1), 0).astype(jnp.float32),
        ]
    ).astype(jnp.bfloat16)
    found = lax.dot_general(marks, low, NT, preferred_element_type=jnp.float32).astype(jnp.int32)
    source = found[:rows] * LANES + found[rows:]
    source_ref[...] = source
    keep_ref[...] = jnp.where(source == 0, 1.0, 0.0)

    celld = celld_ref[...]
    four = jnp.concatenate(lists + lists, 0)
    slotcell_ref[...] = lookup([celld_ref[r : r + 1, :] for r in range(rows)], four)

    counter = (iota((1, LANES), 1) & (NAXES - 1)).astype(jnp.float32)
    height = 1.0 - (2.0 * counter + 1.0) / NAXES
    radius = jnp.sqrt(1.0 - height * height)
    table = (radius * jnp.cos(GOLDEN * counter), radius * jnp.sin(GOLDEN * counter), height)
    picks = [choice_ref[0:1, h * LANES : (h + 1) * LANES] for h in range(blocks)]
    for c in range(comps):
        entries = [take(table[c], pick) for pick in picks]
        normal_ref[c] = lookup(entries, celld)

    ones = (iota((SUBLANES - comps, LANES), 0) == 0).astype(jnp.float32)
    total = jnp.zeros((blocks * 3 * SUBLANES, LANES), jnp.float32)
    group = 4 if rows % 4 == 0 else 1
    for first in range(0, rows, group):
        left, right = [], []
        for r in range(first, first + group):
            cell = cell_ref[0:1, r * LANES : (r + 1) * LANES]
            tile = v_ref[:, r * LANES : (r + 1) * LANES] * keep_ref[r : r + 1, :]
            tile = jnp.concatenate([tile, ones], 0)
            parts = jnp.concatenate(split3(tile), 0)
            left.append(jnp.concatenate([jnp.where((cell >> 7) == h, parts, 0.0) for h in range(blocks)], 0))
            right.append((iota((LANES, LANES), 0) == (cell & (LANES - 1))).astype(jnp.bfloat16))
        left = jnp.concatenate(left, 1).astype(jnp.bfloat16)
        right = jnp.concatenate(right, 1)
        total += lax.dot_general(left, right, NT, preferred_element_type=jnp.float32)
    for h in range(blocks):
        part = total[h * 3 * SUBLANES : (h + 1) * 3 * SUBLANES]
        base_ref[h * SUBLANES : (h + 1) * SUBLANES] = part[:8] + part[8:16] + part[16:]


def relax(a_ref, b_ref, s_ref, vd_ref, source_ref, celld_ref, base_ref, slotcell_ref, normal_ref, send_ref, profile_ref, mean_ref, turned_ref):
    comps, rows, _ = vd_ref.shape
    blocks = base_ref.shape[0] // SUBLANES
    arrived = [a_ref[...], b_ref[...], s_ref[:, :LANES], s_ref[:, LANES:]]

    pad = jnp.zeros((SUBLANES - comps, LANES), jnp.float32)
    left, right = [], []
    for k, block in enumerate(arrived):
        cell = slotcell_ref[k : k + 1, :]
        parts = jnp.concatenate(split3(jnp.concatenate([block, pad], 0)), 0)
        left.append(jnp.concatenate([jnp.where((cell >> 7) == h, parts, 0.0) for h in range(blocks)], 0))
        right.append((iota((LANES, LANES), 0) == (cell & (LANES - 1))).astype(jnp.bfloat16))
    left = jnp.concatenate(left, 1).astype(jnp.bfloat16)
    right = jnp.concatenate(right, 1)
    fresh = lax.dot_general(left, right, NT, preferred_element_type=jnp.float32)
    sums, means = [], []
    for h in range(blocks):
        part = fresh[h * 3 * SUBLANES : (h + 1) * 3 * SUBLANES]
        total = base_ref[h * SUBLANES : (h + 1) * SUBLANES] + (part[:8] + part[8:16] + part[16:])
        sums.append(total)
        means.append(total / jnp.maximum(jnp.broadcast_to(total[comps : comps + 1], total.shape), 1.0))

    both = jnp.concatenate([s[0:1] for s in sums] + [s[comps : comps + 1] for s in sums], 0)
    width = CZ // 2
    while width:
        both = both + pltpu.roll(both, LANES - width, 1)
        width //= 2
    columns = iota((1, LANES), 1)
    start = columns * CZ
    flow = lookup([both[h : h + 1] for h in range(blocks)], start)
    number = lookup([both[blocks + h : blocks + h + 1] for h in range(blocks)], start)
    profile = flow / jnp.maximum(number, 1.0)
    profile_ref[...] = profile[:, :CY]

    source, celld = source_ref[...], celld_ref[...]
    relative, energy = [], jnp.zeros((rows, LANES), jnp.float32)
    for c in range(comps):
        old = vd_ref[c]
        speed = jnp.where(source == 0, old, lookup([x[c : c + 1] for x in arrived], source - LANES))
        mean = lookup([m[c : c + 1] for m in means], celld)
        mean_ref[c] = mean
        relative.append(speed - mean)
        energy += relative[c] * relative[c]
    energy = jnp.sum(energy, 0, keepdims=True)
    energy = energy + pltpu.roll(energy, CY, 1)
    message = jnp.where(columns < CY, profile, energy)
    send_ref[...] = jnp.broadcast_to(message[None], send_ref.shape)

    n = [normal_ref[c] for c in range(comps)]
    along = (n[0] * relative[0] + n[1] * relative[1] + n[2] * relative[2]) * (1.0 - ROT_COS)
    for c in range(comps):
        d, e = (c + 1) % comps, (c + 2) % comps
        cross = n[d] * relative[e] - n[e] * relative[d]
        turned_ref[c] = relative[c] * ROT_COS + cross * ROT_SIN + n[c] * along


def finish(got_ref, target_ref, profile_ref, mean_ref, turned_ref, celld_ref, out_hbm, profile_hbm, out_ref, sems, *, slabs, subs, particles):
    comps, _, _ = mean_ref.shape
    parts = chunks(out_ref.shape[1], 1)
    copies = [pltpu.make_async_copy(profile_ref, profile_hbm, sems.at[len(parts)])]
    copies[0].start()
    got = got_ref[...].reshape(slabs * subs, LANES)
    mine = lax.rem(iota(got.shape, 0), subs) == lax.axis_index("sub")
    lane = iota(got.shape, 1)
    drift = jnp.sum(jnp.where(mine, got, 0.0), 0, keepdims=True) / (CX * slabs)
    work = jnp.sum(jnp.where(lane < CY, 0.0, got), 0, keepdims=True)
    work = jnp.sum(work, 1, keepdims=True)
    scale = lax.rsqrt(work / (3.0 * particles * RESERVOIR_HEAT) + 1e-06)
    extra = FEEDBACK * (target_ref[...] - drift)
    for k, span, own in parts:
        own = slice(own.start, own.stop)
        shape = (own.stop - own.start, LANES)
        line = (celld_ref[own, :] // CZ) & (CY - 1)
        shift = take(jnp.broadcast_to(extra, shape), line)
        for c in range(comps):
            base = mean_ref[c, own, :] + shift if c == 0 else mean_ref[c, own, :]
            out = base + scale * turned_ref[c, own, :]
            for r in range(shape[0]):
                lanes = slice((own.start + r) * LANES, (own.start + r + 1) * LANES)
                out_ref[c : c + 1, lanes] = out[r : r + 1, :]
        copies.append(pltpu.make_async_copy(out_ref.at[:, span], out_hbm.at[:, span], sems.at[k]))
        copies[-1].start()
    for copy in copies:
        copy.wait()


def swap(blocks, axis):
    size = lax.axis_size(axis)
    one, two = blocks
    if size % 2:
        forth = [(i, (i + 1) % size) for i in range(size)]
        back = [(i, (i - 1) % size) for i in range(size)]
        return [lax.ppermute(two, axis, back), lax.ppermute(one, axis, forth)]
    even = [(i, i ^ 1) for i in range(size)]
    odd = [(i, (i + 1 if i % 2 else i - 1) % size) for i in range(size)]
    second = lax.ppermute(two, axis, odd)
    first = lax.ppermute(one, axis, even)
    return [first, second]


def swap_joined(block, axis):
    size = lax.axis_size(axis)
    if size == 2:
        return lax.ppermute(block, axis, [(0, 1), (1, 0)])
    return jnp.concatenate(swap([block[:, :LANES], block[:, LANES:]], axis), 1)


def f32(*shape):
    return pltpu.VMEM(shape, jnp.float32)


def i32(*shape):
    return pltpu.VMEM(shape, jnp.int32)


def call(kernel, out_shape, inputs, scratch=(), flops=0, resident=True):
    size = sum(4 * math.prod(x.shape) for x in inputs)
    place = VMEM
    if resident:
        inputs = [pltpu.with_memory_space_constraint(x, pltpu.VMEM) for x in inputs]
    else:
        place = pl.BlockSpec(memory_space=pl.ANY)
    return pl.pallas_call(
        kernel,
        out_shape=out_shape,
        in_specs=[place] * len(inputs),
        out_specs=jax.tree.map(lambda x: VMEM if isinstance(x, pl.MemoryRef) else pl.BlockSpec(memory_space=pl.ANY), out_shape),
        scratch_shapes=list(scratch),
        cost_estimate=pl.CostEstimate(flops=flops, bytes_accessed=size, transcendentals=0),
    )(*inputs)


def step(speeds, cells, choices, moves, shear_target):
    slabs, subs = lax.axis_size("slab"), lax.axis_size("sub")
    comps, count = speeds.shape
    rows = count // LANES
    blocks = choices.shape[1] // LANES
    b, speeds, moves = call(
        first_departure,
        (f32(comps, LANES), f32(*speeds.shape), i32(*moves.shape)),
        (speeds, moves),
        scratch=[pltpu.SemaphoreType.DMA((len(chunks(count, 2)) + 1,))],
        resident=False,
    )
    a, s = call(
        other_departures,
        (f32(comps, LANES), f32(comps, 2 * LANES)),
        (speeds, moves),
    )
    a, b = swap([a, b], "slab")
    s = swap_joined(s, "sub")
    dense = f32(comps, rows, LANES)
    index = i32(rows, LANES)
    vd, source, celld, base, slotcell, normal, target = call(
        prepare,
        (dense, index, index, f32(blocks * SUBLANES, LANES), i32(SUBLANES, LANES), dense, f32(1, LANES)),
        (speeds, moves, cells, choices, shear_target[None, :]),
        scratch=[pltpu.VMEM((rows, LANES), jnp.float32)],
        flops=2 * count * LANES * 96,
    )
    send, profile, mean, turned = call(
        relax,
        (f32(slabs * subs, 1, LANES), f32(1, CX * CY), dense, dense),
        (a, b, s, vd, source, celld, base, slotcell, normal),
    )
    got = lax.all_to_all(send, AXES, 0, 0, tiled=True)
    return call(
        functools.partial(finish, slabs=slabs, subs=subs, particles=count * slabs * subs),
        (jax.ShapeDtypeStruct((comps, count), jnp.float32), jax.ShapeDtypeStruct((1, CX * CY), jnp.float32)),
        (got, target, profile, mean, turned, celld),
        scratch=[pltpu.VMEM((comps, count), jnp.float32), pltpu.SemaphoreType.DMA((2,))],
    )


def body(velocities, cell_index, axis_choice, moves, shear_target):
    speeds, profile = velocities, None
    for t in range(moves.shape[0]):
        speeds, profile = step(speeds, cell_index[t : t + 1], axis_choice[t : t + 1], moves[t], shear_target)
    return speeds, profile


def solution(mesh):
    in_specs = (
        P(None, ("slab", "sub")),
        P(None, ("slab", "sub")),
        P(None, ("slab", "sub")),
        P(None, None, ("slab", "sub")),
        P("sub"),
    )
    out_specs = (P(None, ("slab", "sub")), P("slab", "sub"))
    return jax.shard_map(body, mesh=mesh, in_specs=in_specs, out_specs=out_specs, check_vma=False)
```

```python
import functools
import math

import jax
import jax.numpy as jnp
from jax import lax
from jax.experimental import pallas as pl
from jax.experimental.pallas import tpu as pltpu
from jax.sharding import PartitionSpec as P


CX = 1
CY = 64
CZ = 8
NAXES = 64

ROT_COS = -0.6427876096865393
ROT_SIN = 0.766044443118978
RESERVOIR_HEAT = 0.9
FEEDBACK = 1.0
GOLDEN = 2.399963229728653

LANES = 128
SUBLANES = 8
AXES = ("slab", "sub")
VMEM = pl.BlockSpec(memory_space=pltpu.VMEM)
NT = (((1,), (1,)), ((), ()))
TAKE = lax.GatherDimensionNumbers(
    offset_dims=(),
    collapsed_slice_dims=(1,),
    start_index_map=(1,),
    operand_batching_dims=(0,),
    start_indices_batching_dims=(0,),
)


def take(rows, lanes):
    return lax.gather(
        rows,
        lanes[:, :, None],
        dimension_numbers=TAKE,
        slice_sizes=(1, 1),
        mode=lax.GatherScatterMode.PROMISE_IN_BOUNDS,
    )


def lookup(rows, index, shift=7):
    high, low = index >> shift, index & (LANES - 1)
    out = jnp.zeros(index.shape, rows[0].dtype)
    for h, row in enumerate(rows):
        out = jnp.where(high == h, take(jnp.broadcast_to(row, index.shape), low), out)
    return out


def iota(shape, axis):
    return lax.broadcasted_iota(jnp.int32, shape, axis)


def split3(x):
    a = x.astype(jnp.bfloat16).astype(jnp.float32)
    rest = x - a
    b = rest.astype(jnp.bfloat16).astype(jnp.float32)
    return a, b, rest - b


def parity(axis):
    if lax.axis_size(axis) % 2:
        return 0
    return lax.rem(lax.axis_index(axis), 2)


def ordered_lists(moves_ref):
    lists = []
    for base, axis in ((0, "slab"), (2, "sub")):
        odd = parity(axis)
        one, two = moves_ref[base : base + 1], moves_ref[base + 1 : base + 2]
        lists += [jnp.where(odd == 0, one, two), jnp.where(odd == 0, two, one)]
    return lists


def chunks(count, pieces):
    rows = count // LANES
    pieces = math.gcd(pieces, rows)
    size = rows // pieces
    return [(k, pl.ds(k * size * LANES, size * LANES), range(k * size, (k + 1) * size)) for k in range(pieces)]


def first_departure(v_hbm, moves_hbm, out_ref, v_ref, moves_ref, sems):
    parts = chunks(v_ref.shape[1], 2)
    copies = [pltpu.make_async_copy(moves_hbm, moves_ref, sems.at[len(parts)])]
    copies += [pltpu.make_async_copy(v_hbm.at[:, span], v_ref.at[:, span], sems.at[k]) for k, span, _ in parts]
    for copy in copies:
        copy.start()
    copies[0].wait()
    index = ordered_lists(moves_ref)[1]
    comps = v_ref.shape[0]
    index = jnp.broadcast_to(index, (comps, LANES))
    high, low = index >> 7, index & (LANES - 1)
    out = jnp.zeros((comps, LANES), jnp.float32)
    for copy, (_, _, rows) in zip(copies[1:], parts):
        copy.wait()
        for r in rows:
            out = jnp.where(high == r, take(v_ref[:, r * LANES : (r + 1) * LANES], low), out)
    out_ref[...] = out


def other_departures(v_ref, moves_ref, a_ref, s_ref):
    comps, count = v_ref.shape
    lists = ordered_lists(moves_ref)
    for k, out_ref, lane in ((0, a_ref, 0), (2, s_ref, 0), (3, s_ref, LANES)):
        index = jnp.broadcast_to(lists[k], (comps, LANES))
        high, low = index >> 7, index & (LANES - 1)
        out = jnp.zeros((comps, LANES), jnp.float32)
        for r in range(count // LANES):
            out = jnp.where(high == r, take(v_ref[:, r * LANES : (r + 1) * LANES], low), out)
        out_ref[:, lane : lane + LANES] = out


def bins(block, cell, blocks):
    parts = jnp.concatenate(split3(block), 0)
    left = jnp.concatenate([jnp.where((cell >> 7) == h, parts, 0.0) for h in range(blocks)], 0)
    right = (iota((LANES, LANES), 0) == (cell & (LANES - 1))).astype(jnp.bfloat16)
    return left, right


def join(parts):
    return parts[:SUBLANES] + parts[SUBLANES : 2 * SUBLANES] + parts[2 * SUBLANES :]


def columns_of(cells):
    return cells // CZ


def prepare(v_ref, moves_ref, cell_ref, choice_ref, shear_ref, a_ref, s_ref, vd_ref, source_ref, celld_ref, base_ref, count_ref, column_ref, spread_ref, normal_ref, target_ref, keep_ref):
    comps, count = v_ref.shape
    rows = count // LANES
    cells = choice_ref.shape[1]
    blocks = cells // LANES
    lists = ordered_lists(moves_ref)
    target_ref[...] = jnp.concatenate([shear_ref[...], jnp.zeros((1, LANES - CY), jnp.float32)], 1)
    for r in range(rows):
        span = slice(r * LANES, (r + 1) * LANES)
        celld_ref[r : r + 1, :] = cell_ref[0:1, span]
        for c in range(comps):
            vd_ref[c, r : r + 1, :] = v_ref[c : c + 1, span]

    order = (1, 0, 2, 3)
    slots = jnp.concatenate([lists[k] for k in order], 1)
    many = slots.shape[1]
    low = (iota((LANES, many), 0) == (slots & (LANES - 1))).astype(jnp.bfloat16)
    here = iota((rows, many), 0) == (slots >> 7)
    lane = iota((rows, many), 1)
    marks = jnp.concatenate(
        [
            jnp.where(here, (lane >> 7) + 1, 0).astype(jnp.float32),
            jnp.where(here, lane & (LANES - 1), 0).astype(jnp.float32),
        ]
    ).astype(jnp.bfloat16)
    found = lax.dot_general(marks, low, NT, preferred_element_type=jnp.float32).astype(jnp.int32)
    source = found[:rows] * LANES + found[rows:]
    keep_ref[...] = jnp.where(source == 0, 1.0, 0.0)
    late = (source >= LANES) & (source < 2 * LANES)
    source_ref[...] = jnp.where(late, source - LANES, -1)

    celld = celld_ref[...]
    four = jnp.concatenate([lists[k] for k in order + order], 0)
    slotcell = lookup([celld_ref[r : r + 1, :] for r in range(rows)], four)

    counter = (iota((1, LANES), 1) & (NAXES - 1)).astype(jnp.float32)
    height = 1.0 - (2.0 * counter + 1.0) / NAXES
    radius = jnp.sqrt(1.0 - height * height)
    table = (radius * jnp.cos(GOLDEN * counter), radius * jnp.sin(GOLDEN * counter), height)
    picks = [choice_ref[0:1, h * LANES : (h + 1) * LANES] for h in range(blocks)]
    for c in range(comps):
        entries = [take(table[c], pick) for pick in picks]
        normal_ref[c] = lookup(entries, celld)

    arrived = [a_ref[...], s_ref[:, :LANES], s_ref[:, LANES:]]
    for c in range(comps):
        old = vd_ref[c]
        vd_ref[c] = jnp.where(source < 2 * LANES, old, lookup([x[c : c + 1] for x in arrived], source - 2 * LANES))

    ones = (iota((SUBLANES - comps, LANES), 0) == 0).astype(jnp.float32)
    total = jnp.zeros((blocks * 3 * SUBLANES, LANES), jnp.float32)
    group = math.gcd(4, rows)
    for first in range(0, rows, group):
        left, right = [], []
        for r in range(first, first + group):
            span = slice(r * LANES, (r + 1) * LANES)
            tile = v_ref[:, span] * keep_ref[r : r + 1, :]
            one, two = bins(jnp.concatenate([tile, ones], 0), cell_ref[0:1, span], blocks)
            left.append(one)
            right.append(two)
        left = jnp.concatenate(left, 1).astype(jnp.bfloat16)
        total += lax.dot_general(left, jnp.concatenate(right, 1), NT, preferred_element_type=jnp.float32)
    left, right = [], []
    for k, block in enumerate(arrived):
        one, two = bins(jnp.concatenate([block, jnp.zeros_like(ones)], 0), slotcell[k + 1 : k + 2], blocks)
        left.append(one)
        right.append(two)
    left = jnp.concatenate(left, 1).astype(jnp.bfloat16)
    total += lax.dot_general(left, jnp.concatenate(right, 1), NT, preferred_element_type=jnp.float32)
    sums = [join(total[h * 3 * SUBLANES : (h + 1) * 3 * SUBLANES]) for h in range(blocks)]

    both = jnp.concatenate([x[0:1] for x in sums] + [x[comps : comps + 1] for x in sums], 0)
    width = CZ // 2
    while width:
        both = both + pltpu.roll(both, LANES - width, 1)
        width //= 2
    start = iota((1, LANES), 1) * CZ
    flow = lookup([both[h : h + 1] for h in range(blocks)], start)
    number = lookup([both[blocks + h : blocks + h + 1] for h in range(blocks)], start)
    column_ref[...] = jnp.concatenate([flow, 1.0 / jnp.maximum(number, 1.0)], 0)

    late_cell = jnp.transpose(jnp.broadcast_to(slotcell[0:1].astype(jnp.float32), (LANES, LANES))).astype(jnp.int32)
    for h in range(blocks):
        span = slice(h * LANES, (h + 1) * LANES)
        base_ref[:, span] = sums[h]
        count_ref[:, span] = 1.0 / jnp.maximum(sums[h][comps : comps + 1], 1.0)
        spread_ref[:, span] = (late_cell == iota((LANES, LANES), 1) + h * LANES).astype(jnp.bfloat16)
    spread_ref[:, cells:] = (columns_of(late_cell) == iota((LANES, LANES), 1)).astype(jnp.bfloat16)


def relax(b_ref, vd_ref, source_ref, celld_ref, base_ref, count_ref, column_ref, spread_ref, normal_ref, send_ref, profile_ref, mean_ref, turned_ref):
    comps, rows, _ = vd_ref.shape
    cells = base_ref.shape[1]
    late = b_ref[...]
    block = jnp.concatenate([late, jnp.zeros((SUBLANES - comps, LANES), jnp.float32)], 0)
    left = jnp.concatenate(split3(block), 0).astype(jnp.bfloat16)
    fresh = join(jnp.dot(left, spread_ref[...], preferred_element_type=jnp.float32))
    means = (base_ref[...] + fresh[:, :cells]) * count_ref[...]
    profile = (column_ref[0:1] + fresh[0:1, cells:]) * column_ref[1:2]
    profile_ref[...] = profile[:, :CY]

    source, celld = source_ref[...], celld_ref[...]
    relative, energy = [], jnp.zeros((rows, LANES), jnp.float32)
    for c in range(comps):
        fill = take(jnp.broadcast_to(late[c : c + 1], source.shape), source & (LANES - 1))
        speed = jnp.where(source < 0, vd_ref[c], fill)
        mean = lookup([means[c : c + 1, h : h + LANES] for h in range(0, cells, LANES)], celld)
        mean_ref[c] = mean
        relative.append(speed - mean)
        energy += relative[c] * relative[c]
    energy = jnp.sum(energy, 0, keepdims=True)
    energy = energy + pltpu.roll(energy, CY, 1)
    message = jnp.where(iota((1, LANES), 1) < CY, profile, energy)
    send_ref[...] = jnp.broadcast_to(message[None], send_ref.shape)

    n = [normal_ref[c] for c in range(comps)]
    along = (n[0] * relative[0] + n[1] * relative[1] + n[2] * relative[2]) * (1.0 - ROT_COS)
    for c in range(comps):
        d, e = (c + 1) % comps, (c + 2) % comps
        cross = n[d] * relative[e] - n[e] * relative[d]
        turned_ref[c] = relative[c] * ROT_COS + cross * ROT_SIN + n[c] * along


def finish(got_ref, target_ref, profile_ref, mean_ref, turned_ref, celld_ref, out_hbm, profile_hbm, out_ref, sems, *, slabs, subs, particles):
    comps, _, _ = mean_ref.shape
    parts = chunks(out_ref.shape[1], 1)
    copies = [pltpu.make_async_copy(profile_ref, profile_hbm, sems.at[len(parts)])]
    copies[0].start()
    got = got_ref[...].reshape(slabs * subs, LANES)
    mine = lax.rem(iota(got.shape, 0), subs) == lax.axis_index("sub")
    lane = iota(got.shape, 1)
    drift = jnp.sum(jnp.where(mine, got, 0.0), 0, keepdims=True) / (CX * slabs)
    work = jnp.sum(jnp.where(lane < CY, 0.0, got), 0, keepdims=True)
    work = jnp.sum(work, 1, keepdims=True)
    scale = lax.rsqrt(work / (3.0 * particles * RESERVOIR_HEAT) + 1e-06)
    extra = FEEDBACK * (target_ref[...] - drift)
    for k, span, own in parts:
        own = slice(own.start, own.stop)
        shape = (own.stop - own.start, LANES)
        line = columns_of(celld_ref[own, :]) & (CY - 1)
        shift = take(jnp.broadcast_to(extra, shape), line)
        for c in range(comps):
            base = mean_ref[c, own, :] + shift if c == 0 else mean_ref[c, own, :]
            out = base + scale * turned_ref[c, own, :]
            for r in range(shape[0]):
                lanes = slice((own.start + r) * LANES, (own.start + r + 1) * LANES)
                out_ref[c : c + 1, lanes] = out[r : r + 1, :]
        copies.append(pltpu.make_async_copy(out_ref.at[:, span], out_hbm.at[:, span], sems.at[k]))
        copies[-1].start()
    for copy in copies:
        copy.wait()


def swap(blocks, axis):
    size = lax.axis_size(axis)
    one, two = blocks
    if size % 2:
        forth = [(i, (i + 1) % size) for i in range(size)]
        back = [(i, (i - 1) % size) for i in range(size)]
        return [lax.ppermute(two, axis, back), lax.ppermute(one, axis, forth)]
    even = [(i, i ^ 1) for i in range(size)]
    odd = [(i, (i + 1 if i % 2 else i - 1) % size) for i in range(size)]
    second = lax.ppermute(two, axis, odd)
    first = lax.ppermute(one, axis, even)
    return [first, second]


def swap_joined(block, axis):
    size = lax.axis_size(axis)
    if size == 2:
        return lax.ppermute(block, axis, [(0, 1), (1, 0)])
    return jnp.concatenate(swap([block[:, :LANES], block[:, LANES:]], axis), 1)


def f32(*shape):
    return pltpu.VMEM(shape, jnp.float32)


def i32(*shape):
    return pltpu.VMEM(shape, jnp.int32)


def call(kernel, out_shape, inputs, scratch=(), flops=0, resident=True):
    size = sum(4 * math.prod(x.shape) for x in inputs)
    place = VMEM
    if resident:
        inputs = [pltpu.with_memory_space_constraint(x, pltpu.VMEM) for x in inputs]
    else:
        place = pl.BlockSpec(memory_space=pl.ANY)
    return pl.pallas_call(
        kernel,
        out_shape=out_shape,
        in_specs=[place] * len(inputs),
        out_specs=jax.tree.map(lambda x: VMEM if isinstance(x, pl.MemoryRef) else pl.BlockSpec(memory_space=pl.ANY), out_shape),
        scratch_shapes=list(scratch),
        cost_estimate=pl.CostEstimate(flops=flops, bytes_accessed=size, transcendentals=0),
    )(*inputs)


def step(speeds, cells, choices, moves, shear_target):
    slabs, subs = lax.axis_size("slab"), lax.axis_size("sub")
    comps, count = speeds.shape
    rows = count // LANES
    b, speeds, moves = call(
        first_departure,
        (f32(comps, LANES), f32(*speeds.shape), i32(*moves.shape)),
        (speeds, moves),
        scratch=[pltpu.SemaphoreType.DMA((len(chunks(count, 2)) + 1,))],
        resident=False,
    )
    a, s = call(
        other_departures,
        (f32(comps, LANES), f32(comps, 2 * LANES)),
        (speeds, moves),
    )
    a, b = swap([a, b], "slab")
    s = swap_joined(s, "sub")
    dense = f32(comps, rows, LANES)
    index = i32(rows, LANES)
    cell_count = choices.shape[1]
    sums = f32(SUBLANES, cell_count)
    vd, source, celld, base, number, column, spread, normal, target = call(
        prepare,
        (dense, index, index, sums, f32(1, cell_count), f32(2, LANES), pltpu.VMEM((LANES, cell_count + LANES), jnp.bfloat16), dense, f32(1, LANES)),
        (speeds, moves, cells, choices, shear_target[None, :], a, s),
        scratch=[pltpu.VMEM((rows, LANES), jnp.float32)],
        flops=2 * count * LANES * 96,
    )
    send, profile, mean, turned = call(
        relax,
        (f32(slabs * subs, 1, LANES), f32(1, CX * CY), dense, dense),
        (b, vd, source, celld, base, number, column, spread, normal),
    )
    got = lax.all_to_all(send, AXES, 0, 0, tiled=True)
    return call(
        functools.partial(finish, slabs=slabs, subs=subs, particles=count * slabs * subs),
        (jax.ShapeDtypeStruct((comps, count), jnp.float32), jax.ShapeDtypeStruct((1, CX * CY), jnp.float32)),
        (got, target, profile, mean, turned, celld),
        scratch=[pltpu.VMEM((comps, count), jnp.float32), pltpu.SemaphoreType.DMA((2,))],
    )


def body(velocities, cell_index, axis_choice, moves, shear_target):
    speeds, profile = velocities, None
    for t in range(moves.shape[0]):
        speeds, profile = step(speeds, cell_index[t : t + 1], axis_choice[t : t + 1], moves[t], shear_target)
    return speeds, profile


def solution(mesh):
    in_specs = (
        P(None, ("slab", "sub")),
        P(None, ("slab", "sub")),
        P(None, ("slab", "sub")),
        P(None, None, ("slab", "sub")),
        P("sub"),
    )
    out_specs = (P(None, ("slab", "sub")), P("slab", "sub"))
    return jax.shard_map(body, mesh=mesh, in_specs=in_specs, out_specs=out_specs, check_vma=False)
```

```python
import functools
import math

import jax
import jax.numpy as jnp
from jax import lax
from jax.experimental import pallas as pl
from jax.experimental.pallas import tpu as pltpu
from jax.sharding import PartitionSpec as P


CX = 1
CY = 64
CZ = 8
NAXES = 64

ROT_COS = -0.6427876096865393
ROT_SIN = 0.766044443118978
RESERVOIR_HEAT = 0.9
FEEDBACK = 1.0
GOLDEN = 2.399963229728653

LANES = 128
SUBLANES = 8
AXES = ("slab", "sub")
VMEM = pl.BlockSpec(memory_space=pltpu.VMEM)
NT = (((1,), (1,)), ((), ()))
TAKE = lax.GatherDimensionNumbers(
    offset_dims=(),
    collapsed_slice_dims=(1,),
    start_index_map=(1,),
    operand_batching_dims=(0,),
    start_indices_batching_dims=(0,),
)


def take(rows, lanes):
    return lax.gather(
        rows,
        lanes[:, :, None],
        dimension_numbers=TAKE,
        slice_sizes=(1, 1),
        mode=lax.GatherScatterMode.PROMISE_IN_BOUNDS,
    )


def lookup(rows, index, shift=7):
    high, low = index >> shift, index & (LANES - 1)
    out = jnp.zeros(index.shape, rows[0].dtype)
    for h, row in enumerate(rows):
        out = jnp.where(high == h, take(jnp.broadcast_to(row, index.shape), low), out)
    return out


def iota(shape, axis):
    return lax.broadcasted_iota(jnp.int32, shape, axis)


def split3(x):
    a = x.astype(jnp.bfloat16).astype(jnp.float32)
    rest = x - a
    b = rest.astype(jnp.bfloat16).astype(jnp.float32)
    return a, b, rest - b


def parity(axis):
    if lax.axis_size(axis) % 2:
        return 0
    return lax.rem(lax.axis_index(axis), 2)


def ordered_lists(moves_ref):
    lists = []
    for base, axis in ((0, "slab"), (2, "sub")):
        odd = parity(axis)
        one, two = moves_ref[base : base + 1], moves_ref[base + 1 : base + 2]
        lists += [jnp.where(odd == 0, one, two), jnp.where(odd == 0, two, one)]
    return lists


def chunks(count, pieces):
    rows = count // LANES
    pieces = math.gcd(pieces, rows)
    size = rows // pieces
    return [(k, pl.ds(k * size * LANES, size * LANES), range(k * size, (k + 1) * size)) for k in range(pieces)]


def first_departure(v_hbm, moves_hbm, out_ref, v_ref, moves_ref, sems):
    parts = chunks(v_ref.shape[1], 2)
    copies = [pltpu.make_async_copy(moves_hbm, moves_ref, sems.at[len(parts)])]
    copies += [pltpu.make_async_copy(v_hbm.at[:, span], v_ref.at[:, span], sems.at[k]) for k, span, _ in parts]
    for copy in copies:
        copy.start()
    copies[0].wait()
    index = ordered_lists(moves_ref)[1]
    comps = v_ref.shape[0]
    index = jnp.broadcast_to(index, (comps, LANES))
    high, low = index >> 7, index & (LANES - 1)
    out = jnp.zeros((comps, LANES), jnp.float32)
    for copy, (_, _, rows) in zip(copies[1:], parts):
        copy.wait()
        for r in rows:
            out = jnp.where(high == r, take(v_ref[:, r * LANES : (r + 1) * LANES], low), out)
    out_ref[...] = out


def other_departures(v_ref, moves_ref, a_ref, s_ref):
    comps, count = v_ref.shape
    lists = ordered_lists(moves_ref)
    for k, out_ref, lane in ((0, a_ref, 0), (2, s_ref, 0), (3, s_ref, LANES)):
        index = jnp.broadcast_to(lists[k], (comps, LANES))
        high, low = index >> 7, index & (LANES - 1)
        out = jnp.zeros((comps, LANES), jnp.float32)
        for r in range(count // LANES):
            out = jnp.where(high == r, take(v_ref[:, r * LANES : (r + 1) * LANES], low), out)
        out_ref[:, lane : lane + LANES] = out


def bins(block, cell, blocks):
    parts = jnp.concatenate(split3(block), 0)
    left = jnp.concatenate([jnp.where((cell >> 7) == h, parts, 0.0) for h in range(blocks)], 0)
    right = (iota((LANES, LANES), 0) == (cell & (LANES - 1))).astype(jnp.bfloat16)
    return left, right


def join(parts):
    return parts[:SUBLANES] + parts[SUBLANES : 2 * SUBLANES] + parts[2 * SUBLANES :]


def columns_of(cells):
    return cells // CZ


def prepare(v_ref, moves_ref, cell_ref, choice_ref, shear_ref, a_ref, s_ref, vd_ref, source_ref, celld_ref, base_ref, count_ref, column_ref, spread_ref, normal_ref, target_ref, shift_ref, slot_ref, energy_ref, keep_ref):
    comps, count = v_ref.shape
    rows = count // LANES
    cells = choice_ref.shape[1]
    blocks = cells // LANES
    lists = ordered_lists(moves_ref)
    target_ref[...] = jnp.concatenate([shear_ref[...], jnp.zeros((1, LANES - CY), jnp.float32)], 1)
    for r in range(rows):
        span = slice(r * LANES, (r + 1) * LANES)
        celld_ref[r : r + 1, :] = cell_ref[0:1, span]
        for c in range(comps):
            vd_ref[c, r : r + 1, :] = v_ref[c : c + 1, span]

    order = (1, 0, 2, 3)
    slots = jnp.concatenate([lists[k] for k in order], 1)
    many = slots.shape[1]
    low = (iota((LANES, many), 0) == (slots & (LANES - 1))).astype(jnp.bfloat16)
    here = iota((rows, many), 0) == (slots >> 7)
    lane = iota((rows, many), 1)
    marks = jnp.concatenate(
        [
            jnp.where(here, (lane >> 7) + 1, 0).astype(jnp.float32),
            jnp.where(here, lane & (LANES - 1), 0).astype(jnp.float32),
        ]
    ).astype(jnp.bfloat16)
    found = lax.dot_general(marks, low, NT, preferred_element_type=jnp.float32).astype(jnp.int32)
    source = found[:rows] * LANES + found[rows:]
    keep_ref[...] = jnp.where(source == 0, 1.0, 0.0)
    late = (source >= LANES) & (source < 2 * LANES)
    source_ref[...] = jnp.where(late, source - LANES, -1)

    celld = celld_ref[...]
    four = jnp.concatenate([lists[k] for k in order + order], 0)
    slotcell = lookup([celld_ref[r : r + 1, :] for r in range(rows)], four)

    counter = (iota((1, LANES), 1) & (NAXES - 1)).astype(jnp.float32)
    height = 1.0 - (2.0 * counter + 1.0) / NAXES
    radius = jnp.sqrt(1.0 - height * height)
    table = (radius * jnp.cos(GOLDEN * counter), radius * jnp.sin(GOLDEN * counter), height)
    picks = [choice_ref[0:1, h * LANES : (h + 1) * LANES] for h in range(blocks)]
    for c in range(comps):
        entries = [take(table[c], pick) for pick in picks]
        normal_ref[c] = lookup(entries, celld)

    arrived = [a_ref[...], s_ref[:, :LANES], s_ref[:, LANES:]]
    for c in range(comps):
        old = vd_ref[c]
        vd_ref[c] = jnp.where(source < 2 * LANES, old, lookup([x[c : c + 1] for x in arrived], source - 2 * LANES))

    ones = (iota((SUBLANES - comps, LANES), 0) == 0).astype(jnp.float32)
    total = jnp.zeros((blocks * 3 * SUBLANES, LANES), jnp.float32)
    group = math.gcd(4, rows)
    for first in range(0, rows, group):
        left, right = [], []
        for r in range(first, first + group):
            span = slice(r * LANES, (r + 1) * LANES)
            tile = v_ref[:, span] * keep_ref[r : r + 1, :]
            one, two = bins(jnp.concatenate([tile, ones], 0), cell_ref[0:1, span], blocks)
            left.append(one)
            right.append(two)
        left = jnp.concatenate(left, 1).astype(jnp.bfloat16)
        total += lax.dot_general(left, jnp.concatenate(right, 1), NT, preferred_element_type=jnp.float32)
    left, right = [], []
    for k, block in enumerate(arrived):
        one, two = bins(jnp.concatenate([block, jnp.zeros_like(ones)], 0), slotcell[k + 1 : k + 2], blocks)
        left.append(one)
        right.append(two)
    left = jnp.concatenate(left, 1).astype(jnp.bfloat16)
    total += lax.dot_general(left, jnp.concatenate(right, 1), NT, preferred_element_type=jnp.float32)
    sums = [join(total[h * 3 * SUBLANES : (h + 1) * 3 * SUBLANES]) for h in range(blocks)]

    both = jnp.concatenate([x[0:1] for x in sums] + [x[comps : comps + 1] for x in sums], 0)
    width = CZ // 2
    while width:
        both = both + pltpu.roll(both, LANES - width, 1)
        width //= 2
    start = iota((1, LANES), 1) * CZ
    flow = lookup([both[h : h + 1] for h in range(blocks)], start)
    number = lookup([both[blocks + h : blocks + h + 1] for h in range(blocks)], start)
    column_ref[...] = jnp.concatenate([flow, 1.0 / jnp.maximum(number, 1.0)], 0)

    late_cell = jnp.transpose(jnp.broadcast_to(slotcell[0:1].astype(jnp.float32), (LANES, LANES))).astype(jnp.int32)
    others = []
    for h in range(blocks):
        span = slice(h * LANES, (h + 1) * LANES)
        hits = (late_cell == iota((LANES, LANES), 1) + h * LANES).astype(jnp.float32)
        spread_ref[:, span] = hits.astype(jnp.bfloat16)
        base_ref[:, span] = sums[h]
        number = sums[h][comps : comps + 1]
        count_ref[:, span] = 1.0 / jnp.maximum(number, 1.0)
        missing = jnp.sum(hits, 0, keepdims=True)
        other = sums[h] / jnp.maximum(number - missing, 1.0)
        others.append(other)
        shift_ref[:, span] = jnp.where(iota((SUBLANES, LANES), 0) < comps, other * missing, 0.0)
    spread_ref[:, cells:] = (columns_of(late_cell) == iota((LANES, LANES), 1)).astype(jnp.bfloat16)
    energy = jnp.zeros((rows, LANES), jnp.float32)
    for c in range(comps):
        parts = [x[c : c + 1] for x in others]
        slot_ref[c : c + 1, :] = lookup(parts, slotcell[0:1])
        apart = vd_ref[c] - lookup(parts, celld)
        energy += apart * apart
    energy_ref[...] = jnp.sum(jnp.where(late, 0.0, energy), 0, keepdims=True)


def on_last_slab():
    return lax.axis_index("slab") == lax.axis_size("slab") - 1


def turn(late, means_ref, vd_ref, source_ref, celld_ref, normal_ref, mean_ref, turned_ref):
    comps = vd_ref.shape[0]
    source, celld = source_ref[...], celld_ref[...]
    relative = []
    for c in range(comps):
        fill = take(jnp.broadcast_to(late[c : c + 1], source.shape), source & (LANES - 1))
        speed = jnp.where(source < 0, vd_ref[c], fill)
        mean = lookup([means_ref[c : c + 1, h : h + LANES] for h in range(0, means_ref.shape[1], LANES)], celld)
        mean_ref[c] = mean
        relative.append(speed - mean)
    n = [normal_ref[c] for c in range(comps)]
    along = (n[0] * relative[0] + n[1] * relative[1] + n[2] * relative[2]) * (1.0 - ROT_COS)
    for c in range(comps):
        d, e = (c + 1) % comps, (c + 2) % comps
        cross = n[d] * relative[e] - n[e] * relative[d]
        turned_ref[c] = relative[c] * ROT_COS + cross * ROT_SIN + n[c] * along


def relax(b_ref, vd_ref, source_ref, celld_ref, base_ref, count_ref, column_ref, spread_ref, normal_ref, shift_ref, slot_ref, energy_ref, send_ref, profile_ref, means_ref, mean_ref, turned_ref):
    comps = vd_ref.shape[0]
    cells = base_ref.shape[1]
    late = b_ref[...]
    block = jnp.concatenate([late, jnp.zeros((SUBLANES - comps, LANES), jnp.float32)], 0)
    left = jnp.concatenate(split3(block), 0).astype(jnp.bfloat16)
    fresh = join(jnp.dot(left, spread_ref[...], preferred_element_type=jnp.float32))
    means_ref[...] = (base_ref[...] + fresh[:, :cells]) * count_ref[...]
    profile = (column_ref[0:1] + fresh[0:1, cells:]) * column_ref[1:2]
    profile_ref[...] = profile[:, :CY]

    moved = fresh[:, :cells] - shift_ref[...]
    less = jnp.sum(moved * moved, 0, keepdims=True) * count_ref[...]
    apart = late - slot_ref[...]
    energy = energy_ref[...] + jnp.sum(apart * apart, 0, keepdims=True)
    for h in range(0, cells, LANES):
        energy = energy - less[:, h : h + LANES]
    energy = energy + pltpu.roll(energy, CY, 1)
    message = jnp.where(iota((1, LANES), 1) < CY, profile, energy)
    send_ref[...] = jnp.broadcast_to(message[None], send_ref.shape)

    @pl.when(jnp.logical_not(on_last_slab()))
    def _():
        turn(late, means_ref, vd_ref, source_ref, celld_ref, normal_ref, mean_ref, turned_ref)


def finish(got_ref, target_ref, profile_ref, mean_ref, turned_ref, b_ref, means_ref, vd_ref, source_ref, celld_ref, normal_ref, out_hbm, profile_hbm, out_ref, own_mean_ref, own_turned_ref, sems, *, slabs, subs, particles):
    comps, rows, _ = mean_ref.shape
    copies = [pltpu.make_async_copy(profile_ref, profile_hbm, sems.at[0]), pltpu.make_async_copy(out_ref, out_hbm, sems.at[1])]
    copies[0].start()
    got = got_ref[...].reshape(slabs * subs, LANES)
    mine = lax.rem(iota(got.shape, 0), subs) == lax.axis_index("sub")
    lane = iota(got.shape, 1)
    drift = jnp.sum(jnp.where(mine, got, 0.0), 0, keepdims=True) / (CX * slabs)
    work = jnp.sum(jnp.where(lane < CY, 0.0, got), 0, keepdims=True)
    work = jnp.maximum(jnp.sum(work, 1, keepdims=True), 0.0)
    scale = lax.rsqrt(work / (3.0 * particles * RESERVOIR_HEAT) + 1e-06)
    extra = FEEDBACK * (target_ref[...] - drift)
    line = columns_of(celld_ref[...]) & (CY - 1)
    shift = take(jnp.broadcast_to(extra, line.shape), line)

    def write(mean_ref, turned_ref):
        for c in range(comps):
            base = mean_ref[c] + shift if c == 0 else mean_ref[c]
            out = base + scale * turned_ref[c]
            for r in range(rows):
                out_ref[c : c + 1, r * LANES : (r + 1) * LANES] = out[r : r + 1, :]

    last = on_last_slab()

    @pl.when(last)
    def _():
        turn(b_ref[...], means_ref, vd_ref, source_ref, celld_ref, normal_ref, own_mean_ref, own_turned_ref)
        write(own_mean_ref, own_turned_ref)

    @pl.when(jnp.logical_not(last))
    def _():
        write(mean_ref, turned_ref)

    copies[1].start()
    for copy in copies:
        copy.wait()


def swap(blocks, axis):
    size = lax.axis_size(axis)
    one, two = blocks
    if size % 2:
        forth = [(i, (i + 1) % size) for i in range(size)]
        back = [(i, (i - 1) % size) for i in range(size)]
        return [lax.ppermute(two, axis, back), lax.ppermute(one, axis, forth)]
    even = [(i, i ^ 1) for i in range(size)]
    odd = [(i, (i + 1 if i % 2 else i - 1) % size) for i in range(size)]
    second = lax.ppermute(two, axis, odd)
    first = lax.ppermute(one, axis, even)
    return [first, second]


def swap_joined(block, axis):
    size = lax.axis_size(axis)
    if size == 2:
        return lax.ppermute(block, axis, [(0, 1), (1, 0)])
    return jnp.concatenate(swap([block[:, :LANES], block[:, LANES:]], axis), 1)


def f32(*shape):
    return pltpu.VMEM(shape, jnp.float32)


def i32(*shape):
    return pltpu.VMEM(shape, jnp.int32)


def call(kernel, out_shape, inputs, scratch=(), flops=0, resident=True):
    size = sum(4 * math.prod(x.shape) for x in inputs)
    place = VMEM
    if resident:
        inputs = [pltpu.with_memory_space_constraint(x, pltpu.VMEM) for x in inputs]
    else:
        place = pl.BlockSpec(memory_space=pl.ANY)
    return pl.pallas_call(
        kernel,
        out_shape=out_shape,
        in_specs=[place] * len(inputs),
        out_specs=jax.tree.map(lambda x: VMEM if isinstance(x, pl.MemoryRef) else pl.BlockSpec(memory_space=pl.ANY), out_shape),
        scratch_shapes=list(scratch),
        cost_estimate=pl.CostEstimate(flops=flops, bytes_accessed=size, transcendentals=0),
    )(*inputs)


def step(speeds, cells, choices, moves, shear_target):
    slabs, subs = lax.axis_size("slab"), lax.axis_size("sub")
    comps, count = speeds.shape
    rows = count // LANES
    b, speeds, moves = call(
        first_departure,
        (f32(comps, LANES), f32(*speeds.shape), i32(*moves.shape)),
        (speeds, moves),
        scratch=[pltpu.SemaphoreType.DMA((len(chunks(count, 2)) + 1,))],
        resident=False,
    )
    a, s = call(
        other_departures,
        (f32(comps, LANES), f32(comps, 2 * LANES)),
        (speeds, moves),
    )
    a, b = swap([a, b], "slab")
    s = swap_joined(s, "sub")
    dense = f32(comps, rows, LANES)
    index = i32(rows, LANES)
    cell_count = choices.shape[1]
    sums = f32(SUBLANES, cell_count)
    vd, source, celld, base, number, column, spread, normal, target, shift, slot, energy = call(
        prepare,
        (
            dense,
            index,
            index,
            sums,
            f32(1, cell_count),
            f32(2, LANES),
            pltpu.VMEM((LANES, cell_count + LANES), jnp.bfloat16),
            dense,
            f32(1, LANES),
            sums,
            f32(comps, LANES),
            f32(1, LANES),
        ),
        (speeds, moves, cells, choices, shear_target[None, :], a, s),
        scratch=[pltpu.VMEM((rows, LANES), jnp.float32)],
        flops=2 * count * LANES * 96,
    )
    send, profile, means, mean, turned = call(
        relax,
        (f32(slabs * subs, 1, LANES), f32(1, CX * CY), sums, dense, dense),
        (b, vd, source, celld, base, number, column, spread, normal, shift, slot, energy),
    )
    got = lax.all_to_all(send, AXES, 0, 0, tiled=True)
    return call(
        functools.partial(finish, slabs=slabs, subs=subs, particles=count * slabs * subs),
        (jax.ShapeDtypeStruct((comps, count), jnp.float32), jax.ShapeDtypeStruct((1, CX * CY), jnp.float32)),
        (got, target, profile, mean, turned, b, means, vd, source, celld, normal),
        scratch=[
            pltpu.VMEM((comps, count), jnp.float32),
            pltpu.VMEM((comps, rows, LANES), jnp.float32),
            pltpu.VMEM((comps, rows, LANES), jnp.float32),
            pltpu.SemaphoreType.DMA((2,)),
        ],
    )


def body(velocities, cell_index, axis_choice, moves, shear_target):
    speeds, profile = velocities, None
    for t in range(moves.shape[0]):
        speeds, profile = step(speeds, cell_index[t : t + 1], axis_choice[t : t + 1], moves[t], shear_target)
    return speeds, profile


def solution(mesh):
    in_specs = (
        P(None, ("slab", "sub")),
        P(None, ("slab", "sub")),
        P(None, ("slab", "sub")),
        P(None, None, ("slab", "sub")),
        P("sub"),
    )
    out_specs = (P(None, ("slab", "sub")), P("slab", "sub"))
    return jax.shard_map(body, mesh=mesh, in_specs=in_specs, out_specs=out_specs, check_vma=False)
```

```python
import functools
import math

import jax
import jax.numpy as jnp
from jax import lax
from jax.experimental import pallas as pl
from jax.experimental.pallas import tpu as pltpu
from jax.sharding import PartitionSpec as P


CX = 1
CY = 64
CZ = 8
NAXES = 64

ROT_COS = -0.6427876096865393
ROT_SIN = 0.766044443118978
RESERVOIR_HEAT = 0.9
FEEDBACK = 1.0
GOLDEN = 2.399963229728653

LANES = 128
SUBLANES = 8
AXES = ("slab", "sub")
VMEM = pl.BlockSpec(memory_space=pltpu.VMEM)
NT = (((1,), (1,)), ((), ()))
TAKE = lax.GatherDimensionNumbers(
    offset_dims=(),
    collapsed_slice_dims=(1,),
    start_index_map=(1,),
    operand_batching_dims=(0,),
    start_indices_batching_dims=(0,),
)


def take(rows, lanes):
    return lax.gather(
        rows,
        lanes[:, :, None],
        dimension_numbers=TAKE,
        slice_sizes=(1, 1),
        mode=lax.GatherScatterMode.PROMISE_IN_BOUNDS,
    )


def lookup(rows, index, shift=7):
    high, low = index >> shift, index & (LANES - 1)
    out = jnp.zeros(index.shape, rows[0].dtype)
    for h, row in enumerate(rows):
        out = jnp.where(high == h, take(jnp.broadcast_to(row, index.shape), low), out)
    return out


def iota(shape, axis):
    return lax.broadcasted_iota(jnp.int32, shape, axis)


def split3(x):
    a = x.astype(jnp.bfloat16).astype(jnp.float32)
    rest = x - a
    b = rest.astype(jnp.bfloat16).astype(jnp.float32)
    return a, b, rest - b


def parity(axis):
    if lax.axis_size(axis) % 2:
        return 0
    return lax.rem(lax.axis_index(axis), 2)


def ordered_lists(moves_ref):
    lists = []
    for base, axis in ((0, "slab"), (2, "sub")):
        odd = parity(axis)
        one, two = moves_ref[base : base + 1], moves_ref[base + 1 : base + 2]
        lists += [jnp.where(odd == 0, one, two), jnp.where(odd == 0, two, one)]
    return lists


def chunks(count, pieces):
    rows = count // LANES
    pieces = math.gcd(pieces, rows)
    size = rows // pieces
    return [(k, pl.ds(k * size * LANES, size * LANES), range(k * size, (k + 1) * size)) for k in range(pieces)]


def first_departure(v_hbm, moves_hbm, out_ref, v_ref, moves_ref, sems):
    parts = chunks(v_ref.shape[1], 2)
    copies = [pltpu.make_async_copy(moves_hbm, moves_ref, sems.at[len(parts)])]
    copies += [pltpu.make_async_copy(v_hbm.at[:, span], v_ref.at[:, span], sems.at[k]) for k, span, _ in parts]
    for copy in copies:
        copy.start()
    copies[0].wait()
    index = ordered_lists(moves_ref)[1]
    comps = v_ref.shape[0]
    index = jnp.broadcast_to(index, (comps, LANES))
    high, low = index >> 7, index & (LANES - 1)
    outs = [jnp.zeros((comps, LANES), jnp.float32) for _ in range(4)]
    for copy, (_, _, rows) in zip(copies[1:], parts):
        copy.wait()
        for r in rows:
            outs[r % 4] = jnp.where(high == r, take(v_ref[:, r * LANES : (r + 1) * LANES], low), outs[r % 4])
    out_ref[...] = (outs[0] + outs[1]) + (outs[2] + outs[3])


def other_departures(v_ref, moves_ref, a_ref, s_ref):
    comps, count = v_ref.shape
    lists = ordered_lists(moves_ref)
    for k, out_ref, lane in ((0, a_ref, 0), (2, s_ref, 0), (3, s_ref, LANES)):
        index = jnp.broadcast_to(lists[k], (comps, LANES))
        high, low = index >> 7, index & (LANES - 1)
        out = jnp.zeros((comps, LANES), jnp.float32)
        for r in range(count // LANES):
            out = jnp.where(high == r, take(v_ref[:, r * LANES : (r + 1) * LANES], low), out)
        out_ref[:, lane : lane + LANES] = out


def bins(block, cell, blocks):
    parts = jnp.concatenate(split3(block), 0)
    left = jnp.concatenate([jnp.where((cell >> 7) == h, parts, 0.0) for h in range(blocks)], 0)
    right = (iota((LANES, LANES), 0) == (cell & (LANES - 1))).astype(jnp.bfloat16)
    return left, right


def join(parts):
    return parts[:SUBLANES] + parts[SUBLANES : 2 * SUBLANES] + parts[2 * SUBLANES :]


def columns_of(cells):
    return cells // CZ


def prepare(v_ref, moves_ref, cell_ref, choice_ref, shear_ref, a_ref, s_ref, vd_ref, source_ref, celld_ref, base_ref, count_ref, column_ref, spread_ref, normal_ref, target_ref, shift_ref, slot_ref, energy_ref, keep_ref):
    comps, count = v_ref.shape
    rows = count // LANES
    cells = choice_ref.shape[1]
    blocks = cells // LANES
    lists = ordered_lists(moves_ref)
    target_ref[...] = jnp.concatenate([shear_ref[...], jnp.zeros((1, LANES - CY), jnp.float32)], 1)
    for r in range(rows):
        span = slice(r * LANES, (r + 1) * LANES)
        celld_ref[r : r + 1, :] = cell_ref[0:1, span]
        for c in range(comps):
            vd_ref[c, r : r + 1, :] = v_ref[c : c + 1, span]

    order = (1, 0, 2, 3)
    slots = jnp.concatenate([lists[k] for k in order], 1)
    many = slots.shape[1]
    low = (iota((LANES, many), 0) == (slots & (LANES - 1))).astype(jnp.bfloat16)
    here = iota((rows, many), 0) == (slots >> 7)
    lane = iota((rows, many), 1)
    marks = jnp.concatenate(
        [
            jnp.where(here, (lane >> 7) + 1, 0).astype(jnp.float32),
            jnp.where(here, lane & (LANES - 1), 0).astype(jnp.float32),
        ]
    ).astype(jnp.bfloat16)
    found = lax.dot_general(marks, low, NT, preferred_element_type=jnp.float32).astype(jnp.int32)
    source = found[:rows] * LANES + found[rows:]
    keep_ref[...] = jnp.where(source == 0, 1.0, 0.0)
    late = (source >= LANES) & (source < 2 * LANES)
    source_ref[...] = jnp.where(late, source - LANES, -1)

    celld = celld_ref[...]
    four = jnp.concatenate([lists[k] for k in order + order], 0)
    slotcell = lookup([celld_ref[r : r + 1, :] for r in range(rows)], four)

    counter = (iota((1, LANES), 1) & (NAXES - 1)).astype(jnp.float32)
    height = 1.0 - (2.0 * counter + 1.0) / NAXES
    radius = jnp.sqrt(1.0 - height * height)
    table = (radius * jnp.cos(GOLDEN * counter), radius * jnp.sin(GOLDEN * counter), height)
    picks = [choice_ref[0:1, h * LANES : (h + 1) * LANES] for h in range(blocks)]
    for c in range(comps):
        entries = [take(table[c], pick) for pick in picks]
        normal_ref[c] = lookup(entries, celld)

    arrived = [a_ref[...], s_ref[:, :LANES], s_ref[:, LANES:]]
    for c in range(comps):
        old = vd_ref[c]
        vd_ref[c] = jnp.where(source < 2 * LANES, old, lookup([x[c : c + 1] for x in arrived], source - 2 * LANES))

    ones = (iota((SUBLANES - comps, LANES), 0) == 0).astype(jnp.float32)
    total = jnp.zeros((blocks * 3 * SUBLANES, LANES), jnp.float32)
    group = math.gcd(4, rows)
    for first in range(0, rows, group):
        left, right = [], []
        for r in range(first, first + group):
            span = slice(r * LANES, (r + 1) * LANES)
            tile = v_ref[:, span] * keep_ref[r : r + 1, :]
            one, two = bins(jnp.concatenate([tile, ones], 0), cell_ref[0:1, span], blocks)
            left.append(one)
            right.append(two)
        left = jnp.concatenate(left, 1).astype(jnp.bfloat16)
        total += lax.dot_general(left, jnp.concatenate(right, 1), NT, preferred_element_type=jnp.float32)
    left, right = [], []
    for k, block in enumerate(arrived):
        one, two = bins(jnp.concatenate([block, jnp.zeros_like(ones)], 0), slotcell[k + 1 : k + 2], blocks)
        left.append(one)
        right.append(two)
    left = jnp.concatenate(left, 1).astype(jnp.bfloat16)
    total += lax.dot_general(left, jnp.concatenate(right, 1), NT, preferred_element_type=jnp.float32)
    sums = [join(total[h * 3 * SUBLANES : (h + 1) * 3 * SUBLANES]) for h in range(blocks)]

    both = jnp.concatenate([x[0:1] for x in sums] + [x[comps : comps + 1] for x in sums], 0)
    width = CZ // 2
    while width:
        both = both + pltpu.roll(both, LANES - width, 1)
        width //= 2
    start = iota((1, LANES), 1) * CZ
    flow = lookup([both[h : h + 1] for h in range(blocks)], start)
    number = lookup([both[blocks + h : blocks + h + 1] for h in range(blocks)], start)
    column_ref[...] = jnp.concatenate([flow, 1.0 / jnp.maximum(number, 1.0)], 0)

    late_cell = jnp.transpose(jnp.broadcast_to(slotcell[0:1].astype(jnp.float32), (LANES, LANES))).astype(jnp.int32)
    others = []
    for h in range(blocks):
        span = slice(h * LANES, (h + 1) * LANES)
        hits = (late_cell == iota((LANES, LANES), 1) + h * LANES).astype(jnp.float32)
        spread_ref[:, span] = hits.astype(jnp.bfloat16)
        base_ref[:, span] = sums[h]
        number = sums[h][comps : comps + 1]
        count_ref[:, span] = jnp.broadcast_to(1.0 / jnp.maximum(number, 1.0), (SUBLANES, LANES))
        missing = jnp.sum(hits, 0, keepdims=True)
        other = sums[h] / jnp.maximum(number - missing, 1.0)
        others.append(other)
        shift_ref[:, span] = jnp.where(iota((SUBLANES, LANES), 0) < comps, other * missing, 0.0)
    spread_ref[:, cells:] = (columns_of(late_cell) == iota((LANES, LANES), 1)).astype(jnp.bfloat16)
    slot_ref[...] = jnp.zeros_like(slot_ref)
    energy = jnp.zeros((rows, LANES), jnp.float32)
    for c in range(comps):
        parts = [x[c : c + 1] for x in others]
        slot_ref[c : c + 1, :] = lookup(parts, slotcell[0:1])
        apart = vd_ref[c] - lookup(parts, celld)
        energy += apart * apart
    energy = jnp.sum(jnp.where(late, 0.0, energy), 0, keepdims=True)
    energy_ref[...] = energy + pltpu.roll(energy, CY, 1)


def on_last_slab():
    return lax.axis_index("slab") == lax.axis_size("slab") - 1


def turn(late, means_ref, vd_ref, source_ref, celld_ref, normal_ref, mean_ref, turned_ref):
    comps = vd_ref.shape[0]
    source, celld = source_ref[...], celld_ref[...]
    relative = []
    for c in range(comps):
        fill = take(jnp.broadcast_to(late[c : c + 1], source.shape), source & (LANES - 1))
        speed = jnp.where(source < 0, vd_ref[c], fill)
        mean = lookup([means_ref[c : c + 1, h : h + LANES] for h in range(0, means_ref.shape[1], LANES)], celld)
        mean_ref[c] = mean
        relative.append(speed - mean)
    n = [normal_ref[c] for c in range(comps)]
    along = (n[0] * relative[0] + n[1] * relative[1] + n[2] * relative[2]) * (1.0 - ROT_COS)
    for c in range(comps):
        d, e = (c + 1) % comps, (c + 2) % comps
        cross = n[d] * relative[e] - n[e] * relative[d]
        turned_ref[c] = relative[c] * ROT_COS + cross * ROT_SIN + n[c] * along


def relax(b_ref, vd_ref, source_ref, celld_ref, base_ref, count_ref, column_ref, spread_ref, normal_ref, shift_ref, slot_ref, energy_ref, send_ref, profile_ref, means_ref, mean_ref, turned_ref):
    comps = vd_ref.shape[0]
    cells = base_ref.shape[1]
    late = b_ref[...]
    block = jnp.concatenate([late, jnp.zeros((SUBLANES - comps, LANES), jnp.float32)], 0)
    left = jnp.concatenate(split3(block), 0).astype(jnp.bfloat16)
    fresh = join(jnp.dot(left, spread_ref[...], preferred_element_type=jnp.float32))
    means_ref[...] = (base_ref[...] + fresh[:, :cells]) * count_ref[...]
    profile = (column_ref[0:1] + fresh[0:1, cells:]) * column_ref[1:2]
    profile_ref[...] = profile[:, :CY]

    apart = block - slot_ref[...]
    moved = fresh[:, :cells] - shift_ref[...]
    less = moved * moved * count_ref[...]
    energy = apart * apart
    for h in range(0, cells, LANES):
        energy = energy - less[:, h : h + LANES]
    energy = jnp.sum(energy + pltpu.roll(energy, CY, 1), 0, keepdims=True) + energy_ref[...]
    message = jnp.where(iota((1, LANES), 1) < CY, profile, energy)
    send_ref[...] = jnp.broadcast_to(message[None], send_ref.shape)

    @pl.when(jnp.logical_not(on_last_slab()))
    def _():
        turn(late, means_ref, vd_ref, source_ref, celld_ref, normal_ref, mean_ref, turned_ref)


def finish(got_ref, target_ref, profile_ref, mean_ref, turned_ref, b_ref, means_ref, vd_ref, source_ref, celld_ref, normal_ref, out_hbm, profile_hbm, out_ref, own_mean_ref, own_turned_ref, sems, *, slabs, subs, particles):
    comps, rows, _ = mean_ref.shape
    copies = [pltpu.make_async_copy(profile_ref, profile_hbm, sems.at[0]), pltpu.make_async_copy(out_ref, out_hbm, sems.at[1])]
    copies[0].start()
    heard = []
    for b in range(subs):
        terms = [got_ref[a * subs + b] for a in range(slabs)]
        while len(terms) > 1:
            terms = [sum(terms[k + 1 : k + 2], terms[k]) for k in range(0, len(terms), 2)]
        heard.append(terms[0])
    drift = heard[0]
    for b in range(1, subs):
        drift = jnp.where(lax.axis_index("sub") == b, heard[b], drift)
    drift = drift / (CX * slabs)
    work = sum(heard[1:], heard[0])
    work = jnp.sum(jnp.where(iota(work.shape, 1) < CY, 0.0, work), 1, keepdims=True)
    work = jnp.maximum(work, 0.0)
    scale = lax.rsqrt(work / (3.0 * particles * RESERVOIR_HEAT) + 1e-06)
    extra = FEEDBACK * (target_ref[...] - drift)
    line = columns_of(celld_ref[...]) & (CY - 1)
    shift = take(jnp.broadcast_to(extra, line.shape), line)

    def write(mean_ref, turned_ref):
        for c in range(comps):
            base = mean_ref[c] + shift if c == 0 else mean_ref[c]
            out = base + scale * turned_ref[c]
            for r in range(rows):
                out_ref[c : c + 1, r * LANES : (r + 1) * LANES] = out[r : r + 1, :]

    last = on_last_slab()

    @pl.when(last)
    def _():
        turn(b_ref[...], means_ref, vd_ref, source_ref, celld_ref, normal_ref, own_mean_ref, own_turned_ref)
        write(own_mean_ref, own_turned_ref)

    @pl.when(jnp.logical_not(last))
    def _():
        write(mean_ref, turned_ref)

    copies[1].start()
    for copy in copies:
        copy.wait()


def swap(blocks, axis):
    size = lax.axis_size(axis)
    one, two = blocks
    if size % 2:
        forth = [(i, (i + 1) % size) for i in range(size)]
        back = [(i, (i - 1) % size) for i in range(size)]
        return [lax.ppermute(two, axis, back), lax.ppermute(one, axis, forth)]
    even = [(i, i ^ 1) for i in range(size)]
    odd = [(i, (i + 1 if i % 2 else i - 1) % size) for i in range(size)]
    second = lax.ppermute(two, axis, odd)
    first = lax.ppermute(one, axis, even)
    return [first, second]


def swap_joined(block, axis):
    size = lax.axis_size(axis)
    if size == 2:
        return lax.ppermute(block, axis, [(0, 1), (1, 0)])
    return jnp.concatenate(swap([block[:, :LANES], block[:, LANES:]], axis), 1)


def f32(*shape):
    return pltpu.VMEM(shape, jnp.float32)


def i32(*shape):
    return pltpu.VMEM(shape, jnp.int32)


def call(kernel, out_shape, inputs, scratch=(), flops=0, resident=True):
    size = sum(4 * math.prod(x.shape) for x in inputs)
    place = VMEM
    if resident:
        inputs = [pltpu.with_memory_space_constraint(x, pltpu.VMEM) for x in inputs]
    else:
        place = pl.BlockSpec(memory_space=pl.ANY)
    return pl.pallas_call(
        kernel,
        out_shape=out_shape,
        in_specs=[place] * len(inputs),
        out_specs=jax.tree.map(lambda x: VMEM if isinstance(x, pl.MemoryRef) else pl.BlockSpec(memory_space=pl.ANY), out_shape),
        scratch_shapes=list(scratch),
        cost_estimate=pl.CostEstimate(flops=flops, bytes_accessed=size, transcendentals=0),
    )(*inputs)


def step(speeds, cells, choices, moves, shear_target):
    slabs, subs = lax.axis_size("slab"), lax.axis_size("sub")
    comps, count = speeds.shape
    rows = count // LANES
    b, speeds, moves = call(
        first_departure,
        (f32(comps, LANES), f32(*speeds.shape), i32(*moves.shape)),
        (speeds, moves),
        scratch=[pltpu.SemaphoreType.DMA((len(chunks(count, 2)) + 1,))],
        resident=False,
    )
    a, s = call(
        other_departures,
        (f32(comps, LANES), f32(comps, 2 * LANES)),
        (speeds, moves),
    )
    a, b = swap([a, b], "slab")
    s = swap_joined(s, "sub")
    dense = f32(comps, rows, LANES)
    index = i32(rows, LANES)
    cell_count = choices.shape[1]
    sums = f32(SUBLANES, cell_count)
    vd, source, celld, base, number, column, spread, normal, target, shift, slot, energy = call(
        prepare,
        (
            dense,
            index,
            index,
            sums,
            sums,
            f32(2, LANES),
            pltpu.VMEM((LANES, cell_count + LANES), jnp.bfloat16),
            dense,
            f32(1, LANES),
            sums,
            f32(SUBLANES, LANES),
            f32(1, LANES),
        ),
        (speeds, moves, cells, choices, shear_target[None, :], a, s),
        scratch=[pltpu.VMEM((rows, LANES), jnp.float32)],
        flops=2 * count * LANES * 96,
    )
    send, profile, means, mean, turned = call(
        relax,
        (f32(slabs * subs, 1, LANES), f32(1, CX * CY), sums, dense, dense),
        (b, vd, source, celld, base, number, column, spread, normal, shift, slot, energy),
    )
    got = lax.all_to_all(send, AXES, 0, 0, tiled=True)
    return call(
        functools.partial(finish, slabs=slabs, subs=subs, particles=count * slabs * subs),
        (jax.ShapeDtypeStruct((comps, count), jnp.float32), jax.ShapeDtypeStruct((1, CX * CY), jnp.float32)),
        (got, target, profile, mean, turned, b, means, vd, source, celld, normal),
        scratch=[
            pltpu.VMEM((comps, count), jnp.float32),
            pltpu.VMEM((comps, rows, LANES), jnp.float32),
            pltpu.VMEM((comps, rows, LANES), jnp.float32),
            pltpu.SemaphoreType.DMA((2,)),
        ],
    )


def body(velocities, cell_index, axis_choice, moves, shear_target):
    speeds, profile = velocities, None
    for t in range(moves.shape[0]):
        speeds, profile = step(speeds, cell_index[t : t + 1], axis_choice[t : t + 1], moves[t], shear_target)
    return speeds, profile


def solution(mesh):
    in_specs = (
        P(None, ("slab", "sub")),
        P(None, ("slab", "sub")),
        P(None, ("slab", "sub")),
        P(None, None, ("slab", "sub")),
        P("sub"),
    )
    out_specs = (P(None, ("slab", "sub")), P("slab", "sub"))
    return jax.shard_map(body, mesh=mesh, in_specs=in_specs, out_specs=out_specs, check_vma=False)
```

```python
import functools
import math

import jax
import jax.numpy as jnp
from jax import lax
from jax.experimental import pallas as pl
from jax.experimental.pallas import tpu as pltpu
from jax.sharding import PartitionSpec as P


CX = 1
CY = 64
CZ = 8
NAXES = 64

ROT_COS = -0.6427876096865393
ROT_SIN = 0.766044443118978
RESERVOIR_HEAT = 0.9
FEEDBACK = 1.0
GOLDEN = 2.399963229728653

LANES = 128
SUBLANES = 8
AXES = ("slab", "sub")
VMEM = pl.BlockSpec(memory_space=pltpu.VMEM)
NT = (((1,), (1,)), ((), ()))
TAKE = lax.GatherDimensionNumbers(
    offset_dims=(),
    collapsed_slice_dims=(1,),
    start_index_map=(1,),
    operand_batching_dims=(0,),
    start_indices_batching_dims=(0,),
)


def take(rows, lanes):
    return lax.gather(
        rows,
        lanes[:, :, None],
        dimension_numbers=TAKE,
        slice_sizes=(1, 1),
        mode=lax.GatherScatterMode.PROMISE_IN_BOUNDS,
    )


def lookup(rows, index, shift=7):
    high, low = index >> shift, index & (LANES - 1)
    out = jnp.zeros(index.shape, rows[0].dtype)
    for h, row in enumerate(rows):
        out = jnp.where(high == h, take(jnp.broadcast_to(row, index.shape), low), out)
    return out


def iota(shape, axis):
    return lax.broadcasted_iota(jnp.int32, shape, axis)


def split3(x):
    a = x.astype(jnp.bfloat16).astype(jnp.float32)
    rest = x - a
    b = rest.astype(jnp.bfloat16).astype(jnp.float32)
    return a, b, rest - b


def parity(axis):
    if lax.axis_size(axis) % 2:
        return 0
    return lax.rem(lax.axis_index(axis), 2)


def ordered_lists(moves_ref):
    lists = []
    for base, axis in ((0, "slab"), (2, "sub")):
        odd = parity(axis)
        one, two = moves_ref[base : base + 1], moves_ref[base + 1 : base + 2]
        lists += [jnp.where(odd == 0, one, two), jnp.where(odd == 0, two, one)]
    return lists


def chunks(count, pieces):
    rows = count // LANES
    pieces = math.gcd(pieces, rows)
    size = rows // pieces
    return [(k, pl.ds(k * size * LANES, size * LANES), range(k * size, (k + 1) * size)) for k in range(pieces)]


def first_departure(v_hbm, moves_hbm, out_ref, v_ref, moves_ref, sems):
    parts = chunks(v_ref.shape[1], 2)
    copies = [pltpu.make_async_copy(moves_hbm, moves_ref, sems.at[len(parts)])]
    copies += [pltpu.make_async_copy(v_hbm.at[:, span], v_ref.at[:, span], sems.at[k]) for k, span, _ in parts]
    for copy in copies:
        copy.start()
    copies[0].wait()
    index = ordered_lists(moves_ref)[1]
    comps = v_ref.shape[0]
    index = jnp.broadcast_to(index, (comps, LANES))
    high, low = index >> 7, index & (LANES - 1)
    out = jnp.zeros((comps, LANES), jnp.float32)
    for copy, (_, _, rows) in zip(copies[1:], parts):
        copy.wait()
        for r in rows:
            out = jnp.where(high == r, take(v_ref[:, r * LANES : (r + 1) * LANES], low), out)
    out_ref[...] = out


def other_departures(v_ref, moves_ref, a_ref, s_ref):
    comps, count = v_ref.shape
    lists = ordered_lists(moves_ref)
    for k, out_ref, lane in ((0, a_ref, 0), (2, s_ref, 0), (3, s_ref, LANES)):
        index = jnp.broadcast_to(lists[k], (comps, LANES))
        high, low = index >> 7, index & (LANES - 1)
        out = jnp.zeros((comps, LANES), jnp.float32)
        for r in range(count // LANES):
            out = jnp.where(high == r, take(v_ref[:, r * LANES : (r + 1) * LANES], low), out)
        out_ref[:, lane : lane + LANES] = out


def bins(block, cell, blocks):
    parts = jnp.concatenate(split3(block), 0)
    left = jnp.concatenate([jnp.where((cell >> 7) == h, parts, 0.0) for h in range(blocks)], 0)
    right = (iota((LANES, LANES), 0) == (cell & (LANES - 1))).astype(jnp.bfloat16)
    return left, right


def join(parts):
    return parts[:SUBLANES] + parts[SUBLANES : 2 * SUBLANES] + parts[2 * SUBLANES :]


def columns_of(cells):
    return cells // CZ


def prepare(v_ref, moves_ref, cell_ref, choice_ref, shear_ref, a_ref, s_ref, vd_ref, source_ref, celld_ref, base_ref, count_ref, column_ref, spread_ref, normal_ref, target_ref, shift_ref, slot_ref, energy_ref, keep_ref):
    comps, count = v_ref.shape
    rows = count // LANES
    cells = choice_ref.shape[1]
    blocks = cells // LANES
    lists = ordered_lists(moves_ref)
    target_ref[...] = jnp.concatenate([shear_ref[...], jnp.zeros((1, LANES - CY), jnp.float32)], 1)
    for r in range(rows):
        span = slice(r * LANES, (r + 1) * LANES)
        celld_ref[r : r + 1, :] = cell_ref[0:1, span]
        for c in range(comps):
            vd_ref[c, r : r + 1, :] = v_ref[c : c + 1, span]

    order = (1, 0, 2, 3)
    slots = jnp.concatenate([lists[k] for k in order], 1)
    many = slots.shape[1]
    low = (iota((LANES, many), 0) == (slots & (LANES - 1))).astype(jnp.bfloat16)
    here = iota((rows, many), 0) == (slots >> 7)
    lane = iota((rows, many), 1)
    marks = jnp.concatenate(
        [
            jnp.where(here, (lane >> 7) + 1, 0).astype(jnp.float32),
            jnp.where(here, lane & (LANES - 1), 0).astype(jnp.float32),
        ]
    ).astype(jnp.bfloat16)
    found = lax.dot_general(marks, low, NT, preferred_element_type=jnp.float32).astype(jnp.int32)
    source = found[:rows] * LANES + found[rows:]
    keep_ref[...] = jnp.where(source == 0, 1.0, 0.0)
    late = (source >= LANES) & (source < 2 * LANES)
    source_ref[...] = jnp.where(late, source - LANES, -1)

    celld = celld_ref[...]
    four = jnp.concatenate([lists[k] for k in order + order], 0)
    slotcell = lookup([celld_ref[r : r + 1, :] for r in range(rows)], four)

    counter = (iota((1, LANES), 1) & (NAXES - 1)).astype(jnp.float32)
    height = 1.0 - (2.0 * counter + 1.0) / NAXES
    radius = jnp.sqrt(1.0 - height * height)
    table = (radius * jnp.cos(GOLDEN * counter), radius * jnp.sin(GOLDEN * counter), height)
    picks = [choice_ref[0:1, h * LANES : (h + 1) * LANES] for h in range(blocks)]
    for c in range(comps):
        entries = [take(table[c], pick) for pick in picks]
        normal_ref[c] = lookup(entries, celld)

    arrived = [a_ref[...], s_ref[:, :LANES], s_ref[:, LANES:]]
    for c in range(comps):
        old = vd_ref[c]
        vd_ref[c] = jnp.where(source < 2 * LANES, old, lookup([x[c : c + 1] for x in arrived], source - 2 * LANES))

    ones = (iota((SUBLANES - comps, LANES), 0) == 0).astype(jnp.float32)
    total = jnp.zeros((blocks * 3 * SUBLANES, LANES), jnp.float32)
    group = math.gcd(4, rows)
    for first in range(0, rows, group):
        left, right = [], []
        for r in range(first, first + group):
            span = slice(r * LANES, (r + 1) * LANES)
            tile = v_ref[:, span] * keep_ref[r : r + 1, :]
            one, two = bins(jnp.concatenate([tile, ones], 0), cell_ref[0:1, span], blocks)
            left.append(one)
            right.append(two)
        left = jnp.concatenate(left, 1).astype(jnp.bfloat16)
        total += lax.dot_general(left, jnp.concatenate(right, 1), NT, preferred_element_type=jnp.float32)
    left, right = [], []
    for k, block in enumerate(arrived):
        one, two = bins(jnp.concatenate([block, jnp.zeros_like(ones)], 0), slotcell[k + 1 : k + 2], blocks)
        left.append(one)
        right.append(two)
    left = jnp.concatenate(left, 1).astype(jnp.bfloat16)
    total += lax.dot_general(left, jnp.concatenate(right, 1), NT, preferred_element_type=jnp.float32)
    sums = [join(total[h * 3 * SUBLANES : (h + 1) * 3 * SUBLANES]) for h in range(blocks)]

    both = jnp.concatenate([x[0:1] for x in sums] + [x[comps : comps + 1] for x in sums], 0)
    width = CZ // 2
    while width:
        both = both + pltpu.roll(both, LANES - width, 1)
        width //= 2
    start = iota((1, LANES), 1) * CZ
    flow = lookup([both[h : h + 1] for h in range(blocks)], start)
    number = lookup([both[blocks + h : blocks + h + 1] for h in range(blocks)], start)
    column_ref[...] = jnp.concatenate([flow, 1.0 / jnp.maximum(number, 1.0)], 0)

    late_cell = jnp.transpose(jnp.broadcast_to(slotcell[0:1].astype(jnp.float32), (LANES, LANES))).astype(jnp.int32)
    others = []
    for h in range(blocks):
        span = slice(h * LANES, (h + 1) * LANES)
        hits = (late_cell == iota((LANES, LANES), 1) + h * LANES).astype(jnp.float32)
        spread_ref[:, span] = hits.astype(jnp.bfloat16)
        base_ref[:, span] = sums[h]
        number = sums[h][comps : comps + 1]
        count_ref[:, span] = jnp.broadcast_to(1.0 / jnp.maximum(number, 1.0), (SUBLANES, LANES))
        missing = jnp.sum(hits, 0, keepdims=True)
        other = sums[h] / jnp.maximum(number - missing, 1.0)
        others.append(other)
        shift_ref[:, span] = jnp.where(iota((SUBLANES, LANES), 0) < comps, other * missing, 0.0)
    spread_ref[:, cells:] = (columns_of(late_cell) == iota((LANES, LANES), 1)).astype(jnp.bfloat16)
    slot_ref[...] = jnp.zeros_like(slot_ref)
    energy = jnp.zeros((rows, LANES), jnp.float32)
    for c in range(comps):
        parts = [x[c : c + 1] for x in others]
        slot_ref[c : c + 1, :] = lookup(parts, slotcell[0:1])
        apart = vd_ref[c] - lookup(parts, celld)
        energy += apart * apart
    energy = jnp.sum(jnp.where(late, 0.0, energy), 0, keepdims=True)
    energy_ref[...] = energy + pltpu.roll(energy, CY, 1)


def on_last_slab():
    return lax.axis_index("slab") == lax.axis_size("slab") - 1


def turn(late, means_ref, vd_ref, source_ref, celld_ref, normal_ref, mean_ref, turned_ref):
    comps = vd_ref.shape[0]
    source, celld = source_ref[...], celld_ref[...]
    relative = []
    for c in range(comps):
        fill = take(jnp.broadcast_to(late[c : c + 1], source.shape), source & (LANES - 1))
        speed = jnp.where(source < 0, vd_ref[c], fill)
        mean = lookup([means_ref[c : c + 1, h : h + LANES] for h in range(0, means_ref.shape[1], LANES)], celld)
        mean_ref[c] = mean
        relative.append(speed - mean)
    n = [normal_ref[c] for c in range(comps)]
    along = (n[0] * relative[0] + n[1] * relative[1] + n[2] * relative[2]) * (1.0 - ROT_COS)
    for c in range(comps):
        d, e = (c + 1) % comps, (c + 2) % comps
        cross = n[d] * relative[e] - n[e] * relative[d]
        turned_ref[c] = relative[c] * ROT_COS + cross * ROT_SIN + n[c] * along


def relax(b_ref, vd_ref, source_ref, celld_ref, base_ref, count_ref, column_ref, spread_ref, normal_ref, shift_ref, slot_ref, energy_ref, send_ref, profile_ref, means_ref, mean_ref, turned_ref):
    comps = vd_ref.shape[0]
    cells = base_ref.shape[1]
    late = b_ref[...]
    block = jnp.concatenate([late, jnp.zeros((SUBLANES - comps, LANES), jnp.float32)], 0)
    left = jnp.concatenate(split3(block), 0).astype(jnp.bfloat16)
    fresh = join(jnp.dot(left, spread_ref[...], preferred_element_type=jnp.float32))
    means_ref[...] = (base_ref[...] + fresh[:, :cells]) * count_ref[...]
    profile = (column_ref[0:1] + fresh[0:1, cells:]) * column_ref[1:2]
    profile_ref[...] = profile[:, :CY]

    apart = block - slot_ref[...]
    moved = fresh[:, :cells] - shift_ref[...]
    less = moved * moved * count_ref[...]
    energy = apart * apart
    for h in range(0, cells, LANES):
        energy = energy - less[:, h : h + LANES]
    energy = jnp.sum(energy + pltpu.roll(energy, CY, 1), 0, keepdims=True) + energy_ref[...]
    message = jnp.where(iota((1, LANES), 1) < CY, profile, energy)
    send_ref[...] = jnp.broadcast_to(message[None], send_ref.shape)

    @pl.when(jnp.logical_not(on_last_slab()))
    def _():
        turn(late, means_ref, vd_ref, source_ref, celld_ref, normal_ref, mean_ref, turned_ref)


def finish(got_ref, target_ref, profile_ref, mean_ref, turned_ref, b_ref, means_ref, vd_ref, source_ref, celld_ref, normal_ref, out_hbm, profile_hbm, out_ref, own_mean_ref, own_turned_ref, sems, *, slabs, subs, particles):
    comps, _, _ = mean_ref.shape
    parts = chunks(out_ref.shape[1], 2)
    copies = [pltpu.make_async_copy(profile_ref, profile_hbm, sems.at[0])]
    copies += [pltpu.make_async_copy(out_ref.at[:, span], out_hbm.at[:, span], sems.at[1 + k]) for k, span, _ in parts]
    copies[0].start()
    got = got_ref[...].reshape(slabs * subs, LANES)
    mine = lax.rem(iota(got.shape, 0), subs) == lax.axis_index("sub")
    lane = iota(got.shape, 1)
    drift = jnp.sum(jnp.where(mine, got, 0.0), 0, keepdims=True) / (CX * slabs)
    work = jnp.sum(jnp.where(lane < CY, 0.0, got), 0, keepdims=True)
    work = jnp.maximum(jnp.sum(work, 1, keepdims=True), 0.0)
    scale = lax.rsqrt(work / (3.0 * particles * RESERVOIR_HEAT) + 1e-06)
    extra = FEEDBACK * (target_ref[...] - drift)
    line = columns_of(celld_ref[...]) & (CY - 1)
    shift = take(jnp.broadcast_to(extra, line.shape), line)

    def write(mean_ref, turned_ref):
        for (_, _, own), copy in zip(parts, copies[1:]):
            span = slice(own.start // SUBLANES * SUBLANES, -(-own.stop // SUBLANES) * SUBLANES)
            for c in range(comps):
                base = mean_ref[c, span, :] + shift[span] if c == 0 else mean_ref[c, span, :]
                out = base + scale * turned_ref[c, span, :]
                for r in own:
                    at = r - span.start
                    out_ref[c : c + 1, r * LANES : (r + 1) * LANES] = out[at : at + 1, :]
            copy.start()

    last = on_last_slab()

    @pl.when(last)
    def _():
        turn(b_ref[...], means_ref, vd_ref, source_ref, celld_ref, normal_ref, own_mean_ref, own_turned_ref)
        write(own_mean_ref, own_turned_ref)

    @pl.when(jnp.logical_not(last))
    def _():
        write(mean_ref, turned_ref)

    for copy in copies:
        copy.wait()


def swap(blocks, axis):
    size = lax.axis_size(axis)
    one, two = blocks
    if size % 2:
        forth = [(i, (i + 1) % size) for i in range(size)]
        back = [(i, (i - 1) % size) for i in range(size)]
        return [lax.ppermute(two, axis, back), lax.ppermute(one, axis, forth)]
    even = [(i, i ^ 1) for i in range(size)]
    odd = [(i, (i + 1 if i % 2 else i - 1) % size) for i in range(size)]
    second = lax.ppermute(two, axis, odd)
    first = lax.ppermute(one, axis, even)
    return [first, second]


def swap_joined(block, axis):
    size = lax.axis_size(axis)
    if size == 2:
        return lax.ppermute(block, axis, [(0, 1), (1, 0)])
    return jnp.concatenate(swap([block[:, :LANES], block[:, LANES:]], axis), 1)


def f32(*shape):
    return pltpu.VMEM(shape, jnp.float32)


def i32(*shape):
    return pltpu.VMEM(shape, jnp.int32)


def call(kernel, out_shape, inputs, scratch=(), flops=0, resident=True):
    size = sum(4 * math.prod(x.shape) for x in inputs)
    place = VMEM
    if resident:
        inputs = [pltpu.with_memory_space_constraint(x, pltpu.VMEM) for x in inputs]
    else:
        place = pl.BlockSpec(memory_space=pl.ANY)
    return pl.pallas_call(
        kernel,
        out_shape=out_shape,
        in_specs=[place] * len(inputs),
        out_specs=jax.tree.map(lambda x: VMEM if isinstance(x, pl.MemoryRef) else pl.BlockSpec(memory_space=pl.ANY), out_shape),
        scratch_shapes=list(scratch),
        cost_estimate=pl.CostEstimate(flops=flops, bytes_accessed=size, transcendentals=0),
    )(*inputs)


def step(speeds, cells, choices, moves, shear_target):
    slabs, subs = lax.axis_size("slab"), lax.axis_size("sub")
    comps, count = speeds.shape
    rows = count // LANES
    b, speeds, moves = call(
        first_departure,
        (f32(comps, LANES), f32(*speeds.shape), i32(*moves.shape)),
        (speeds, moves),
        scratch=[pltpu.SemaphoreType.DMA((len(chunks(count, 2)) + 1,))],
        resident=False,
    )
    a, s = call(
        other_departures,
        (f32(comps, LANES), f32(comps, 2 * LANES)),
        (speeds, moves),
    )
    a, b = swap([a, b], "slab")
    s = swap_joined(s, "sub")
    dense = f32(comps, rows, LANES)
    index = i32(rows, LANES)
    cell_count = choices.shape[1]
    sums = f32(SUBLANES, cell_count)
    vd, source, celld, base, number, column, spread, normal, target, shift, slot, energy = call(
        prepare,
        (
            dense,
            index,
            index,
            sums,
            sums,
            f32(2, LANES),
            pltpu.VMEM((LANES, cell_count + LANES), jnp.bfloat16),
            dense,
            f32(1, LANES),
            sums,
            f32(SUBLANES, LANES),
            f32(1, LANES),
        ),
        (speeds, moves, cells, choices, shear_target[None, :], a, s),
        scratch=[pltpu.VMEM((rows, LANES), jnp.float32)],
        flops=2 * count * LANES * 96,
    )
    send, profile, means, mean, turned = call(
        relax,
        (f32(slabs * subs, 1, LANES), f32(1, CX * CY), sums, dense, dense),
        (b, vd, source, celld, base, number, column, spread, normal, shift, slot, energy),
    )
    got = lax.all_to_all(send, AXES, 0, 0, tiled=True)
    return call(
        functools.partial(finish, slabs=slabs, subs=subs, particles=count * slabs * subs),
        (jax.ShapeDtypeStruct((comps, count), jnp.float32), jax.ShapeDtypeStruct((1, CX * CY), jnp.float32)),
        (got, target, profile, mean, turned, b, means, vd, source, celld, normal),
        scratch=[
            pltpu.VMEM((comps, count), jnp.float32),
            pltpu.VMEM((comps, rows, LANES), jnp.float32),
            pltpu.VMEM((comps, rows, LANES), jnp.float32),
            pltpu.SemaphoreType.DMA((3,)),
        ],
    )


def body(velocities, cell_index, axis_choice, moves, shear_target):
    speeds, profile = velocities, None
    for t in range(moves.shape[0]):
        speeds, profile = step(speeds, cell_index[t : t + 1], axis_choice[t : t + 1], moves[t], shear_target)
    return speeds, profile


def solution(mesh):
    in_specs = (
        P(None, ("slab", "sub")),
        P(None, ("slab", "sub")),
        P(None, ("slab", "sub")),
        P(None, None, ("slab", "sub")),
        P("sub"),
    )
    out_specs = (P(None, ("slab", "sub")), P("slab", "sub"))
    return jax.shard_map(body, mesh=mesh, in_specs=in_specs, out_specs=out_specs, check_vma=False)
```

```python
import functools
import math

import jax
import jax.numpy as jnp
from jax import lax
from jax.experimental import pallas as pl
from jax.experimental.pallas import tpu as pltpu
from jax.sharding import PartitionSpec as P


CX = 1
CY = 64
CZ = 8
NAXES = 64

ROT_COS = -0.6427876096865393
ROT_SIN = 0.766044443118978
RESERVOIR_HEAT = 0.9
FEEDBACK = 1.0
GOLDEN = 2.399963229728653

LANES = 128
SUBLANES = 8
AXES = ("slab", "sub")
VMEM = pl.BlockSpec(memory_space=pltpu.VMEM)
NT = (((1,), (1,)), ((), ()))
TAKE = lax.GatherDimensionNumbers(
    offset_dims=(),
    collapsed_slice_dims=(1,),
    start_index_map=(1,),
    operand_batching_dims=(0,),
    start_indices_batching_dims=(0,),
)


def take(rows, lanes):
    return lax.gather(
        rows,
        lanes[:, :, None],
        dimension_numbers=TAKE,
        slice_sizes=(1, 1),
        mode=lax.GatherScatterMode.PROMISE_IN_BOUNDS,
    )


def lookup(rows, index, shift=7):
    high, low = index >> shift, index & (LANES - 1)
    out = jnp.zeros(index.shape, rows[0].dtype)
    for h, row in enumerate(rows):
        out = jnp.where(high == h, take(jnp.broadcast_to(row, index.shape), low), out)
    return out


def iota(shape, axis):
    return lax.broadcasted_iota(jnp.int32, shape, axis)


def split3(x):
    a = x.astype(jnp.bfloat16).astype(jnp.float32)
    rest = x - a
    b = rest.astype(jnp.bfloat16).astype(jnp.float32)
    return a, b, rest - b


def parity(axis):
    if lax.axis_size(axis) % 2:
        return 0
    return lax.rem(lax.axis_index(axis), 2)


def ordered_lists(moves_ref):
    lists = []
    for base, axis in ((0, "slab"), (2, "sub")):
        odd = parity(axis)
        one, two = moves_ref[base : base + 1], moves_ref[base + 1 : base + 2]
        lists += [jnp.where(odd == 0, one, two), jnp.where(odd == 0, two, one)]
    return lists


def chunks(count, pieces):
    rows = count // LANES
    pieces = math.gcd(pieces, rows)
    size = rows // pieces
    return [(k, pl.ds(k * size * LANES, size * LANES), range(k * size, (k + 1) * size)) for k in range(pieces)]


def first_departure(v_hbm, moves_hbm, out_ref, v_ref, moves_ref, sems):
    parts = chunks(v_ref.shape[1], 2)
    copies = [pltpu.make_async_copy(moves_hbm, moves_ref, sems.at[len(parts)])]
    copies += [pltpu.make_async_copy(v_hbm.at[:, span], v_ref.at[:, span], sems.at[k]) for k, span, _ in parts]
    for copy in copies:
        copy.start(priority=1)
    copies[0].wait()
    index = ordered_lists(moves_ref)[1]
    comps = v_ref.shape[0]
    index = jnp.broadcast_to(index, (comps, LANES))
    high, low = index >> 7, index & (LANES - 1)
    out = jnp.zeros((comps, LANES), jnp.float32)
    for copy, (_, _, rows) in zip(copies[1:], parts):
        copy.wait()
        for r in rows:
            out = jnp.where(high == r, take(v_ref[:, r * LANES : (r + 1) * LANES], low), out)
    out_ref[...] = out


def other_departures(v_ref, moves_ref, a_ref, s_ref):
    comps, count = v_ref.shape
    lists = ordered_lists(moves_ref)
    for k, out_ref, lane in ((0, a_ref, 0), (2, s_ref, 0), (3, s_ref, LANES)):
        index = jnp.broadcast_to(lists[k], (comps, LANES))
        high, low = index >> 7, index & (LANES - 1)
        out = jnp.zeros((comps, LANES), jnp.float32)
        for r in range(count // LANES):
            out = jnp.where(high == r, take(v_ref[:, r * LANES : (r + 1) * LANES], low), out)
        out_ref[:, lane : lane + LANES] = out


def bins(block, cell, blocks):
    parts = jnp.concatenate(split3(block), 0)
    left = jnp.concatenate([jnp.where((cell >> 7) == h, parts, 0.0) for h in range(blocks)], 0)
    right = (iota((LANES, LANES), 0) == (cell & (LANES - 1))).astype(jnp.bfloat16)
    return left, right


def join(parts):
    return parts[:SUBLANES] + parts[SUBLANES : 2 * SUBLANES] + parts[2 * SUBLANES :]


def columns_of(cells):
    return cells // CZ


def prepare(v_ref, moves_ref, cell_ref, choice_ref, shear_ref, a_ref, s_ref, vd_ref, source_ref, celld_ref, base_ref, count_ref, column_ref, spread_ref, normal_ref, target_ref, shift_ref, slot_ref, energy_ref, keep_ref):
    comps, count = v_ref.shape
    rows = count // LANES
    cells = choice_ref.shape[1]
    blocks = cells // LANES
    lists = ordered_lists(moves_ref)
    target_ref[...] = jnp.concatenate([shear_ref[...], jnp.zeros((1, LANES - CY), jnp.float32)], 1)
    for r in range(rows):
        span = slice(r * LANES, (r + 1) * LANES)
        celld_ref[r : r + 1, :] = cell_ref[0:1, span]
        for c in range(comps):
            vd_ref[c, r : r + 1, :] = v_ref[c : c + 1, span]

    order = (1, 0, 2, 3)
    slots = jnp.concatenate([lists[k] for k in order], 1)
    many = slots.shape[1]
    low = (iota((LANES, many), 0) == (slots & (LANES - 1))).astype(jnp.bfloat16)
    here = iota((rows, many), 0) == (slots >> 7)
    lane = iota((rows, many), 1)
    marks = jnp.concatenate(
        [
            jnp.where(here, (lane >> 7) + 1, 0).astype(jnp.float32),
            jnp.where(here, lane & (LANES - 1), 0).astype(jnp.float32),
        ]
    ).astype(jnp.bfloat16)
    found = lax.dot_general(marks, low, NT, preferred_element_type=jnp.float32).astype(jnp.int32)
    source = found[:rows] * LANES + found[rows:]
    keep_ref[...] = jnp.where(source == 0, 1.0, 0.0)
    late = (source >= LANES) & (source < 2 * LANES)
    source_ref[...] = jnp.where(late, source - LANES, -1)

    celld = celld_ref[...]
    four = jnp.concatenate([lists[k] for k in order + order], 0)
    slotcell = lookup([celld_ref[r : r + 1, :] for r in range(rows)], four)

    counter = (iota((1, LANES), 1) & (NAXES - 1)).astype(jnp.float32)
    height = 1.0 - (2.0 * counter + 1.0) / NAXES
    radius = jnp.sqrt(1.0 - height * height)
    table = (radius * jnp.cos(GOLDEN * counter), radius * jnp.sin(GOLDEN * counter), height)
    picks = [choice_ref[0:1, h * LANES : (h + 1) * LANES] for h in range(blocks)]
    for c in range(comps):
        entries = [take(table[c], pick) for pick in picks]
        normal_ref[c] = lookup(entries, celld)

    arrived = [a_ref[...], s_ref[:, :LANES], s_ref[:, LANES:]]
    for c in range(comps):
        old = vd_ref[c]
        vd_ref[c] = jnp.where(source < 2 * LANES, old, lookup([x[c : c + 1] for x in arrived], source - 2 * LANES))

    ones = (iota((SUBLANES - comps, LANES), 0) == 0).astype(jnp.float32)
    total = jnp.zeros((blocks * 3 * SUBLANES, LANES), jnp.float32)
    group = math.gcd(4, rows)
    for first in range(0, rows, group):
        left, right = [], []
        for r in range(first, first + group):
            span = slice(r * LANES, (r + 1) * LANES)
            tile = v_ref[:, span] * keep_ref[r : r + 1, :]
            one, two = bins(jnp.concatenate([tile, ones], 0), cell_ref[0:1, span], blocks)
            left.append(one)
            right.append(two)
        left = jnp.concatenate(left, 1).astype(jnp.bfloat16)
        total += lax.dot_general(left, jnp.concatenate(right, 1), NT, preferred_element_type=jnp.float32)
    left, right = [], []
    for k, block in enumerate(arrived):
        one, two = bins(jnp.concatenate([block, jnp.zeros_like(ones)], 0), slotcell[k + 1 : k + 2], blocks)
        left.append(one)
        right.append(two)
    left = jnp.concatenate(left, 1).astype(jnp.bfloat16)
    total += lax.dot_general(left, jnp.concatenate(right, 1), NT, preferred_element_type=jnp.float32)
    sums = [join(total[h * 3 * SUBLANES : (h + 1) * 3 * SUBLANES]) for h in range(blocks)]

    both = jnp.concatenate([x[0:1] for x in sums] + [x[comps : comps + 1] for x in sums], 0)
    width = CZ // 2
    while width:
        both = both + pltpu.roll(both, LANES - width, 1)
        width //= 2
    start = iota((1, LANES), 1) * CZ
    flow = lookup([both[h : h + 1] for h in range(blocks)], start)
    number = lookup([both[blocks + h : blocks + h + 1] for h in range(blocks)], start)
    column_ref[...] = jnp.concatenate([flow, 1.0 / jnp.maximum(number, 1.0)], 0)

    late_cell = jnp.transpose(jnp.broadcast_to(slotcell[0:1].astype(jnp.float32), (LANES, LANES))).astype(jnp.int32)
    others = []
    for h in range(blocks):
        span = slice(h * LANES, (h + 1) * LANES)
        hits = (late_cell == iota((LANES, LANES), 1) + h * LANES).astype(jnp.float32)
        spread_ref[:, span] = hits.astype(jnp.bfloat16)
        base_ref[:, span] = sums[h]
        number = sums[h][comps : comps + 1]
        count_ref[:, span] = jnp.broadcast_to(1.0 / jnp.maximum(number, 1.0), (SUBLANES, LANES))
        missing = jnp.sum(hits, 0, keepdims=True)
        other = sums[h] / jnp.maximum(number - missing, 1.0)
        others.append(other)
        shift_ref[:, span] = jnp.where(iota((SUBLANES, LANES), 0) < comps, other * missing, 0.0)
    spread_ref[:, cells:] = (columns_of(late_cell) == iota((LANES, LANES), 1)).astype(jnp.bfloat16)
    slot_ref[...] = jnp.zeros_like(slot_ref)
    energy = jnp.zeros((rows, LANES), jnp.float32)
    for c in range(comps):
        parts = [x[c : c + 1] for x in others]
        slot_ref[c : c + 1, :] = lookup(parts, slotcell[0:1])
        apart = vd_ref[c] - lookup(parts, celld)
        energy += apart * apart
    energy = jnp.sum(jnp.where(late, 0.0, energy), 0, keepdims=True)
    energy_ref[...] = energy + pltpu.roll(energy, CY, 1)


def on_last_slab():
    return lax.axis_index("slab") == lax.axis_size("slab") - 1


def turn(late, means_ref, vd_ref, source_ref, celld_ref, normal_ref, mean_ref, turned_ref):
    comps = vd_ref.shape[0]
    source, celld = source_ref[...], celld_ref[...]
    relative = []
    for c in range(comps):
        fill = take(jnp.broadcast_to(late[c : c + 1], source.shape), source & (LANES - 1))
        speed = jnp.where(source < 0, vd_ref[c], fill)
        mean = lookup([means_ref[c : c + 1, h : h + LANES] for h in range(0, means_ref.shape[1], LANES)], celld)
        mean_ref[c] = mean
        relative.append(speed - mean)
    n = [normal_ref[c] for c in range(comps)]
    along = (n[0] * relative[0] + n[1] * relative[1] + n[2] * relative[2]) * (1.0 - ROT_COS)
    for c in range(comps):
        d, e = (c + 1) % comps, (c + 2) % comps
        cross = n[d] * relative[e] - n[e] * relative[d]
        turned_ref[c] = relative[c] * ROT_COS + cross * ROT_SIN + n[c] * along


def relax(b_ref, vd_ref, source_ref, celld_ref, base_ref, count_ref, column_ref, spread_ref, normal_ref, shift_ref, slot_ref, energy_ref, send_ref, profile_ref, means_ref, mean_ref, turned_ref):
    comps = vd_ref.shape[0]
    cells = base_ref.shape[1]
    late = b_ref[...]
    block = jnp.concatenate([late, jnp.zeros((SUBLANES - comps, LANES), jnp.float32)], 0)
    left = jnp.concatenate(split3(block), 0).astype(jnp.bfloat16)
    fresh = join(jnp.dot(left, spread_ref[...], preferred_element_type=jnp.float32))
    means_ref[...] = (base_ref[...] + fresh[:, :cells]) * count_ref[...]
    profile = (column_ref[0:1] + fresh[0:1, cells:]) * column_ref[1:2]
    profile_ref[...] = profile[:, :CY]

    apart = block - slot_ref[...]
    moved = fresh[:, :cells] - shift_ref[...]
    less = moved * moved * count_ref[...]
    energy = apart * apart
    for h in range(0, cells, LANES):
        energy = energy - less[:, h : h + LANES]
    energy = jnp.sum(energy + pltpu.roll(energy, CY, 1), 0, keepdims=True) + energy_ref[...]
    message = jnp.where(iota((1, LANES), 1) < CY, profile, energy)
    send_ref[...] = jnp.broadcast_to(message[None], send_ref.shape)

    @pl.when(jnp.logical_not(on_last_slab()))
    def _():
        turn(late, means_ref, vd_ref, source_ref, celld_ref, normal_ref, mean_ref, turned_ref)


def finish(got_ref, target_ref, profile_ref, mean_ref, turned_ref, b_ref, means_ref, vd_ref, source_ref, celld_ref, normal_ref, out_hbm, profile_hbm, out_ref, own_mean_ref, own_turned_ref, sems, *, slabs, subs, particles):
    comps, rows, _ = mean_ref.shape
    copies = [pltpu.make_async_copy(profile_ref, profile_hbm, sems.at[0]), pltpu.make_async_copy(out_ref, out_hbm, sems.at[1])]
    copies[0].start()
    got = got_ref[...].reshape(slabs * subs, LANES)
    mine = lax.rem(iota(got.shape, 0), subs) == lax.axis_index("sub")
    lane = iota(got.shape, 1)
    drift = jnp.sum(jnp.where(mine, got, 0.0), 0, keepdims=True) / (CX * slabs)
    work = jnp.sum(jnp.where(lane < CY, 0.0, got), 0, keepdims=True)
    work = jnp.maximum(jnp.sum(work, 1, keepdims=True), 0.0)
    scale = lax.rsqrt(work / (3.0 * particles * RESERVOIR_HEAT) + 1e-06)
    extra = FEEDBACK * (target_ref[...] - drift)
    line = columns_of(celld_ref[...]) & (CY - 1)
    shift = take(jnp.broadcast_to(extra, line.shape), line)

    def write(mean_ref, turned_ref):
        for c in range(comps):
            base = mean_ref[c] + shift if c == 0 else mean_ref[c]
            out = base + scale * turned_ref[c]
            for r in range(rows):
                out_ref[c : c + 1, r * LANES : (r + 1) * LANES] = out[r : r + 1, :]

    last = on_last_slab()

    @pl.when(last)
    def _():
        turn(b_ref[...], means_ref, vd_ref, source_ref, celld_ref, normal_ref, own_mean_ref, own_turned_ref)
        write(own_mean_ref, own_turned_ref)

    @pl.when(jnp.logical_not(last))
    def _():
        write(mean_ref, turned_ref)

    copies[1].start()
    for copy in copies:
        copy.wait()


def swap(blocks, axis):
    size = lax.axis_size(axis)
    one, two = blocks
    if size % 2:
        forth = [(i, (i + 1) % size) for i in range(size)]
        back = [(i, (i - 1) % size) for i in range(size)]
        return [lax.ppermute(two, axis, back), lax.ppermute(one, axis, forth)]
    even = [(i, i ^ 1) for i in range(size)]
    odd = [(i, (i + 1 if i % 2 else i - 1) % size) for i in range(size)]
    second = lax.ppermute(two, axis, odd)
    first = lax.ppermute(one, axis, even)
    return [first, second]


def swap_joined(block, axis):
    size = lax.axis_size(axis)
    if size == 2:
        return lax.ppermute(block, axis, [(0, 1), (1, 0)])
    return jnp.concatenate(swap([block[:, :LANES], block[:, LANES:]], axis), 1)


def f32(*shape):
    return pltpu.VMEM(shape, jnp.float32)


def i32(*shape):
    return pltpu.VMEM(shape, jnp.int32)


def call(kernel, out_shape, inputs, scratch=(), flops=0, resident=True):
    size = sum(4 * math.prod(x.shape) for x in inputs)
    place = VMEM
    if resident:
        inputs = [pltpu.with_memory_space_constraint(x, pltpu.VMEM) for x in inputs]
    else:
        place = pl.BlockSpec(memory_space=pl.ANY)
    return pl.pallas_call(
        kernel,
        out_shape=out_shape,
        in_specs=[place] * len(inputs),
        out_specs=jax.tree.map(lambda x: VMEM if isinstance(x, pl.MemoryRef) else pl.BlockSpec(memory_space=pl.ANY), out_shape),
        scratch_shapes=list(scratch),
        cost_estimate=pl.CostEstimate(flops=flops, bytes_accessed=size, transcendentals=0),
    )(*inputs)


def step(speeds, cells, choices, moves, shear_target):
    slabs, subs = lax.axis_size("slab"), lax.axis_size("sub")
    comps, count = speeds.shape
    rows = count // LANES
    b, speeds, moves = call(
        first_departure,
        (f32(comps, LANES), f32(*speeds.shape), i32(*moves.shape)),
        (speeds, moves),
        scratch=[pltpu.SemaphoreType.DMA((len(chunks(count, 2)) + 1,))],
        resident=False,
    )
    a, s = call(
        other_departures,
        (f32(comps, LANES), f32(comps, 2 * LANES)),
        (speeds, moves),
    )
    a, b = swap([a, b], "slab")
    s = swap_joined(s, "sub")
    dense = f32(comps, rows, LANES)
    index = i32(rows, LANES)
    cell_count = choices.shape[1]
    sums = f32(SUBLANES, cell_count)
    vd, source, celld, base, number, column, spread, normal, target, shift, slot, energy = call(
        prepare,
        (
            dense,
            index,
            index,
            sums,
            sums,
            f32(2, LANES),
            pltpu.VMEM((LANES, cell_count + LANES), jnp.bfloat16),
            dense,
            f32(1, LANES),
            sums,
            f32(SUBLANES, LANES),
            f32(1, LANES),
        ),
        (speeds, moves, cells, choices, shear_target[None, :], a, s),
        scratch=[pltpu.VMEM((rows, LANES), jnp.float32)],
        flops=2 * count * LANES * 96,
    )
    send, profile, means, mean, turned = call(
        relax,
        (f32(slabs * subs, 1, LANES), f32(1, CX * CY), sums, dense, dense),
        (b, vd, source, celld, base, number, column, spread, normal, shift, slot, energy),
    )
    got = lax.all_to_all(send, AXES, 0, 0, tiled=True)
    return call(
        functools.partial(finish, slabs=slabs, subs=subs, particles=count * slabs * subs),
        (jax.ShapeDtypeStruct((comps, count), jnp.float32), jax.ShapeDtypeStruct((1, CX * CY), jnp.float32)),
        (got, target, profile, mean, turned, b, means, vd, source, celld, normal),
        scratch=[
            pltpu.VMEM((comps, count), jnp.float32),
            pltpu.VMEM((comps, rows, LANES), jnp.float32),
            pltpu.VMEM((comps, rows, LANES), jnp.float32),
            pltpu.SemaphoreType.DMA((2,)),
        ],
    )


def body(velocities, cell_index, axis_choice, moves, shear_target):
    speeds, profile = velocities, None
    for t in range(moves.shape[0]):
        speeds, profile = step(speeds, cell_index[t : t + 1], axis_choice[t : t + 1], moves[t], shear_target)
    return speeds, profile


def solution(mesh):
    in_specs = (
        P(None, ("slab", "sub")),
        P(None, ("slab", "sub")),
        P(None, ("slab", "sub")),
        P(None, None, ("slab", "sub")),
        P("sub"),
    )
    out_specs = (P(None, ("slab", "sub")), P("slab", "sub"))
    return jax.shard_map(body, mesh=mesh, in_specs=in_specs, out_specs=out_specs, check_vma=False)
```
